32 devices in a mesh: groups: 2 (over y), orient: 4 (over z), img: 2 (over x), brick: 2 (over core).
Axes of the slice: x: 2, y: 2, z: 4, core: 2. Of those that a mesh axis runs over, the one named last changes fastest.
Arguments:
- images: bfloat16 [1024, 4096], P(('groups', 'orient', 'img', 'brick')), parts along dimension 0, may hold values from -8 to 8
- offsets: int32 [1024, 2], P('groups'), parts along dimension 0, may hold values from -6 to 6
- slices: bfloat16 [2048, 4096], P(('groups', 'orient')), parts along dimension 0, may hold values from -3 to 3
- seg_map: int32 [8192, 1], replicated, may hold values from 0 to 15; in each aligned block of 512 rows (0 to 511, 512 to 1023, ...) at most 64 rows name the same one
- interp: int32 [16, 8, 256, 256], P(('orient', 'img', 'brick')), may hold values from 0 to 4095
Outputs:
- brick_values: float32 [32, 2, 256], P(('groups', 'orient', 'img', 'brick')), parts along dimension 0
- brick_weight: float32 [32, 256], P(('groups', 'orient', 'img', 'brick')), parts along dimension 0
The draws below stay inside these ranges and needn't reach their ends.
There are 2 independent parts, one for each index of `groups`. The reference program is written for one: setup_inputs(seed, part) draws one part's arguments, and reference() takes and returns one part's arrays. A program takes and returns all parts, laid end to end along the dimension named above; an argument that names none is the same for every part. Nothing has to cross between parts.
Inputs may be any that keep to these rules, and one draw needn't show every extreme that they name: `seg_map`: in each aligned block of 512 rows no brick is named by more than 64 rows; in every draw some block names some brick exactly 64 times.
All inputs are finite; a program needn't handle non-finite values.
Results may differ from the reference program's by a relative error of at most 0.019.
Values may be sent and summed in bfloat16 or wider, within the bound.
No kernel may reach another device: no remote copies, remote signals or barrier semaphores. Data moves between devices by JAX's collectives and lax.ppermute only.
A program may use at most 64 MiB of HBM per device.

```python
import math
import jax
import jax.numpy as jnp
import numpy as np
from jax import lax

K = 2048
SHIFTS = 16
SEG = 256
VOX = 256
NIMG = 512
ORIENT = 1024
NSEG = 8
NBRICK = 16
SEG_ROWS = 512
CAP = 64
N_ORIENT = 4
N_IMG = 2
N_BRICK = 2


def offsets_law(key):
    return jax.random.randint(jax.random.fold_in(key, 7), (NIMG, 2), -6, 7).astype(jnp.int32)


def slices_law(key):
    base = jax.random.normal(jax.random.fold_in(key, 11), (ORIENT, 2 * K), jnp.float32)
    values = jnp.clip(0.5 * base, -3.0, 3.0)
    chosen = jax.random.permutation(jax.random.fold_in(key, 13), ORIENT)[:6]
    values = values.at[chosen[3:]].set(1.015 * values[chosen[:3]])
    return values


def draw_offsets(key, part):
    return offsets_law(key)


def draw_slices(key, part):
    return slices_law(key).astype(jnp.bfloat16)


def draw_images(key, part):
    values = jnp.clip(jax.random.normal(jax.random.fold_in(key, 17), (NIMG, 2 * K), jnp.float32), -6.0, 6.0)
    strength = jnp.array([2.5, 2.75, 3.0], jnp.float32)[:, None]
    slices = slices_law(key)
    chosen = jax.random.permutation(jax.random.fold_in(key, 13), ORIENT)[:3]
    targets = jax.random.permutation(jax.random.fold_in(key, 19), NIMG)[:3]
    pick_shift = jax.random.randint(jax.random.fold_in(key, 23), (3,), 0, SHIFTS)
    chosen_offsets = offsets_law(key)[targets]
    shift_x = chosen_offsets[:, 0] + pick_shift % 4 - 2
    shift_y = chosen_offsets[:, 1] + pick_shift // 4 - 2
    coef_index = jnp.arange(K, dtype=jnp.int32)
    column_freq = coef_index % 64 - 32
    row_freq = coef_index // 64
    phase_index = jnp.mod(shift_x[:, None] * column_freq[None, :] + shift_y[:, None] * row_freq[None, :], 64)
    angle = phase_index.astype(jnp.float32) * (2.0 * jnp.pi / 64.0)
    slice_real = slices[chosen, :K]
    slice_imag = slices[chosen, K:]
    real_part = strength * (slice_real * jnp.cos(angle) - slice_imag * jnp.sin(angle))
    imag_part = strength * (slice_real * jnp.sin(angle) + slice_imag * jnp.cos(angle))
    values = values.at[targets].set(jnp.concatenate([real_part, imag_part], axis=1))
    return jnp.clip(values, -8.0, 8.0).astype(jnp.bfloat16)


def touch_ends(drawn, stream_key, low, largest):
    index_at = [jax.random.randint(jax.random.fold_in(stream_key, axis), (), 0, length) for axis, length in enumerate(drawn.shape)]
    longest = drawn.shape.index(max(drawn.shape))
    next_to = index_at[:longest] + [(index_at[longest] + 1) % drawn.shape[longest]] + index_at[longest + 1:]
    return drawn.at[tuple(index_at)].set(low).at[tuple(next_to)].set(largest)


def assign_block(own_key, own, number, rows, count, top, most, lean):
    sequence = jax.random.permutation(own_key, count)
    crowded, ordinary = shares(count, rows * top, most, lean, True), shares(count, rows * top, most, lean, False)
    places = jnp.arange(count)

    def named(sizes, rotation):
        used = int((sizes > 0).sum())
        fixed = max(1, used // 4)
        moved = fixed + (places - fixed + rotation * (used - fixed)) % max(1, count - fixed)
        return jnp.zeros((count,), jnp.int32).at[sequence[jnp.where(places < fixed, places, moved)]].set(jnp.asarray(sizes, jnp.int32))

    sizes = jnp.where(number % 4 == 0, named(crowded, number // 4), named(ordinary, number - number // 4 - 1))
    mixed = jax.random.permutation(jax.random.fold_in(own, 3), count)
    donor, sink = mixed[0:count // 2 * 2:2], mixed[1:count // 2 * 2:2]
    slack = jnp.minimum(sizes[donor] - 1, most - sizes[sink]) // 2
    slack = jnp.where((donor == sequence[0]) | (sink == sequence[0]) | (sizes[sink] == 0), 0, jnp.maximum(slack, 0))
    moved = jax.random.randint(jax.random.fold_in(own, 4), (count // 2,), 0, 1 << 20) % (slack + 1)
    sizes = sizes.at[donor].add(-moved).at[sink].add(moved)
    items = jnp.searchsorted(jnp.cumsum(sizes), jnp.arange(rows * top), side="right").astype(jnp.int32)
    listing = items.reshape(top, rows).T
    listing = listing[jax.random.permutation(jax.random.fold_in(own, 1), rows)]
    rotation = jax.random.randint(jax.random.fold_in(own, 2), (rows, 1), 0, top)
    return jnp.take_along_axis(listing, (jnp.arange(top)[None, :] + rotation) % top, axis=1)


def shares(number_of, total, bound, slope, full):
    loads = [(1 << 20) // math.isqrt(grade ** slope) + 1 for grade in range(1, number_of + 1)]
    largest = bound if full else min(bound, max(-(-total // number_of), total * loads[0] // sum(loads)))
    least = 1 if total - largest >= number_of - 1 else 0
    counts, rest = [largest] + [least] * (number_of - 1), total - largest - least * (number_of - 1)
    while rest > 0:
        free = [i for i in range(1, number_of) if counts[i] < largest] or [i for i in range(1, number_of) if counts[i] < bound]
        whole, left = sum([loads[i] for i in free]), rest
        for i in free:
            addition = min(bound - counts[i], max(1, left * loads[i] // whole), rest)
            counts[i] = counts[i] + addition
            rest = rest - addition
    return np.array(counts)


def setup_inputs(seed: int = 0, part: int = 0) -> dict:
    seeds = jax.random.split(jax.random.key(seed), 6)
    part_keys = jax.random.split(jax.random.fold_in(seeds[5], part), 6)
    images = draw_images(jax.random.fold_in(jax.random.fold_in(seeds[5], part), 71), part)
    offsets = draw_offsets(jax.random.fold_in(jax.random.fold_in(seeds[5], part), 71), part)
    slices = draw_slices(jax.random.fold_in(jax.random.fold_in(seeds[5], part), 71), part)
    seg_map_keys = jax.random.split(jax.random.fold_in(seeds[3], 1), (ORIENT * NSEG) // SEG_ROWS)
    seg_map_turns = jax.random.permutation(jax.random.fold_in(seeds[3], 3), (ORIENT * NSEG) // SEG_ROWS)
    seg_map = jax.vmap(lambda own, number: assign_block(jax.random.fold_in(seeds[3], 2), own, number, SEG_ROWS, NBRICK, 1, CAP, 2))(seg_map_keys, seg_map_turns).reshape((ORIENT * NSEG, 1))
    interp = touch_ends(jax.random.randint(seeds[4], (NBRICK, NSEG, SEG, VOX), 0, 4096), jax.random.fold_in(seeds[4], 1), 0, 4095).astype(jnp.int32)
    return dict(images=images, offsets=offsets, slices=slices, seg_map=seg_map, interp=interp)


frame_side = 64
interp_scale = 1.0 / 256.0


def shift_images(image_rows, image_offsets):
    row_count = image_rows.shape[0]
    coeffs = image_rows.shape[1] // 2
    coef_index = jnp.arange(coeffs, dtype=jnp.int32)
    column_freq = coef_index % frame_side - frame_side // 2
    row_freq = coef_index // frame_side
    shift_index = jnp.arange(SHIFTS, dtype=jnp.int32)
    shift_x = image_offsets[:, 0][:, None] + (shift_index % 4 - 2)[None, :]
    shift_y = image_offsets[:, 1][:, None] + (shift_index // 4 - 2)[None, :]
    phase_index = jnp.mod(shift_x[:, :, None] * column_freq[None, None, :] + shift_y[:, :, None] * row_freq[None, None, :], frame_side)
    angle = phase_index.astype(jnp.float32) * (2.0 * jnp.pi / frame_side)
    cosine = jnp.cos(angle)
    sine = jnp.sin(angle)
    real_part = image_rows[:, :coeffs].astype(jnp.float32)[:, None, :]
    imag_part = image_rows[:, coeffs:].astype(jnp.float32)[:, None, :]
    out_real = real_part * cosine + imag_part * sine
    out_imag = imag_part * cosine - real_part * sine
    joined = jnp.concatenate([out_real, out_imag], axis=-1).astype(jnp.bfloat16)
    return joined.reshape(row_count * SHIFTS, 2 * coeffs)


def reference(images, offsets, slices, seg_map, interp):
    inv_noise = 100.0 / K
    group_count = N_IMG * N_BRICK
    per_shard = NIMG // (N_ORIENT * group_count)
    grouped_images = images.reshape(N_ORIENT, group_count, per_shard, 2 * K)
    grouped_offsets = offsets.reshape(N_ORIENT, group_count, per_shard, 2)
    half_norm = 0.5 * jnp.sum(jnp.square(slices.astype(jnp.float32)), axis=1)

    def one_group(carry, group_index):
        rows = lax.dynamic_index_in_dim(grouped_images, group_index, 1, keepdims=False).reshape(N_ORIENT * per_shard, 2 * K)
        shifts = lax.dynamic_index_in_dim(grouped_offsets, group_index, 1, keepdims=False).reshape(N_ORIENT * per_shard, 2)
        shifted = shift_images(rows, shifts)
        intersections = lax.dot_general(shifted, slices, (((1,), (1,)), ((), ())), preferred_element_type=jnp.float32)
        score = inv_noise * (intersections - half_norm[None, :])
        per_image = score.reshape(N_ORIENT * per_shard, SHIFTS * ORIENT)
        top_score = jnp.max(per_image, axis=1, keepdims=True)
        exp_terms = jnp.exp(per_image - top_score)
        mass_total = jnp.sum(exp_terms, axis=1, keepdims=True)
        posterior = (exp_terms / mass_total).astype(jnp.bfloat16).reshape(-1, ORIENT)
        partial_value = lax.dot_general(posterior, shifted, (((0,), (0,)), ((), ())), preferred_element_type=jnp.float32)
        part_mass = jnp.sum(posterior.astype(jnp.float32), axis=0)
        partial_value = lax.optimization_barrier(partial_value.astype(jnp.bfloat16)).astype(jnp.float32)
        part_mass = lax.optimization_barrier(part_mass.astype(jnp.bfloat16)).astype(jnp.float32)
        return (carry[0] + partial_value, carry[1] + part_mass), None

    start = (jnp.zeros((ORIENT, 2 * K), jnp.float32), jnp.zeros((ORIENT,), jnp.float32))
    (slice_sum, slice_mass), _ = lax.scan(one_group, start, jnp.arange(group_count, dtype=jnp.int32))

    segments = slice_sum.reshape(ORIENT, 2, NSEG, SEG).transpose(0, 2, 1, 3).reshape(ORIENT * NSEG, 2, SEG)
    seg_index = jnp.arange(ORIENT * NSEG, dtype=jnp.int32)
    target_key = seg_map[:, 0].astype(jnp.int32) * NSEG + seg_index % NSEG
    seg_total = jax.ops.segment_sum(segments, target_key, num_segments=NBRICK * NSEG).reshape(NBRICK, NSEG, 2, SEG)
    mass_rows = jnp.repeat(slice_mass, NSEG)
    mass_total = jax.ops.segment_sum(mass_rows, target_key, num_segments=NBRICK * NSEG).reshape(NBRICK, NSEG)

    def insert(packed):
        seg_block, mass_block, weight_block = packed
        weights = weight_block.astype(jnp.float32) * interp_scale
        values = jnp.einsum("jps,jsv->pv", seg_block, weights, precision=lax.Precision.HIGHEST)
        coverage = jnp.sum(weights, axis=1)
        weight_out = jnp.einsum("j,jv->v", mass_block, coverage, precision=lax.Precision.HIGHEST)
        return values, weight_out

    brick_values, brick_weight = lax.map(insert, (seg_total, mass_total, interp))
    return brick_values, brick_weight
```

```python
import functools

import jax
import jax.numpy as jnp
import numpy as np
from jax import lax
from jax.experimental import pallas as pl
from jax.experimental.pallas import tpu as pltpu
from jax.sharding import PartitionSpec as P

SHIFTS = 16
SEG = 256
NSEG = 8
K = SEG * NSEG
LANES = 128

frame_side = 64
interp_bits = 4
interp_scale = 1.0 / 256.0
PAIRS = SHIFTS // 2


def phase_tables():
    coef = np.arange(K)
    u = coef % frame_side - frame_side // 2
    w = coef // frame_side
    shift = np.arange(PAIRS)
    dx = 2 * (shift % 4) - 3
    dy = 2 * (shift // 4) - 3
    angle = (u[None, :] * dx[:, None] + w[None, :] * dy[:, None]) % (2 * frame_side)
    angle = angle * (2.0 * np.pi / (2 * frame_side))
    return np.cos(angle).astype(np.float32), np.sin(angle).astype(np.float32)


def cos_sin(steps):
    centred = jnp.bitwise_and(steps + frame_side, 2 * frame_side - 1) - frame_side
    x = centred.astype(jnp.float32) * (np.pi / frame_side)
    x2 = x * x
    c = jnp.full_like(x, (-1.0) ** 10 / float(np.prod(np.arange(1.0, 21.0))))
    s = jnp.full_like(x, (-1.0) ** 10 / float(np.prod(np.arange(1.0, 22.0))))
    for k in range(9, -1, -1):
        c = c * x2 + (-1.0) ** k / float(np.prod(np.arange(1.0, 2 * k + 1.0)))
        s = s * x2 + (-1.0) ** k / float(np.prod(np.arange(1.0, 2 * k + 2.0)))
    return c, s * x


def norm_kernel(slices_ref, out_ref):
    orient = slices_ref.shape[0]
    total = jnp.zeros((orient, LANES), jnp.float32)
    for k in range(2 * K // LANES):
        piece = slices_ref[:, k * LANES : (k + 1) * LANES].astype(jnp.float32)
        total = total + piece * piece
    ones = jnp.ones((8, LANES), jnp.float32)
    out_ref[...] = 0.5 * lax.dot_general(
        ones,
        total,
        (((1,), (1,)), ((), ())),
        precision=lax.Precision.HIGHEST,
        preferred_element_type=jnp.float32,
    )


def interp_kernel(interp_ref, weight_ref, cover_ref):
    raw = interp_ref[0, 0]
    high = jnp.right_shift(raw, interp_bits)
    low = jnp.bitwise_and(raw, (1 << interp_bits) - 1)
    vox = raw.shape[1]
    weight_ref[:, :vox] = high.astype(jnp.float32).astype(jnp.bfloat16)
    weight_ref[:, vox:] = low.astype(jnp.float32).astype(jnp.bfloat16)
    total = jnp.sum(raw.astype(jnp.float32), axis=0, keepdims=True)
    cover_ref[0] = total * interp_scale


def score_kernel(
    first, where_ref, images_ref, offsets_ref, slices_ref, norm_ref, cos_ref, sin_ref, *rest
):
    if first:
        terms_ref, based_ref, stats_ref, left_ref = rest
    else:
        _, _, stats_in_ref, terms_ref, based_ref, stats_ref, left_ref = rest
    inv_noise = 100.0 / K
    rows = images_ref.shape[0]
    off = 2 * offsets_ref[...] - 1
    off_x, off_y = off[:, 0:1], off[:, 1:2]
    lane = lax.broadcasted_iota(jnp.int32, (rows, LANES), 1)
    u = jnp.bitwise_and(lane, frame_side - 1) - frame_side // 2
    half = jnp.right_shift(lane, 6)
    c1, s1 = cos_sin(u * off_x + half * off_y)
    c2, s2 = cos_sin(2 * lane * off_y)
    for k in range(K // LANES):
        re_at = slice(k * LANES, (k + 1) * LANES)
        im_at = slice(K + k * LANES, K + (k + 1) * LANES)
        x_re = images_ref[:, re_at].astype(jnp.float32)
        x_im = images_ref[:, im_at].astype(jnp.float32)
        ck, sk = c2[:, k : k + 1], s2[:, k : k + 1]
        cb = c1 * ck - s1 * sk
        sb = s1 * ck + c1 * sk
        y_re = x_re * cb + x_im * sb
        y_im = x_im * cb - x_re * sb
        based_ref[:, re_at] = y_re.astype(jnp.bfloat16)
        based_ref[:, im_at] = y_im.astype(jnp.bfloat16)
        re_rows, im_rows = [], []
        for t in range(PAIRS):
            cos_t = cos_ref[t : t + 1, re_at]
            sin_t = sin_ref[t : t + 1, re_at]
            re_rows += [y_re * cos_t, y_im * sin_t]
            im_rows += [y_im * cos_t, -(y_re * sin_t)]
        left_ref[:, re_at] = jnp.concatenate(re_rows, axis=0).astype(jnp.bfloat16)
        left_ref[:, im_at] = jnp.concatenate(im_rows, axis=0).astype(jnp.bfloat16)
    both = lax.dot_general(
        left_ref[...],
        slices_ref[...],
        (((1,), (1,)), ((), ())),
        preferred_element_type=jnp.float32,
    )
    norm = norm_ref[0:1, :]
    scores = []
    for t in range(PAIRS):
        even = both[2 * t * rows : (2 * t + 1) * rows] - norm
        odd = both[(2 * t + 1) * rows : (2 * t + 2) * rows]
        scores += [inv_noise * (even + odd), inv_noise * (even - odd)]
    top = scores[0]
    for s in scores[1:]:
        top = jnp.maximum(top, s)
    top = jnp.max(top, axis=1, keepdims=True)
    mass = jnp.zeros_like(scores[0])
    for i, s in enumerate(scores):
        term = jnp.exp(s - top)
        mass = mass + term
        terms_ref[i] = term.astype(jnp.bfloat16)
    mass = jnp.sum(mass, axis=1, keepdims=True)
    count = stats_ref.shape[1]
    row = lax.broadcasted_iota(jnp.int32, (rows, count), 0)
    col = lax.broadcasted_iota(jnp.int32, (rows, count), 1)
    mine = col == row + where_ref[0] * rows
    top_row = jnp.sum(jnp.where(mine, top, 0.0), axis=0, keepdims=True)
    mass_row = jnp.sum(jnp.where(mine, mass, 0.0), axis=0, keepdims=True)
    which = lax.broadcasted_iota(jnp.int32, (8, count), 0)
    part = jnp.where(which == 0, top_row, jnp.where(which == 1, mass_row, 0.0))
    stats_ref[...] = part if first else part + stats_in_ref[...]


def brick_kernel(others, bricks, terms_ref, based_ref, seg_ref, cos_ref, sin_ref, *rest):
    stats_refs, (out_ref, pairs_ref) = rest[:others], rest[others:]
    count = based_ref.shape[0]
    orient = terms_ref.shape[2]
    own_top = stats_refs[0][0:1, :]
    top = own_top
    for ref in stats_refs[1:]:
        top = jnp.maximum(top, ref[0:1, :])
    mass = jnp.zeros_like(top)
    for ref in stats_refs:
        mass = mass + ref[1:2, :] * jnp.exp(ref[0:1, :] - top)
    factor = jnp.exp(own_top - top) / mass
    brick = lax.broadcasted_iota(jnp.int32, (bricks, orient), 0)
    hit = jnp.concatenate(
        [(brick == seg_ref[j : j + 1, :]).astype(jnp.float32) for j in range(NSEG)], axis=0
    ).astype(jnp.bfloat16)
    mass_sum = jnp.zeros((NSEG * bricks, count), jnp.float32)
    for t in range(PAIRS):
        plus, minus = (
            lax.dot_general(
                hit,
                terms_ref[2 * t + i],
                (((1,), (1,)), ((), ())),
                preferred_element_type=jnp.float32,
            )
            for i in range(2)
        )
        even = (plus + minus) * factor
        odd = (plus - minus) * factor
        mass_sum = mass_sum + even
        for j in range(NSEG):
            at = slice(j * bricks, (j + 1) * bricks)
            pairs_ref[j, t * bricks : (t + 1) * bricks, :] = even[at].astype(jnp.bfloat16)
            pairs_ref[j, (PAIRS + t) * bricks : (PAIRS + t + 1) * bricks, :] = odd[at].astype(
                jnp.bfloat16
            )
    mass_sum = jnp.sum(mass_sum, axis=1, keepdims=True)
    mass_high = mass_sum.astype(jnp.bfloat16).astype(jnp.float32)
    mass_low = mass_sum - mass_high
    lane = lax.broadcasted_iota(jnp.int32, (bricks, LANES), 1)
    tail = jnp.zeros((bricks, LANES), jnp.float32)
    for j in range(NSEG):
        at = slice(j * bricks, (j + 1) * bricks)
        tail = jnp.where(lane == j, mass_high[at], tail)
        tail = jnp.where(lane == NSEG + j, mass_low[at], tail)
        re_at = slice(j * SEG, (j + 1) * SEG)
        im_at = slice(K + j * SEG, K + (j + 1) * SEG)
        left = pairs_ref[j]
        with_re = jnp.dot(left, based_ref[:, re_at], preferred_element_type=jnp.float32)
        with_im = jnp.dot(left, based_ref[:, im_at], preferred_element_type=jnp.float32)
        sum_re = jnp.zeros((bricks, SEG), jnp.float32)
        sum_im = jnp.zeros((bricks, SEG), jnp.float32)
        for t in range(PAIRS):
            cos_t = cos_ref[t : t + 1, re_at]
            sin_t = sin_ref[t : t + 1, re_at]
            even = slice(t * bricks, (t + 1) * bricks)
            odd = slice((PAIRS + t) * bricks, (PAIRS + t + 1) * bricks)
            sum_re = sum_re + cos_t * with_re[even] + sin_t * with_im[odd]
            sum_im = sum_im + cos_t * with_im[even] - sin_t * with_re[odd]
        out_ref[:, re_at] = sum_re.astype(jnp.bfloat16)
        out_ref[:, im_at] = sum_im.astype(jnp.bfloat16)
    out_ref[:, 2 * K :] = tail.astype(jnp.bfloat16)


def final_kernel(arrived_ref, weight_ref, cover_ref, values_ref, mass_ref):
    vox = cover_ref.shape[2]
    total = jnp.sum(arrived_ref[...].astype(jnp.float32), axis=0, keepdims=True)
    re, im = total[:, :K], total[:, K : 2 * K]
    seg_mass = total[:, 2 * K :]
    parts = []
    for _ in range(3):
        high = [x.astype(jnp.bfloat16).astype(jnp.float32) for x in (re, im)]
        parts += high
        re, im = re - high[0], im - high[1]
    left = jnp.concatenate(parts + [jnp.zeros_like(re)] * 2, axis=0).astype(jnp.bfloat16)
    product = jnp.dot(left, weight_ref[...], preferred_element_type=jnp.float32)
    product = product[0:2] + product[2:4] + product[4:6]
    values_ref[0] = (product[:, :vox] * float(1 << interp_bits) + product[:, vox:]) * interp_scale
    weight = jnp.zeros((1, vox), jnp.float32)
    for j in range(NSEG):
        mass_j = seg_mass[:, j : j + 1] + seg_mass[:, NSEG + j : NSEG + j + 1]
        weight = weight + mass_j * cover_ref[j]
    mass_ref[0] = weight


def per_device(images, offsets, slices, seg_map, interp):
    orient_count = lax.axis_size("orient")
    group_count = lax.axis_size("img") * lax.axis_size("brick")
    group_index = lax.axis_index("img") * lax.axis_size("brick") + lax.axis_index("brick")
    plane = lax.axis_index("orient")
    bricks = orient_count * group_count
    rows = images.shape[0]
    orient = slices.shape[0]
    count = rows * orient_count
    vox = interp.shape[3]
    cos_table, sin_table = (jnp.asarray(t) for t in phase_tables())

    arrived = [images] + [
        lax.ppermute(
            images, "orient", [(i, (i + k) % orient_count) for i in range(orient_count)]
        )
        for k in range(1, orient_count)
    ]

    norm = pl.pallas_call(
        norm_kernel,
        out_shape=jax.ShapeDtypeStruct((8, orient), jnp.float32),
        name="norms",
    )(slices)
    weights, cover = pl.pallas_call(
        interp_kernel,
        grid=(NSEG,),
        in_specs=[pl.BlockSpec((1, 1, SEG, vox), lambda j: (0, j, 0, 0))],
        out_specs=[
            pl.BlockSpec((SEG, 2 * vox), lambda j: (j, 0)),
            pl.BlockSpec((1, 1, vox), lambda j: (j, 0, 0)),
        ],
        out_shape=[
            jax.ShapeDtypeStruct((NSEG * SEG, 2 * vox), jnp.bfloat16),
            jax.ShapeDtypeStruct((NSEG, 1, vox), jnp.float32),
        ],
        name="weights",
    )(interp)

    def whole(shape):
        return pl.BlockSpec(shape, lambda i, where: (0,) * len(shape))

    state = ()
    for k in range(orient_count):
        source = (plane - k) % orient_count
        where = jnp.stack([source, source * group_count + group_index]).astype(jnp.int32)
        first = k == 0
        state_shapes = [
            jax.ShapeDtypeStruct((SHIFTS, count, orient), jnp.bfloat16),
            jax.ShapeDtypeStruct((count, 2 * K), jnp.bfloat16),
            jax.ShapeDtypeStruct((8, count), jnp.float32),
        ]
        state = pl.pallas_call(
            functools.partial(score_kernel, first),
            grid_spec=pltpu.PrefetchScalarGridSpec(
                num_scalar_prefetch=1,
                grid=(1,),
                in_specs=[
                    whole((rows, 2 * K)),
                    pl.BlockSpec((rows, 2), lambda i, where: (where[1], 0)),
                    whole((orient, 2 * K)),
                    whole((8, orient)),
                    whole((PAIRS, K)),
                    whole((PAIRS, K)),
                ]
                + (
                    []
                    if first
                    else [
                        pl.BlockSpec(memory_space=pl.ANY),
                        pl.BlockSpec(memory_space=pl.ANY),
                        whole((8, count)),
                    ]
                ),
                out_specs=[
                    pl.BlockSpec((SHIFTS, rows, orient), lambda i, where: (0, where[0], 0)),
                    pl.BlockSpec((rows, 2 * K), lambda i, where: (where[0], 0)),
                    whole((8, count)),
                ],
                scratch_shapes=[pltpu.VMEM((SHIFTS * rows, 2 * K), jnp.bfloat16)],
            ),
            out_shape=state_shapes,
            input_output_aliases={} if first else {7: 0, 8: 1, 9: 2},
            name="scores",
        )(where, arrived[k], offsets, slices, norm, cos_table, sin_table, *state)
    terms, based, stats = state

    everyone = [stats] + [
        lax.ppermute(stats, "orient", [(i, (i + k) % orient_count) for i in range(orient_count)])
        for k in range(1, orient_count)
    ]
    own_map = lax.dynamic_slice_in_dim(
        seg_map.reshape(orient_count * orient, NSEG), plane * orient, orient, 0
    ).T
    outgoing = pl.pallas_call(
        functools.partial(brick_kernel, orient_count, bricks),
        out_shape=jax.ShapeDtypeStruct((bricks, 2 * K + LANES), jnp.bfloat16),
        scratch_shapes=[pltpu.VMEM((NSEG, SHIFTS * bricks, count), jnp.bfloat16)],
        name="bricks",
    )(terms, based, own_map, cos_table, sin_table, *everyone)
    received = lax.all_to_all(
        outgoing, ("orient", "img", "brick"), split_axis=0, concat_axis=0, tiled=True
    )
    return pl.pallas_call(
        final_kernel,
        out_shape=[
            jax.ShapeDtypeStruct((1, 2, vox), jnp.float32),
            jax.ShapeDtypeStruct((1, 1, vox), jnp.float32),
        ],
        name="insert",
    )(received, weights, cover)


def solution(mesh):
    placed = (
        P(("groups", "orient", "img", "brick"), None),
        P("groups", None),
        P(("groups", "orient"), None),
        P(),
        P(("orient", "img", "brick"), None, None, None),
    )

    def device(*args):
        values, weight = per_device(*args)
        return values, weight.reshape(1, -1)

    return jax.shard_map(
        device,
        mesh=mesh,
        in_specs=placed,
        out_specs=(
            P(("groups", "orient", "img", "brick"), None, None),
            P(("groups", "orient", "img", "brick"), None),
        ),
        check_vma=False,
    )
```

```python
import functools

import jax
import jax.numpy as jnp
import numpy as np
from jax import lax
from jax.experimental import pallas as pl
from jax.experimental.pallas import tpu as pltpu
from jax.sharding import PartitionSpec as P

SHIFTS = 16
SEG = 256
NSEG = 8
K = SEG * NSEG
LANES = 128

frame_side = 64
interp_bits = 4
interp_scale = 1.0 / 256.0
PAIRS = SHIFTS // 2


def phase_tables():
    coef = np.arange(K)
    u = coef % frame_side - frame_side // 2
    w = coef // frame_side
    shift = np.arange(PAIRS)
    dx = 2 * (shift % 4) - 3
    dy = 2 * (shift // 4) - 3
    angle = (u[None, :] * dx[:, None] + w[None, :] * dy[:, None]) % (2 * frame_side)
    angle = angle * (2.0 * np.pi / (2 * frame_side))
    return np.cos(angle).astype(np.float32), np.sin(angle).astype(np.float32)


def cos_sin(steps):
    centred = jnp.bitwise_and(steps + frame_side, 2 * frame_side - 1) - frame_side
    x = centred.astype(jnp.float32) * (np.pi / frame_side)
    x2 = x * x
    c = jnp.full_like(x, (-1.0) ** 10 / float(np.prod(np.arange(1.0, 21.0))))
    s = jnp.full_like(x, (-1.0) ** 10 / float(np.prod(np.arange(1.0, 22.0))))
    for k in range(9, -1, -1):
        c = c * x2 + (-1.0) ** k / float(np.prod(np.arange(1.0, 2 * k + 1.0)))
        s = s * x2 + (-1.0) ** k / float(np.prod(np.arange(1.0, 2 * k + 2.0)))
    return c, s * x


def setup_kernel(bricks, interp_ref, map_ref, weight_ref, cover_ref, hit_ref):
    vox = interp_ref.shape[3]
    covers = []
    for j in range(NSEG):
        raw = interp_ref[0, j]
        high = jnp.right_shift(raw, interp_bits).astype(jnp.float32)
        low = jnp.bitwise_and(raw, (1 << interp_bits) - 1).astype(jnp.float32)
        weight_ref[:, 2 * j * vox : (2 * j + 1) * vox] = high.astype(jnp.bfloat16)
        weight_ref[:, (2 * j + 1) * vox : (2 * j + 2) * vox] = low.astype(jnp.bfloat16)
        covers.append(jnp.sum(raw.astype(jnp.float32), axis=0, keepdims=True) * interp_scale)
    cover_ref[...] = jnp.concatenate(covers, axis=0)
    orient = hit_ref.shape[1]
    rows = orient * NSEG // LANES
    per_row = LANES // NSEG
    start = pl.multiple_of(lax.axis_index("orient") * rows, rows)
    entries = map_ref[pl.ds(start, rows), :].astype(jnp.float32)
    lane = lax.broadcasted_iota(jnp.int32, (rows, LANES), 1)
    masked = jnp.concatenate(
        [jnp.where(lane % NSEG == j, entries, 0.0) for j in range(NSEG)], axis=0
    )
    source = lax.broadcasted_iota(jnp.int32, (LANES, orient), 0) // NSEG
    target = lax.broadcasted_iota(jnp.int32, (LANES, orient), 1) % per_row
    spread = jnp.dot(
        masked,
        (source == target).astype(jnp.float32),
        precision=lax.Precision.HIGHEST,
        preferred_element_type=jnp.float32,
    )
    row = lax.broadcasted_iota(jnp.int32, (rows, orient), 0)
    own = lax.broadcasted_iota(jnp.int32, (rows, orient), 1) // per_row == row
    brick = lax.broadcasted_iota(jnp.int32, (bricks, orient), 0).astype(jnp.float32)
    hits = []
    for j in range(NSEG):
        named = jnp.where(own, spread[j * rows : (j + 1) * rows], 0.0)
        named = jnp.sum(named, axis=0, keepdims=True)
        hits.append((brick == named).astype(jnp.float32))
    hit_ref[...] = jnp.concatenate(hits, axis=0).astype(jnp.bfloat16)


def source_plane(source):
    kind, amount = source
    plane = lax.axis_index("orient")
    if kind == "xor":
        return jnp.bitwise_xor(plane, amount)
    count = lax.axis_size("orient")
    return lax.rem(plane + count - amount, count)


def score_kernel(first, source, choices, *refs):
    images_refs, refs = refs[:choices], refs[choices:]
    offsets_ref, slices_ref, cos_ref, sin_ref = refs[:4]
    if first:
        terms_ref, based_ref, stats_ref, norm_ref, left_ref = refs[4:]
    else:
        norm_ref, _, _, stats_in_ref, _ = refs[4:9]
        terms_ref, based_ref, stats_ref, left_ref = refs[9:]
    inv_noise = 100.0 / K
    rows = images_refs[0].shape[0]
    plane = source_plane(source)
    group = lax.axis_index("img") * lax.axis_size("brick") + lax.axis_index("brick")
    groups = lax.axis_size("img") * lax.axis_size("brick")
    count = offsets_ref.shape[1]
    row = lax.broadcasted_iota(jnp.int32, (rows, count), 0)
    col = lax.broadcasted_iota(jnp.int32, (rows, count), 1)
    mine = col == row + (plane * groups + group) * rows
    off = 2.0 * offsets_ref[...].astype(jnp.float32) - 1.0
    off_x, off_y = (
        jnp.sum(jnp.where(mine, off[i : i + 1, :], 0.0), axis=1, keepdims=True).astype(jnp.int32)
        for i in range(2)
    )
    if first:
        orient = slices_ref.shape[0]
        total = jnp.zeros((orient, LANES), jnp.float32)
        for k in range(2 * K // LANES):
            piece = slices_ref[:, k * LANES : (k + 1) * LANES].astype(jnp.float32)
            total = total + piece * piece
        norm_ref[...] = 0.5 * lax.dot_general(
            jnp.ones((8, LANES), jnp.float32),
            total,
            (((1,), (1,)), ((), ())),
            precision=lax.Precision.HIGHEST,
            preferred_element_type=jnp.float32,
        )
    lane = lax.broadcasted_iota(jnp.int32, (rows, LANES), 1)
    u = jnp.bitwise_and(lane, frame_side - 1) - frame_side // 2
    half = jnp.right_shift(lane, 6)
    c1, s1 = cos_sin(u * off_x + half * off_y)
    c2, s2 = cos_sin(2 * lane * off_y)
    at_end = (lax.axis_index("orient") == 0) | (
        lax.axis_index("orient") == lax.axis_size("orient") - 1
    )

    def pixels(at):
        if choices == 1:
            return images_refs[0][:, at].astype(jnp.float32)
        return jnp.where(at_end, images_refs[0][:, at], images_refs[1][:, at]).astype(jnp.float32)

    for k in range(K // LANES):
        re_at = slice(k * LANES, (k + 1) * LANES)
        im_at = slice(K + k * LANES, K + (k + 1) * LANES)
        x_re, x_im = pixels(re_at), pixels(im_at)
        ck, sk = c2[:, k : k + 1], s2[:, k : k + 1]
        cb = c1 * ck - s1 * sk
        sb = s1 * ck + c1 * sk
        y_re = x_re * cb + x_im * sb
        y_im = x_im * cb - x_re * sb
        where = pl.ds(pl.multiple_of(plane * rows, rows), rows)
        based_ref[where, re_at] = y_re.astype(jnp.bfloat16)
        based_ref[where, im_at] = y_im.astype(jnp.bfloat16)
        re_rows, im_rows = [], []
        for t in range(PAIRS):
            cos_t = cos_ref[t : t + 1, re_at]
            sin_t = sin_ref[t : t + 1, re_at]
            re_rows += [y_re * cos_t, y_im * sin_t]
            im_rows += [y_im * cos_t, -(y_re * sin_t)]
        left_ref[:, re_at] = jnp.concatenate(re_rows, axis=0).astype(jnp.bfloat16)
        left_ref[:, im_at] = jnp.concatenate(im_rows, axis=0).astype(jnp.bfloat16)
    both = lax.dot_general(
        left_ref[...],
        slices_ref[...],
        (((1,), (1,)), ((), ())),
        preferred_element_type=jnp.float32,
    )
    norm = norm_ref[0:1, :]
    scores = []
    for t in range(PAIRS):
        even = both[2 * t * rows : (2 * t + 1) * rows] - norm
        odd = both[(2 * t + 1) * rows : (2 * t + 2) * rows]
        scores += [inv_noise * (even + odd), inv_noise * (even - odd)]
    top = scores[0]
    for s in scores[1:]:
        top = jnp.maximum(top, s)
    top = jnp.max(top, axis=1, keepdims=True)
    mass = jnp.zeros_like(scores[0])
    for i, s in enumerate(scores):
        term = jnp.exp(s - top)
        mass = mass + term
        terms_ref[i, where, :] = term.astype(jnp.bfloat16)
    mass = jnp.sum(mass, axis=1, keepdims=True)
    count = stats_ref.shape[1]
    row = lax.broadcasted_iota(jnp.int32, (rows, count), 0)
    col = lax.broadcasted_iota(jnp.int32, (rows, count), 1)
    mine = col == row + plane * rows
    top_row = jnp.sum(jnp.where(mine, top, 0.0), axis=0, keepdims=True)
    mass_row = jnp.sum(jnp.where(mine, mass, 0.0), axis=0, keepdims=True)
    which = lax.broadcasted_iota(jnp.int32, (8, count), 0)
    part = jnp.where(which == 0, top_row, jnp.where(which == 1, mass_row, 0.0))
    stats_ref[...] = part if first else part + stats_in_ref[...]


def brick_kernel(others, terms_ref, based_ref, hit_ref, cos_ref, sin_ref, *rest):
    stats_refs, (out_ref, pairs_ref, sums_ref) = rest[:others], rest[others:]
    bricks = hit_ref.shape[0] // NSEG
    count = based_ref.shape[0]
    own_top = stats_refs[0][0:1, :]
    top = own_top
    for ref in stats_refs[1:]:
        top = jnp.maximum(top, ref[0:1, :])
    mass = jnp.zeros_like(top)
    for ref in stats_refs:
        mass = mass + ref[1:2, :] * jnp.exp(ref[0:1, :] - top)
    factor = jnp.exp(own_top - top) / mass
    mass_sum = jnp.zeros((NSEG * bricks, count), jnp.float32)
    for t in range(PAIRS):
        plus, minus = (
            lax.dot_general(
                hit_ref[...],
                terms_ref[2 * t + i],
                (((1,), (1,)), ((), ())),
                preferred_element_type=jnp.float32,
            )
            for i in range(2)
        )
        even = (plus + minus) * factor
        odd = (plus - minus) * factor
        mass_sum = mass_sum + even
        for j in range(NSEG):
            at = slice(j * bricks, (j + 1) * bricks)
            pairs_ref[j, t * bricks : (t + 1) * bricks, :] = even[at].astype(jnp.bfloat16)
            pairs_ref[j, (PAIRS + t) * bricks : (PAIRS + t + 1) * bricks, :] = odd[at].astype(
                jnp.bfloat16
            )
    mass_sum = jnp.sum(mass_sum, axis=1, keepdims=True)
    mass_high = mass_sum.astype(jnp.bfloat16).astype(jnp.float32)
    mass_low = mass_sum - mass_high
    lane = lax.broadcasted_iota(jnp.int32, (bricks, LANES), 1)
    for j in range(NSEG):
        at = slice(j * bricks, (j + 1) * bricks)
        re_at = slice(j * SEG, (j + 1) * SEG)
        im_at = slice(K + j * SEG, K + (j + 1) * SEG)
        left = pairs_ref[j]
        with_re = jnp.dot(left, based_ref[:, re_at], preferred_element_type=jnp.float32)
        with_im = jnp.dot(left, based_ref[:, im_at], preferred_element_type=jnp.float32)
        sum_re = jnp.zeros((bricks, SEG), jnp.float32)
        sum_im = jnp.zeros((bricks, SEG), jnp.float32)
        for t in range(PAIRS):
            cos_t = cos_ref[t : t + 1, re_at]
            sin_t = sin_ref[t : t + 1, re_at]
            even = slice(t * bricks, (t + 1) * bricks)
            odd = slice((PAIRS + t) * bricks, (PAIRS + t + 1) * bricks)
            sum_re = sum_re + cos_t * with_re[even] + sin_t * with_im[odd]
            sum_im = sum_im + cos_t * with_im[even] - sin_t * with_re[odd]
        sums_ref[:, j, :SEG] = sum_re
        sums_ref[:, j, SEG : 2 * SEG] = sum_im
        sums_ref[:, j, 2 * SEG :] = jnp.where(
            lane == 0, mass_high[at], jnp.where(lane == 1, mass_low[at], 0.0)
        )
    out_ref[...] = sums_ref[...].astype(jnp.bfloat16)


def final_kernel(arrived_ref, weight_ref, cover_ref, values_ref, mass_ref):
    vox = cover_ref.shape[1]
    total = jnp.sum(arrived_ref[...].astype(jnp.float32), axis=0)
    re, im = total[:, :SEG], total[:, SEG : 2 * SEG]
    seg_mass = total[:, 2 * SEG : 2 * SEG + 1] + total[:, 2 * SEG + 1 : 2 * SEG + 2]
    parts = []
    for _ in range(3):
        high = [x.astype(jnp.bfloat16).astype(jnp.float32) for x in (re, im)]
        parts += high
        re, im = re - high[0], im - high[1]
    left = jnp.concatenate(parts, axis=0).astype(jnp.bfloat16)
    row = lax.broadcasted_iota(jnp.int32, (left.shape[0], 2 * vox), 0) % NSEG
    product = jnp.zeros((left.shape[0], 2 * vox), jnp.float32)
    for j in range(NSEG):
        full = jnp.dot(
            left,
            weight_ref[:, 2 * j * vox : 2 * (j + 1) * vox],
            preferred_element_type=jnp.float32,
        )
        product = jnp.where(row == j, full, product)
    step = 2 * NSEG
    product = product[:step] + product[step : 2 * step] + product[2 * step :]
    for p in range(2):
        line = jnp.sum(product[p * NSEG : (p + 1) * NSEG], axis=0, keepdims=True)
        values_ref[0, p : p + 1, :] = (
            line[:, :vox] * float(1 << interp_bits) + line[:, vox:]
        ) * interp_scale
    mass_ref[0] = jnp.sum(seg_mass * cover_ref[...], axis=0, keepdims=True)


def on_chip(*arrays):
    return [pltpu.with_memory_space_constraint(x, pltpu.VMEM) for x in arrays]


def call(kernel, name, out_shape, inputs, scratch=(), aliases=None, chip_out=True):
    spec = pl.BlockSpec(memory_space=pltpu.VMEM)
    single = not isinstance(out_shape, list)
    shapes = [out_shape] if single else out_shape
    if chip_out:
        shapes = [pltpu.VMEM(x.shape, x.dtype) for x in shapes]
    out = pl.pallas_call(
        kernel,
        in_specs=[spec] * len(inputs),
        out_specs=[spec] * len(shapes),
        out_shape=shapes,
        scratch_shapes=list(scratch),
        input_output_aliases=aliases or {},
        compiler_params=pltpu.CompilerParams(vmem_limit_bytes=VMEM_LIMIT),
        name=name,
    )(*inputs)
    return out[0] if single else out


VMEM_LIMIT = 24 * 2**20


def swap(array, amount):
    count = lax.axis_size("orient")
    return lax.ppermute(array, "orient", [(i, i ^ amount) for i in range(count)])


def shift(array, amount):
    count = lax.axis_size("orient")
    return lax.ppermute(array, "orient", [(i, (i + amount) % count) for i in range(count)])


def image_rounds(images):
    count = lax.axis_size("orient")
    rounds = [(("shift", 0), [images])]
    if count != 4:
        return rounds + [(("shift", k), [shift(images, k)]) for k in range(1, count)]
    far = swap(images, 2)
    near = swap(images, 1)
    relayed = lax.ppermute(far, "orient", [(1, 0), (2, 3)])
    middle = lax.ppermute(images, "orient", [(1, 2), (2, 1)])
    return rounds + [
        (("xor", 1), [near]),
        (("xor", 2), [far]),
        (("xor", 3), [relayed, middle]),
    ]


def everyone(array):
    count = lax.axis_size("orient")
    if count != 4:
        return [array] + [shift(array, k) for k in range(1, count)]
    return [array] + [swap(array, k) for k in (3, 2, 1)]


def per_device(images, offsets, slices, seg_map, interp):
    orient_count = lax.axis_size("orient")
    group_count = lax.axis_size("img") * lax.axis_size("brick")
    bricks = orient_count * group_count
    rows = images.shape[0]
    orient = slices.shape[0]
    count = rows * orient_count
    vox = interp.shape[3]
    cos_table, sin_table = on_chip(*(jnp.asarray(t) for t in phase_tables()))
    f32, bf16 = jnp.float32, jnp.bfloat16

    rounds = image_rounds(images)
    weights, cover, hit = call(
        functools.partial(setup_kernel, bricks),
        "setup",
        [
            jax.ShapeDtypeStruct((SEG, 2 * NSEG * vox), bf16),
            jax.ShapeDtypeStruct((NSEG, vox), f32),
            jax.ShapeDtypeStruct((NSEG * bricks, orient), bf16),
        ],
        [interp, seg_map.reshape(-1, LANES)],
    )
    slices_v, offsets_v = on_chip(slices, offsets.T)
    state_shapes = [
        jax.ShapeDtypeStruct((SHIFTS, count, orient), bf16),
        jax.ShapeDtypeStruct((count, 2 * K), bf16),
        jax.ShapeDtypeStruct((8, count), f32),
    ]
    for k, (source, arrays) in enumerate(rounds):
        first = k == 0
        inputs = on_chip(*arrays) + [offsets_v, slices_v, cos_table, sin_table]
        if not first:
            inputs += on_chip(norm, *state, cover)
        at = len(arrays) + 5
        out = call(
            functools.partial(score_kernel, first, source, len(arrays)),
            "scores",
            state_shapes + ([jax.ShapeDtypeStruct((8, orient), f32)] if first else []),
            inputs,
            scratch=[pltpu.VMEM((SHIFTS * rows, 2 * K), bf16)],
            aliases={} if first else {at + i: i for i in range(3)},
        )
        if first:
            norm = out[3]
        state = out[:3]
    terms, based, stats = state
    outgoing = call(
        functools.partial(brick_kernel, orient_count),
        "bricks",
        jax.ShapeDtypeStruct((bricks, NSEG, 2 * SEG + LANES), bf16),
        on_chip(terms, based, hit) + [cos_table, sin_table] + on_chip(*everyone(stats)),
        scratch=[
            pltpu.VMEM((NSEG, SHIFTS * bricks, count), bf16),
            pltpu.VMEM((bricks, NSEG, 2 * SEG + LANES), f32),
        ],
    )
    received = lax.all_to_all(
        outgoing, ("orient", "img", "brick"), split_axis=0, concat_axis=0, tiled=True
    )
    return call(
        final_kernel,
        "insert",
        [
            jax.ShapeDtypeStruct((1, 2, vox), f32),
            jax.ShapeDtypeStruct((1, 1, vox), f32),
        ],
        on_chip(received, weights, cover),
        chip_out=False,
    )


def solution(mesh):
    placed = (
        P(("groups", "orient", "img", "brick"), None),
        P("groups", None),
        P(("groups", "orient"), None),
        P(),
        P(("orient", "img", "brick"), None, None, None),
    )

    def device(*args):
        values, weight = per_device(*args)
        return values, weight.reshape(1, -1)

    return jax.shard_map(
        device,
        mesh=mesh,
        in_specs=placed,
        out_specs=(
            P(("groups", "orient", "img", "brick"), None, None),
            P(("groups", "orient", "img", "brick"), None),
        ),
        check_vma=False,
    )
```

```python
import functools

import jax
import jax.numpy as jnp
import numpy as np
from jax import lax
from jax.experimental import pallas as pl
from jax.experimental.pallas import tpu as pltpu
from jax.sharding import PartitionSpec as P

SHIFTS = 16
SEG = 256
NSEG = 8
K = SEG * NSEG
LANES = 128

frame_side = 64
interp_bits = 4
interp_scale = 1.0 / 256.0
PAIRS = SHIFTS // 2


def cos_sin(steps):
    centred = jnp.bitwise_and(steps + frame_side, 2 * frame_side - 1) - frame_side
    x = centred.astype(jnp.float32) * (np.pi / frame_side)
    x2 = x * x
    c = jnp.full_like(x, (-1.0) ** 10 / float(np.prod(np.arange(1.0, 21.0))))
    s = jnp.full_like(x, (-1.0) ** 10 / float(np.prod(np.arange(1.0, 22.0))))
    for k in range(9, -1, -1):
        c = c * x2 + (-1.0) ** k / float(np.prod(np.arange(1.0, 2 * k + 1.0)))
        s = s * x2 + (-1.0) ** k / float(np.prod(np.arange(1.0, 2 * k + 2.0)))
    return c, s * x


def setup_kernel(
    bricks,
    interp_hbm,
    map_hbm,
    images_hbm,
    offsets_hbm,
    weight_ref,
    cover_ref,
    hit_ref,
    cos_ref,
    sin_ref,
    images_ref,
    offsets_ref,
    interp_ref,
    map_ref,
    sems,
):
    small = [
        pltpu.make_async_copy(source, target, sems.at[NSEG + i])
        for i, (source, target) in enumerate(
            [(images_hbm, images_ref), (offsets_hbm, offsets_ref), (map_hbm, map_ref)]
        )
    ]
    large = [
        pltpu.make_async_copy(interp_hbm.at[0, j], interp_ref.at[j], sems.at[j])
        for j in range(NSEG)
    ]
    for copy in small + large:
        copy.start()
    coef = lax.broadcasted_iota(jnp.int32, (PAIRS, K), 1)
    pair = lax.broadcasted_iota(jnp.int32, (PAIRS, K), 0)
    u = jnp.bitwise_and(coef, frame_side - 1) - frame_side // 2
    w = coef // frame_side
    dx = 2 * jnp.bitwise_and(pair, 3) - 3
    dy = 2 * (pair // 4) - 3
    cos_ref[...], sin_ref[...] = cos_sin(u * dx + w * dy)
    for copy in small:
        copy.wait()
    vox = interp_ref.shape[2]
    covers = []
    for j in range(NSEG):
        large[j].wait()
        raw = interp_ref[j]
        high = jnp.right_shift(raw, interp_bits).astype(jnp.float32)
        low = jnp.bitwise_and(raw, (1 << interp_bits) - 1).astype(jnp.float32)
        weight_ref[:, 2 * j * vox : (2 * j + 1) * vox] = high.astype(jnp.bfloat16)
        weight_ref[:, (2 * j + 1) * vox : (2 * j + 2) * vox] = low.astype(jnp.bfloat16)
        covers.append(jnp.sum(raw.astype(jnp.float32), axis=0, keepdims=True) * interp_scale)
    cover_ref[...] = jnp.concatenate(covers, axis=0)
    orient = hit_ref.shape[1]
    rows = orient * NSEG // LANES
    per_row = LANES // NSEG
    start = pl.multiple_of(lax.axis_index("orient") * rows, rows)
    entries = map_ref[pl.ds(start, rows), :].astype(jnp.float32)
    lane = lax.broadcasted_iota(jnp.int32, (rows, LANES), 1)
    masked = jnp.concatenate(
        [jnp.where(lane % NSEG == j, entries, 0.0) for j in range(NSEG)], axis=0
    )
    source = lax.broadcasted_iota(jnp.int32, (LANES, orient), 0) // NSEG
    target = lax.broadcasted_iota(jnp.int32, (LANES, orient), 1) % per_row
    spread = jnp.dot(
        masked,
        (source == target).astype(jnp.float32),
        precision=lax.Precision.HIGHEST,
        preferred_element_type=jnp.float32,
    )
    row = lax.broadcasted_iota(jnp.int32, (rows, orient), 0)
    own = lax.broadcasted_iota(jnp.int32, (rows, orient), 1) // per_row == row
    brick = lax.broadcasted_iota(jnp.int32, (bricks, orient), 0).astype(jnp.float32)
    hits = []
    for j in range(NSEG):
        named = jnp.where(own, spread[j * rows : (j + 1) * rows], 0.0)
        named = jnp.sum(named, axis=0, keepdims=True)
        hits.append((brick == named).astype(jnp.float32))
    hit_ref[...] = jnp.concatenate(hits, axis=0).astype(jnp.bfloat16)


def source_plane(source):
    kind, amount = source
    plane = lax.axis_index("orient")
    if kind == "xor":
        return jnp.bitwise_xor(plane, amount)
    count = lax.axis_size("orient")
    return lax.rem(plane + count - amount, count)


def score_kernel(first, source, choices, *refs):
    images_refs, refs = refs[:choices], refs[choices:]
    offsets_ref, slices_ref, cos_ref, sin_ref = refs[:4]
    if first:
        terms_ref, based_ref, stats_ref, norm_ref, left_ref = refs[4:]
    else:
        norm_ref, _, _, stats_in_ref = refs[4:8]
        terms_ref, based_ref, stats_ref, left_ref = refs[8:]
    inv_noise = 100.0 / K
    rows = images_refs[0].shape[0]
    plane = source_plane(source)
    group = lax.axis_index("img") * lax.axis_size("brick") + lax.axis_index("brick")
    groups = lax.axis_size("img") * lax.axis_size("brick")
    count = offsets_ref.shape[1]
    row = lax.broadcasted_iota(jnp.int32, (rows, count), 0)
    col = lax.broadcasted_iota(jnp.int32, (rows, count), 1)
    mine = col == row + (plane * groups + group) * rows
    off = 2.0 * offsets_ref[...].astype(jnp.float32) - 1.0
    off_x, off_y = (
        jnp.sum(jnp.where(mine, off[i : i + 1, :], 0.0), axis=1, keepdims=True).astype(jnp.int32)
        for i in range(2)
    )
    if first:
        orient = slices_ref.shape[0]
        total = jnp.zeros((orient, LANES), jnp.float32)
        for k in range(2 * K // LANES):
            piece = slices_ref[:, k * LANES : (k + 1) * LANES].astype(jnp.float32)
            total = total + piece * piece
        norm_ref[...] = 0.5 * lax.dot_general(
            jnp.ones((8, LANES), jnp.float32),
            total,
            (((1,), (1,)), ((), ())),
            precision=lax.Precision.HIGHEST,
            preferred_element_type=jnp.float32,
        )
    lane = lax.broadcasted_iota(jnp.int32, (rows, LANES), 1)
    u = jnp.bitwise_and(lane, frame_side - 1) - frame_side // 2
    half = jnp.right_shift(lane, 6)
    c1, s1 = cos_sin(u * off_x + half * off_y)
    c2, s2 = cos_sin(2 * lane * off_y)
    at_end = (lax.axis_index("orient") == 0) | (
        lax.axis_index("orient") == lax.axis_size("orient") - 1
    )

    def pixels(at):
        if choices == 1:
            return images_refs[0][:, at].astype(jnp.float32)
        return jnp.where(at_end, images_refs[0][:, at], images_refs[1][:, at]).astype(jnp.float32)

    for k in range(K // LANES):
        re_at = slice(k * LANES, (k + 1) * LANES)
        im_at = slice(K + k * LANES, K + (k + 1) * LANES)
        x_re, x_im = pixels(re_at), pixels(im_at)
        ck, sk = c2[:, k : k + 1], s2[:, k : k + 1]
        cb = c1 * ck - s1 * sk
        sb = s1 * ck + c1 * sk
        y_re = x_re * cb + x_im * sb
        y_im = x_im * cb - x_re * sb
        where = pl.ds(pl.multiple_of(plane * rows, rows), rows)
        based_ref[where, re_at] = y_re.astype(jnp.bfloat16)
        based_ref[where, im_at] = y_im.astype(jnp.bfloat16)
        re_rows, im_rows = [], []
        for t in range(PAIRS):
            cos_t = cos_ref[t : t + 1, re_at]
            sin_t = sin_ref[t : t + 1, re_at]
            re_rows += [y_re * cos_t, y_im * sin_t]
            im_rows += [y_im * cos_t, -(y_re * sin_t)]
        left_ref[:, re_at] = jnp.concatenate(re_rows, axis=0).astype(jnp.bfloat16)
        left_ref[:, im_at] = jnp.concatenate(im_rows, axis=0).astype(jnp.bfloat16)
    both = lax.dot_general(
        left_ref[...],
        slices_ref[...],
        (((1,), (1,)), ((), ())),
        preferred_element_type=jnp.float32,
    )
    norm = norm_ref[0:1, :]
    scores = []
    for t in range(PAIRS):
        even = both[2 * t * rows : (2 * t + 1) * rows] - norm
        odd = both[(2 * t + 1) * rows : (2 * t + 2) * rows]
        scores += [inv_noise * (even + odd), inv_noise * (even - odd)]
    top = scores[0]
    for s in scores[1:]:
        top = jnp.maximum(top, s)
    top = jnp.max(top, axis=1, keepdims=True)
    mass = jnp.zeros_like(scores[0])
    for i, s in enumerate(scores):
        term = jnp.exp(s - top)
        mass = mass + term
        terms_ref[i, where, :] = term.astype(jnp.bfloat16)
    mass = jnp.sum(mass, axis=1, keepdims=True)
    count = stats_ref.shape[1]
    row = lax.broadcasted_iota(jnp.int32, (rows, count), 0)
    col = lax.broadcasted_iota(jnp.int32, (rows, count), 1)
    mine = col == row + plane * rows
    top_row = jnp.sum(jnp.where(mine, top, 0.0), axis=0, keepdims=True)
    mass_row = jnp.sum(jnp.where(mine, mass, 0.0), axis=0, keepdims=True)
    which = lax.broadcasted_iota(jnp.int32, (8, count), 0)
    part = jnp.where(which == 0, top_row, jnp.where(which == 1, mass_row, 0.0))
    stats_ref[...] = part if first else part + stats_in_ref[...]


def brick_kernel(others, terms_ref, based_ref, hit_ref, cos_ref, sin_ref, *rest):
    stats_refs, (out_ref, pairs_ref, sums_ref) = rest[:others], rest[others:]
    bricks = hit_ref.shape[0] // NSEG
    count = based_ref.shape[0]
    own_top = stats_refs[0][0:1, :]
    top = own_top
    for ref in stats_refs[1:]:
        top = jnp.maximum(top, ref[0:1, :])
    mass = jnp.zeros_like(top)
    for ref in stats_refs:
        mass = mass + ref[1:2, :] * jnp.exp(ref[0:1, :] - top)
    factor = jnp.exp(own_top - top) / mass
    mass_sum = jnp.zeros((NSEG * bricks, count), jnp.float32)
    for t in range(PAIRS):
        plus, minus = (
            lax.dot_general(
                hit_ref[...],
                terms_ref[2 * t + i],
                (((1,), (1,)), ((), ())),
                preferred_element_type=jnp.float32,
            )
            for i in range(2)
        )
        even = (plus + minus) * factor
        odd = (plus - minus) * factor
        mass_sum = mass_sum + even
        for j in range(NSEG):
            at = slice(j * bricks, (j + 1) * bricks)
            pairs_ref[j, t * bricks : (t + 1) * bricks, :] = even[at].astype(jnp.bfloat16)
            pairs_ref[j, (PAIRS + t) * bricks : (PAIRS + t + 1) * bricks, :] = odd[at].astype(
                jnp.bfloat16
            )
    mass_sum = jnp.sum(mass_sum, axis=1, keepdims=True)
    mass_high = mass_sum.astype(jnp.bfloat16).astype(jnp.float32)
    mass_low = mass_sum - mass_high
    lane = lax.broadcasted_iota(jnp.int32, (bricks, LANES), 1)
    for j in range(NSEG):
        at = slice(j * bricks, (j + 1) * bricks)
        re_at = slice(j * SEG, (j + 1) * SEG)
        im_at = slice(K + j * SEG, K + (j + 1) * SEG)
        left = pairs_ref[j]
        with_re = jnp.dot(left, based_ref[:, re_at], preferred_element_type=jnp.float32)
        with_im = jnp.dot(left, based_ref[:, im_at], preferred_element_type=jnp.float32)
        sum_re = jnp.zeros((bricks, SEG), jnp.float32)
        sum_im = jnp.zeros((bricks, SEG), jnp.float32)
        for t in range(PAIRS):
            cos_t = cos_ref[t : t + 1, re_at]
            sin_t = sin_ref[t : t + 1, re_at]
            even = slice(t * bricks, (t + 1) * bricks)
            odd = slice((PAIRS + t) * bricks, (PAIRS + t + 1) * bricks)
            sum_re = sum_re + cos_t * with_re[even] + sin_t * with_im[odd]
            sum_im = sum_im + cos_t * with_im[even] - sin_t * with_re[odd]
        sums_ref[:, j, :SEG] = sum_re
        sums_ref[:, j, SEG : 2 * SEG] = sum_im
        sums_ref[:, j, 2 * SEG :] = jnp.where(
            lane == 0, mass_high[at], jnp.where(lane == 1, mass_low[at], 0.0)
        )
    out_ref[...] = sums_ref[...].astype(jnp.bfloat16)


def final_kernel(arrived_ref, weight_ref, cover_ref, values_ref, mass_ref):
    vox = cover_ref.shape[1]
    total = jnp.sum(arrived_ref[...].astype(jnp.float32), axis=0)
    re, im = total[:, :SEG], total[:, SEG : 2 * SEG]
    seg_mass = total[:, 2 * SEG : 2 * SEG + 1] + total[:, 2 * SEG + 1 : 2 * SEG + 2]
    parts = []
    for _ in range(3):
        high = [x.astype(jnp.bfloat16).astype(jnp.float32) for x in (re, im)]
        parts += high
        re, im = re - high[0], im - high[1]
    left = jnp.concatenate(parts, axis=0).astype(jnp.bfloat16)
    row = lax.broadcasted_iota(jnp.int32, (left.shape[0], 2 * vox), 0) % NSEG
    product = jnp.zeros((left.shape[0], 2 * vox), jnp.float32)
    for j in range(NSEG):
        full = jnp.dot(
            left,
            weight_ref[:, 2 * j * vox : 2 * (j + 1) * vox],
            preferred_element_type=jnp.float32,
        )
        product = jnp.where(row == j, full, product)
    step = 2 * NSEG
    product = product[:step] + product[step : 2 * step] + product[2 * step :]
    for p in range(2):
        line = jnp.sum(product[p * NSEG : (p + 1) * NSEG], axis=0, keepdims=True)
        values_ref[0, p : p + 1, :] = (
            line[:, :vox] * float(1 << interp_bits) + line[:, vox:]
        ) * interp_scale
    mass_ref[0] = jnp.sum(seg_mass * cover_ref[...], axis=0, keepdims=True)


def on_chip(*arrays):
    return [pltpu.with_memory_space_constraint(x, pltpu.VMEM) for x in arrays]


def call(kernel, name, out_shape, inputs, scratch=(), aliases=None, chip_out=True, hbm_in=False):
    spec = pl.BlockSpec(memory_space=pltpu.VMEM)
    in_spec = pl.BlockSpec(memory_space=pltpu.HBM) if hbm_in else spec
    single = not isinstance(out_shape, list)
    shapes = [out_shape] if single else out_shape
    if chip_out:
        shapes = [pltpu.VMEM(x.shape, x.dtype) for x in shapes]
    out = pl.pallas_call(
        kernel,
        in_specs=[in_spec] * len(inputs),
        out_specs=[spec] * len(shapes),
        out_shape=shapes,
        scratch_shapes=list(scratch),
        input_output_aliases=aliases or {},
        compiler_params=pltpu.CompilerParams(vmem_limit_bytes=VMEM_LIMIT),
        name=name,
    )(*inputs)
    return out[0] if single else out


VMEM_LIMIT = 24 * 2**20


def swap(array, amount):
    count = lax.axis_size("orient")
    return lax.ppermute(array, "orient", [(i, i ^ amount) for i in range(count)])


def shift(array, amount):
    count = lax.axis_size("orient")
    return lax.ppermute(array, "orient", [(i, (i + amount) % count) for i in range(count)])


def everyone(array):
    count = lax.axis_size("orient")
    if count != 4:
        return [array] + [shift(array, k) for k in range(1, count)]
    return [array] + [swap(array, k) for k in (3, 2, 1)]


def per_device(images, offsets, slices, seg_map, interp):
    orient_count = lax.axis_size("orient")
    group_count = lax.axis_size("img") * lax.axis_size("brick")
    bricks = orient_count * group_count
    rows = images.shape[0]
    orient = slices.shape[0]
    count = rows * orient_count
    vox = interp.shape[3]
    f32, bf16 = jnp.float32, jnp.bfloat16
    relay = orient_count == 4
    if relay:
        far = swap(images, 2)
        near = swap(images, 1)
        waiting = [(("xor", 1), [near])]
    else:
        waiting = [(("shift", k), [shift(images, k)]) for k in range(1, orient_count)]

    weights, cover, hit, cos_table, sin_table, own, offsets_v = call(
        functools.partial(setup_kernel, bricks),
        "setup",
        [
            jax.ShapeDtypeStruct((SEG, 2 * NSEG * vox), bf16),
            jax.ShapeDtypeStruct((NSEG, vox), f32),
            jax.ShapeDtypeStruct((NSEG * bricks, orient), bf16),
            jax.ShapeDtypeStruct((PAIRS, K), f32),
            jax.ShapeDtypeStruct((PAIRS, K), f32),
            jax.ShapeDtypeStruct(images.shape, bf16),
            jax.ShapeDtypeStruct(offsets.shape[::-1], jnp.int32),
        ],
        [
            pltpu.with_memory_space_constraint(x, pltpu.HBM)
            for x in (interp, seg_map.reshape(-1, LANES), images, offsets.T)
        ],
        scratch=[
            pltpu.VMEM(interp.shape[1:], jnp.int32),
            pltpu.VMEM((seg_map.shape[0] // LANES, LANES), jnp.int32),
            pltpu.SemaphoreType.DMA((NSEG + 3,)),
        ],
        hbm_in=True,
    )
    constant = on_chip(offsets_v, slices, cos_table, sin_table)
    state_shapes = [
        jax.ShapeDtypeStruct((SHIFTS, count, orient), bf16),
        jax.ShapeDtypeStruct((count, 2 * K), bf16),
        jax.ShapeDtypeStruct((8, count), f32),
    ]

    def scored(source, arrays, earlier):
        first = earlier is None
        inputs = on_chip(*arrays) + constant
        if not first:
            inputs += on_chip(*earlier)
        at = len(arrays) + 5
        return call(
            functools.partial(score_kernel, first, source, len(arrays)),
            "scores",
            state_shapes + ([jax.ShapeDtypeStruct((8, orient), f32)] if first else []),
            inputs,
            scratch=[pltpu.VMEM((SHIFTS * rows, 2 * K), bf16)],
            aliases={} if first else {at + i: i for i in range(3)},
        )

    *state, norm = scored(("shift", 0), [own], None)
    for source, arrays in waiting:
        state = scored(source, arrays, [norm, *state])
    if relay:
        terms, based, stats = state
        stats, far, again = lax.optimization_barrier((stats, far, images))
        state = [terms, based, stats]
        relayed = lax.ppermute(far, "orient", [(1, 0), (2, 3)])
        middle = lax.ppermute(again, "orient", [(1, 2), (2, 1)])
        state = scored(("xor", 2), [far], [norm, *state])
        state = scored(("xor", 3), [relayed, middle], [norm, *state])
    terms, based, stats = state
    outgoing = call(
        functools.partial(brick_kernel, orient_count),
        "bricks",
        jax.ShapeDtypeStruct((bricks, NSEG, 2 * SEG + LANES), bf16),
        on_chip(terms, based, hit) + [cos_table, sin_table] + on_chip(*everyone(stats)),
        scratch=[
            pltpu.VMEM((NSEG, SHIFTS * bricks, count), bf16),
            pltpu.VMEM((bricks, NSEG, 2 * SEG + LANES), f32),
        ],
    )
    received = lax.all_to_all(
        outgoing, ("orient", "img", "brick"), split_axis=0, concat_axis=0, tiled=True
    )
    return call(
        final_kernel,
        "insert",
        [
            jax.ShapeDtypeStruct((1, 2, vox), f32),
            jax.ShapeDtypeStruct((1, 1, vox), f32),
        ],
        on_chip(received, weights, cover),
        chip_out=False,
    )


def solution(mesh):
    placed = (
        P(("groups", "orient", "img", "brick"), None),
        P("groups", None),
        P(("groups", "orient"), None),
        P(),
        P(("orient", "img", "brick"), None, None, None),
    )

    def device(*args):
        values, weight = per_device(*args)
        return values, weight.reshape(1, -1)

    return jax.shard_map(
        device,
        mesh=mesh,
        in_specs=placed,
        out_specs=(
            P(("groups", "orient", "img", "brick"), None, None),
            P(("groups", "orient", "img", "brick"), None),
        ),
        check_vma=False,
    )
```

```python
import functools

import jax
import jax.numpy as jnp
import numpy as np
from jax import lax
from jax.experimental import pallas as pl
from jax.experimental.pallas import tpu as pltpu
from jax.sharding import PartitionSpec as P

SHIFTS = 16
SEG = 256
NSEG = 8
K = SEG * NSEG
LANES = 128

frame_side = 64
interp_bits = 4
interp_scale = 1.0 / 256.0
PAIRS = SHIFTS // 2


def cos_sin(steps):
    centred = jnp.bitwise_and(steps + frame_side, 2 * frame_side - 1) - frame_side
    x = centred.astype(jnp.float32) * (np.pi / frame_side)
    x2 = x * x
    c = jnp.full_like(x, (-1.0) ** 10 / float(np.prod(np.arange(1.0, 21.0))))
    s = jnp.full_like(x, (-1.0) ** 10 / float(np.prod(np.arange(1.0, 22.0))))
    for k in range(9, -1, -1):
        c = c * x2 + (-1.0) ** k / float(np.prod(np.arange(1.0, 2 * k + 1.0)))
        s = s * x2 + (-1.0) ** k / float(np.prod(np.arange(1.0, 2 * k + 2.0)))
    return c, s * x


def setup_kernel(
    bricks,
    interp_hbm,
    map_hbm,
    images_hbm,
    offsets_hbm,
    weight_ref,
    cover_ref,
    hit_ref,
    cos_ref,
    sin_ref,
    images_ref,
    offsets_ref,
    interp_ref,
    map_ref,
    sems,
):
    small = [
        pltpu.make_async_copy(source, target, sems.at[NSEG + i])
        for i, (source, target) in enumerate(
            [(images_hbm, images_ref), (offsets_hbm, offsets_ref), (map_hbm, map_ref)]
        )
    ]
    large = [
        pltpu.make_async_copy(interp_hbm.at[0, j], interp_ref.at[j], sems.at[j])
        for j in range(NSEG)
    ]
    for copy in small + large:
        copy.start()
    coef = lax.broadcasted_iota(jnp.int32, (PAIRS, K), 1)
    pair = lax.broadcasted_iota(jnp.int32, (PAIRS, K), 0)
    u = jnp.bitwise_and(coef, frame_side - 1) - frame_side // 2
    w = coef // frame_side
    dx = 2 * jnp.bitwise_and(pair, 3) - 3
    dy = 2 * (pair // 4) - 3
    cos_ref[...], sin_ref[...] = cos_sin(u * dx + w * dy)
    for copy in small:
        copy.wait()
    vox = interp_ref.shape[2]
    covers = []
    for j in range(NSEG):
        large[j].wait()
        raw = interp_ref[j]
        high = jnp.right_shift(raw, interp_bits).astype(jnp.float32)
        low = jnp.bitwise_and(raw, (1 << interp_bits) - 1).astype(jnp.float32)
        weight_ref[:, 2 * j * vox : (2 * j + 1) * vox] = high.astype(jnp.bfloat16)
        weight_ref[:, (2 * j + 1) * vox : (2 * j + 2) * vox] = low.astype(jnp.bfloat16)
        covers.append(jnp.sum(raw.astype(jnp.float32), axis=0, keepdims=True) * interp_scale)
    cover_ref[...] = jnp.concatenate(covers, axis=0)
    orient = hit_ref.shape[1]
    rows = orient * NSEG // LANES
    per_row = LANES // NSEG
    start = pl.multiple_of(lax.axis_index("orient") * rows, rows)
    entries = map_ref[pl.ds(start, rows), :].astype(jnp.float32)
    lane = lax.broadcasted_iota(jnp.int32, (rows, LANES), 1)
    masked = jnp.concatenate(
        [jnp.where(lane % NSEG == j, entries, 0.0) for j in range(NSEG)], axis=0
    )
    source = lax.broadcasted_iota(jnp.int32, (LANES, orient), 0) // NSEG
    target = lax.broadcasted_iota(jnp.int32, (LANES, orient), 1) % per_row
    spread = jnp.dot(
        masked,
        (source == target).astype(jnp.float32),
        precision=lax.Precision.HIGHEST,
        preferred_element_type=jnp.float32,
    )
    row = lax.broadcasted_iota(jnp.int32, (rows, orient), 0)
    own = lax.broadcasted_iota(jnp.int32, (rows, orient), 1) // per_row == row
    brick = lax.broadcasted_iota(jnp.int32, (bricks, orient), 0).astype(jnp.float32)
    hits = []
    for j in range(NSEG):
        named = jnp.where(own, spread[j * rows : (j + 1) * rows], 0.0)
        named = jnp.sum(named, axis=0, keepdims=True)
        hits.append((brick == named).astype(jnp.float32))
    hit_ref[...] = jnp.concatenate(hits, axis=0).astype(jnp.bfloat16)


def source_plane(source):
    factor, offset, modulus = source
    return lax.rem(factor * lax.axis_index("orient") + offset, modulus)


def score_kernel(first, source, choices, *refs):
    images_refs, refs = refs[:choices], refs[choices:]
    offsets_ref, slices_ref, cos_ref, sin_ref = refs[:4]
    if first:
        terms_ref, based_ref, stats_ref, norm_ref, left_ref = refs[4:]
    else:
        norm_ref, _, _, stats_in_ref = refs[4:8]
        terms_ref, based_ref, stats_ref, left_ref = refs[8:]
    inv_noise = 100.0 / K
    rows = images_refs[0].shape[0]
    plane = source_plane(source)
    group = lax.axis_index("img") * lax.axis_size("brick") + lax.axis_index("brick")
    groups = lax.axis_size("img") * lax.axis_size("brick")
    count = offsets_ref.shape[1]
    row = lax.broadcasted_iota(jnp.int32, (rows, count), 0)
    col = lax.broadcasted_iota(jnp.int32, (rows, count), 1)
    mine = col == row + (plane * groups + group) * rows
    off = 2.0 * offsets_ref[...].astype(jnp.float32) - 1.0
    off_x, off_y = (
        jnp.sum(jnp.where(mine, off[i : i + 1, :], 0.0), axis=1, keepdims=True).astype(jnp.int32)
        for i in range(2)
    )
    if first:
        orient = slices_ref.shape[0]
        total = jnp.zeros((orient, LANES), jnp.float32)
        for k in range(2 * K // LANES):
            piece = slices_ref[:, k * LANES : (k + 1) * LANES].astype(jnp.float32)
            total = total + piece * piece
        norm_ref[...] = 0.5 * lax.dot_general(
            jnp.ones((8, LANES), jnp.float32),
            total,
            (((1,), (1,)), ((), ())),
            precision=lax.Precision.HIGHEST,
            preferred_element_type=jnp.float32,
        )
    lane = lax.broadcasted_iota(jnp.int32, (rows, LANES), 1)
    u = jnp.bitwise_and(lane, frame_side - 1) - frame_side // 2
    half = jnp.right_shift(lane, 6)
    c1, s1 = cos_sin(u * off_x + half * off_y)
    c2, s2 = cos_sin(2 * lane * off_y)
    at_end = (lax.axis_index("orient") == 0) | (
        lax.axis_index("orient") == lax.axis_size("orient") - 1
    )

    def pixels(at):
        if choices == 1:
            return images_refs[0][:, at].astype(jnp.float32)
        return jnp.where(at_end, images_refs[0][:, at], images_refs[1][:, at]).astype(jnp.float32)

    for k in range(K // LANES):
        re_at = slice(k * LANES, (k + 1) * LANES)
        im_at = slice(K + k * LANES, K + (k + 1) * LANES)
        x_re, x_im = pixels(re_at), pixels(im_at)
        ck, sk = c2[:, k : k + 1], s2[:, k : k + 1]
        cb = c1 * ck - s1 * sk
        sb = s1 * ck + c1 * sk
        y_re = x_re * cb + x_im * sb
        y_im = x_im * cb - x_re * sb
        where = pl.ds(pl.multiple_of(plane * rows, rows), rows)
        based_ref[where, re_at] = y_re.astype(jnp.bfloat16)
        based_ref[where, im_at] = y_im.astype(jnp.bfloat16)
        re_rows, im_rows = [], []
        for t in range(PAIRS):
            cos_t = cos_ref[t : t + 1, re_at]
            sin_t = sin_ref[t : t + 1, re_at]
            re_rows += [y_re * cos_t, y_im * sin_t]
            im_rows += [y_im * cos_t, -(y_re * sin_t)]
        left_ref[:, re_at] = jnp.concatenate(re_rows, axis=0).astype(jnp.bfloat16)
        left_ref[:, im_at] = jnp.concatenate(im_rows, axis=0).astype(jnp.bfloat16)
    both = lax.dot_general(
        left_ref[...],
        slices_ref[...],
        (((1,), (1,)), ((), ())),
        preferred_element_type=jnp.float32,
    )
    norm = norm_ref[0:1, :]
    scores = []
    for t in range(PAIRS):
        even = both[2 * t * rows : (2 * t + 1) * rows] - norm
        odd = both[(2 * t + 1) * rows : (2 * t + 2) * rows]
        scores += [inv_noise * (even + odd), inv_noise * (even - odd)]
    top = scores[0]
    for s in scores[1:]:
        top = jnp.maximum(top, s)
    top = jnp.max(top, axis=1, keepdims=True)
    mass = jnp.zeros_like(scores[0])
    for i, s in enumerate(scores):
        term = jnp.exp(s - top)
        mass = mass + term
        terms_ref[i, where, :] = term.astype(jnp.bfloat16)
    mass = jnp.sum(mass, axis=1, keepdims=True)
    count = stats_ref.shape[1]
    row = lax.broadcasted_iota(jnp.int32, (rows, count), 0)
    col = lax.broadcasted_iota(jnp.int32, (rows, count), 1)
    mine = col == row + plane * rows
    top_row = jnp.sum(jnp.where(mine, top, 0.0), axis=0, keepdims=True)
    mass_row = jnp.sum(jnp.where(mine, mass, 0.0), axis=0, keepdims=True)
    which = lax.broadcasted_iota(jnp.int32, (8, count), 0)
    part = jnp.where(which == 0, top_row, jnp.where(which == 1, mass_row, 0.0))
    stats_ref[...] = part if first else part + stats_in_ref[...]


def share_kernel(terms_ref, hit_ref, share_ref):
    for t in range(PAIRS):
        plus, minus = (
            lax.dot_general(
                hit_ref[...],
                terms_ref[2 * t + i],
                (((1,), (1,)), ((), ())),
                preferred_element_type=jnp.float32,
            )
            for i in range(2)
        )
        share_ref[2 * t] = plus + minus
        share_ref[2 * t + 1] = plus - minus


def brick_kernel(others, share_ref, based_ref, cos_ref, sin_ref, *rest):
    stats_refs, (out_ref, pairs_ref, sums_ref) = rest[:others], rest[others:]
    bricks = share_ref.shape[1] // NSEG
    count = based_ref.shape[0]
    own_top = stats_refs[0][0:1, :]
    top = own_top
    for ref in stats_refs[1:]:
        top = jnp.maximum(top, ref[0:1, :])
    mass = jnp.zeros_like(top)
    for ref in stats_refs:
        mass = mass + ref[1:2, :] * jnp.exp(ref[0:1, :] - top)
    factor = jnp.exp(own_top - top) / mass
    mass_sum = jnp.zeros((NSEG * bricks, count), jnp.float32)
    for t in range(PAIRS):
        even = share_ref[2 * t] * factor
        odd = share_ref[2 * t + 1] * factor
        mass_sum = mass_sum + even
        for j in range(NSEG):
            at = slice(j * bricks, (j + 1) * bricks)
            pairs_ref[j, t * bricks : (t + 1) * bricks, :] = even[at].astype(jnp.bfloat16)
            pairs_ref[j, (PAIRS + t) * bricks : (PAIRS + t + 1) * bricks, :] = odd[at].astype(
                jnp.bfloat16
            )
    mass_sum = jnp.sum(mass_sum, axis=1, keepdims=True)
    mass_high = mass_sum.astype(jnp.bfloat16).astype(jnp.float32)
    mass_low = mass_sum - mass_high
    lane = lax.broadcasted_iota(jnp.int32, (bricks, LANES), 1)
    for j in range(NSEG):
        at = slice(j * bricks, (j + 1) * bricks)
        re_at = slice(j * SEG, (j + 1) * SEG)
        im_at = slice(K + j * SEG, K + (j + 1) * SEG)
        left = pairs_ref[j]
        with_re = jnp.dot(left, based_ref[:, re_at], preferred_element_type=jnp.float32)
        with_im = jnp.dot(left, based_ref[:, im_at], preferred_element_type=jnp.float32)
        sum_re = jnp.zeros((bricks, SEG), jnp.float32)
        sum_im = jnp.zeros((bricks, SEG), jnp.float32)
        for t in range(PAIRS):
            cos_t = cos_ref[t : t + 1, re_at]
            sin_t = sin_ref[t : t + 1, re_at]
            even = slice(t * bricks, (t + 1) * bricks)
            odd = slice((PAIRS + t) * bricks, (PAIRS + t + 1) * bricks)
            sum_re = sum_re + cos_t * with_re[even] + sin_t * with_im[odd]
            sum_im = sum_im + cos_t * with_im[even] - sin_t * with_re[odd]
        sums_ref[:, j, :SEG] = sum_re
        sums_ref[:, j, SEG : 2 * SEG] = sum_im
        sums_ref[:, j, 2 * SEG :] = jnp.where(
            lane == 0, mass_high[at], jnp.where(lane == 1, mass_low[at], 0.0)
        )
    out_ref[...] = sums_ref[...].astype(jnp.bfloat16)


def final_kernel(arrived_ref, weight_ref, cover_ref, values_ref, mass_ref):
    vox = cover_ref.shape[1]
    total = jnp.sum(arrived_ref[...].astype(jnp.float32), axis=0)
    re, im = total[:, :SEG], total[:, SEG : 2 * SEG]
    seg_mass = total[:, 2 * SEG : 2 * SEG + 1] + total[:, 2 * SEG + 1 : 2 * SEG + 2]
    parts = []
    for _ in range(3):
        high = [x.astype(jnp.bfloat16).astype(jnp.float32) for x in (re, im)]
        parts += high
        re, im = re - high[0], im - high[1]
    left = jnp.concatenate(parts, axis=0).astype(jnp.bfloat16)
    row = lax.broadcasted_iota(jnp.int32, (left.shape[0], 2 * vox), 0) % NSEG
    product = jnp.zeros((left.shape[0], 2 * vox), jnp.float32)
    for j in range(NSEG):
        full = jnp.dot(
            left,
            weight_ref[:, 2 * j * vox : 2 * (j + 1) * vox],
            preferred_element_type=jnp.float32,
        )
        product = jnp.where(row == j, full, product)
    step = 2 * NSEG
    product = product[:step] + product[step : 2 * step] + product[2 * step :]
    for p in range(2):
        line = jnp.sum(product[p * NSEG : (p + 1) * NSEG], axis=0, keepdims=True)
        values_ref[0, p : p + 1, :] = (
            line[:, :vox] * float(1 << interp_bits) + line[:, vox:]
        ) * interp_scale
    mass_ref[0] = jnp.sum(seg_mass * cover_ref[...], axis=0, keepdims=True)


def on_chip(*arrays):
    return [pltpu.with_memory_space_constraint(x, pltpu.VMEM) for x in arrays]


def call(kernel, name, out_shape, inputs, scratch=(), aliases=None, chip_out=True, hbm_in=False):
    spec = pl.BlockSpec(memory_space=pltpu.VMEM)
    in_spec = pl.BlockSpec(memory_space=pltpu.HBM) if hbm_in else spec
    single = not isinstance(out_shape, list)
    shapes = [out_shape] if single else out_shape
    if chip_out:
        shapes = [pltpu.VMEM(x.shape, x.dtype) for x in shapes]
    out = pl.pallas_call(
        kernel,
        in_specs=[in_spec] * len(inputs),
        out_specs=[spec] * len(shapes),
        out_shape=shapes,
        scratch_shapes=list(scratch),
        input_output_aliases=aliases or {},
        compiler_params=pltpu.CompilerParams(vmem_limit_bytes=VMEM_LIMIT),
        name=name,
    )(*inputs)
    return out[0] if single else out


VMEM_LIMIT = 24 * 2**20


def swap(array, amount):
    count = lax.axis_size("orient")
    return lax.ppermute(array, "orient", [(i, i ^ amount) for i in range(count)])


def shift(array, amount):
    count = lax.axis_size("orient")
    return lax.ppermute(array, "orient", [(i, (i + amount) % count) for i in range(count)])


def everyone(array):
    count = lax.axis_size("orient")
    if count != 4:
        return [array] + [shift(array, k) for k in range(1, count)]
    return [array] + [swap(array, k) for k in (3, 2, 1)]


def after(state, images):
    terms, based, stats = state
    stats, images = lax.optimization_barrier((stats, images))
    return [terms, based, stats], images


def per_device(images, offsets, slices, seg_map, interp):
    orient_count = lax.axis_size("orient")
    group_count = lax.axis_size("img") * lax.axis_size("brick")
    bricks = orient_count * group_count
    rows = images.shape[0]
    orient = slices.shape[0]
    count = rows * orient_count
    vox = interp.shape[3]
    f32, bf16 = jnp.float32, jnp.bfloat16
    relay = orient_count == 4
    if relay:
        first = lax.ppermute(images, "orient", [(0, 2), (3, 1), (2, 3), (1, 0)])
    else:
        waiting = [
            ((1, orient_count - k, orient_count), shift(images, k))
            for k in range(1, orient_count)
        ]

    weights, cover, hit, cos_table, sin_table, own, offsets_v = call(
        functools.partial(setup_kernel, bricks),
        "setup",
        [
            jax.ShapeDtypeStruct((SEG, 2 * NSEG * vox), bf16),
            jax.ShapeDtypeStruct((NSEG, vox), f32),
            jax.ShapeDtypeStruct((NSEG * bricks, orient), bf16),
            jax.ShapeDtypeStruct((PAIRS, K), f32),
            jax.ShapeDtypeStruct((PAIRS, K), f32),
            jax.ShapeDtypeStruct(images.shape, bf16),
            jax.ShapeDtypeStruct(offsets.shape[::-1], jnp.int32),
        ],
        [
            pltpu.with_memory_space_constraint(x, pltpu.HBM)
            for x in (interp, seg_map.reshape(-1, LANES), images, offsets.T)
        ],
        scratch=[
            pltpu.VMEM(interp.shape[1:], jnp.int32),
            pltpu.VMEM((seg_map.shape[0] // LANES, LANES), jnp.int32),
            pltpu.SemaphoreType.DMA((NSEG + 3,)),
        ],
        hbm_in=True,
    )
    constant = on_chip(offsets_v, slices, cos_table, sin_table)
    state_shapes = [
        jax.ShapeDtypeStruct((SHIFTS, count, orient), bf16),
        jax.ShapeDtypeStruct((count, 2 * K), bf16),
        jax.ShapeDtypeStruct((8, count), f32),
    ]

    def scored(source, arrays, earlier):
        first = earlier is None
        inputs = on_chip(*arrays) + constant
        if not first:
            inputs += on_chip(*earlier)
        at = len(arrays) + 5
        return call(
            functools.partial(score_kernel, first, source, len(arrays)),
            "scores",
            state_shapes + ([jax.ShapeDtypeStruct((8, orient), f32)] if first else []),
            inputs,
            scratch=[pltpu.VMEM((SHIFTS * rows, 2 * K), bf16)],
            aliases={} if first else {at + i: i for i in range(3)},
        )

    *state, norm = scored((1, 0, orient_count), [own], None)
    if relay:
        state, again = after(state, images)
        second = lax.ppermute(again, "orient", [(0, 1), (3, 2), (1, 3), (2, 0)])
        first, again = lax.optimization_barrier((first, again))
        relayed = lax.ppermute(first, "orient", [(2, 3), (1, 0)])
        middle = lax.ppermute(again, "orient", [(1, 2), (2, 1)])
        state = scored((2, 1, 5), [first], [norm, *state])
        state = scored((3, 2, 5), [second], [norm, *state])
        state = scored((4, 3, 5), [relayed, middle], [norm, *state])
    else:
        for source, array in waiting:
            state = scored(source, [array], [norm, *state])
    terms, based, stats = state
    gathered = everyone(stats)
    shares = call(
        share_kernel,
        "shares",
        jax.ShapeDtypeStruct((SHIFTS, NSEG * bricks, count), f32),
        on_chip(terms, hit),
    )
    outgoing = call(
        functools.partial(brick_kernel, orient_count),
        "bricks",
        jax.ShapeDtypeStruct((bricks, NSEG, 2 * SEG + LANES), bf16),
        on_chip(shares, based, cos_table, sin_table, *gathered),
        scratch=[
            pltpu.VMEM((NSEG, SHIFTS * bricks, count), bf16),
            pltpu.VMEM((bricks, NSEG, 2 * SEG + LANES), f32),
        ],
    )
    received = lax.all_to_all(
        outgoing, ("orient", "img", "brick"), split_axis=0, concat_axis=0, tiled=True
    )
    return call(
        final_kernel,
        "insert",
        [
            jax.ShapeDtypeStruct((1, 2, vox), f32),
            jax.ShapeDtypeStruct((1, 1, vox), f32),
        ],
        on_chip(received, weights, cover),
        chip_out=False,
    )


def solution(mesh):
    placed = (
        P(("groups", "orient", "img", "brick"), None),
        P("groups", None),
        P(("groups", "orient"), None),
        P(),
        P(("orient", "img", "brick"), None, None, None),
    )

    def device(*args):
        values, weight = per_device(*args)
        return values, weight.reshape(1, -1)

    return jax.shard_map(
        device,
        mesh=mesh,
        in_specs=placed,
        out_specs=(
            P(("groups", "orient", "img", "brick"), None, None),
            P(("groups", "orient", "img", "brick"), None),
        ),
        check_vma=False,
    )
```

```python
import functools

import jax
import jax.numpy as jnp
import numpy as np
from jax import lax
from jax.experimental import pallas as pl
from jax.experimental.pallas import tpu as pltpu
from jax.sharding import PartitionSpec as P

SHIFTS = 16
SEG = 256
NSEG = 8
K = SEG * NSEG
LANES = 128

frame_side = 64
interp_bits = 4
interp_scale = 1.0 / 256.0
PAIRS = SHIFTS // 2


def cos_sin(steps):
    centred = jnp.bitwise_and(steps + frame_side, 2 * frame_side - 1) - frame_side
    x = centred.astype(jnp.float32) * (np.pi / frame_side)
    x2 = x * x
    c = jnp.full_like(x, (-1.0) ** 10 / float(np.prod(np.arange(1.0, 21.0))))
    s = jnp.full_like(x, (-1.0) ** 10 / float(np.prod(np.arange(1.0, 22.0))))
    for k in range(9, -1, -1):
        c = c * x2 + (-1.0) ** k / float(np.prod(np.arange(1.0, 2 * k + 1.0)))
        s = s * x2 + (-1.0) ** k / float(np.prod(np.arange(1.0, 2 * k + 2.0)))
    return c, s * x


def setup_kernel(
    bricks,
    interp_hbm,
    map_hbm,
    images_hbm,
    offsets_hbm,
    weight_ref,
    cover_ref,
    hit_ref,
    cos_ref,
    sin_ref,
    images_ref,
    offsets_ref,
    interp_ref,
    map_ref,
    sems,
):
    small = [
        pltpu.make_async_copy(source, target, sems.at[NSEG + i])
        for i, (source, target) in enumerate(
            [(images_hbm, images_ref), (offsets_hbm, offsets_ref), (map_hbm, map_ref)]
        )
    ]
    large = [
        pltpu.make_async_copy(interp_hbm.at[0, j], interp_ref.at[j], sems.at[j])
        for j in range(NSEG)
    ]
    for copy in small + large:
        copy.start()
    coef = lax.broadcasted_iota(jnp.int32, (PAIRS, K), 1)
    pair = lax.broadcasted_iota(jnp.int32, (PAIRS, K), 0)
    u = jnp.bitwise_and(coef, frame_side - 1) - frame_side // 2
    w = coef // frame_side
    dx = 2 * jnp.bitwise_and(pair, 3) - 3
    dy = 2 * (pair // 4) - 3
    cos_ref[...], sin_ref[...] = cos_sin(u * dx + w * dy)
    for copy in small:
        copy.wait()
    vox = interp_ref.shape[2]
    covers = []
    for j in range(NSEG):
        large[j].wait()
        raw = interp_ref[j]
        high = jnp.right_shift(raw, interp_bits).astype(jnp.float32)
        low = jnp.bitwise_and(raw, (1 << interp_bits) - 1).astype(jnp.float32)
        weight_ref[j * SEG : (j + 1) * SEG, :vox] = high.astype(jnp.bfloat16)
        weight_ref[j * SEG : (j + 1) * SEG, vox:] = low.astype(jnp.bfloat16)
        covers.append(jnp.sum(raw.astype(jnp.float32), axis=0, keepdims=True) * interp_scale)
    cover_ref[...] = jnp.concatenate(covers, axis=0)
    orient = hit_ref.shape[1]
    rows = orient * NSEG // LANES
    per_row = LANES // NSEG
    start = pl.multiple_of(lax.axis_index("orient") * rows, rows)
    entries = map_ref[pl.ds(start, rows), :].astype(jnp.float32)
    lane = lax.broadcasted_iota(jnp.int32, (rows, LANES), 1)
    masked = jnp.concatenate(
        [jnp.where(lane % NSEG == j, entries, 0.0) for j in range(NSEG)], axis=0
    )
    source = lax.broadcasted_iota(jnp.int32, (LANES, orient), 0) // NSEG
    target = lax.broadcasted_iota(jnp.int32, (LANES, orient), 1) % per_row
    spread = jnp.dot(
        masked,
        (source == target).astype(jnp.float32),
        precision=lax.Precision.HIGHEST,
        preferred_element_type=jnp.float32,
    )
    row = lax.broadcasted_iota(jnp.int32, (rows, orient), 0)
    own = lax.broadcasted_iota(jnp.int32, (rows, orient), 1) // per_row == row
    brick = lax.broadcasted_iota(jnp.int32, (bricks, orient), 0).astype(jnp.float32)
    hits = []
    for j in range(NSEG):
        named = jnp.where(own, spread[j * rows : (j + 1) * rows], 0.0)
        named = jnp.sum(named, axis=0, keepdims=True)
        hits.append((brick == named).astype(jnp.float32))
    hit_ref[...] = jnp.concatenate(hits, axis=0).astype(jnp.bfloat16)


def source_plane(source):
    factor, offset, modulus = source
    return lax.rem(factor * lax.axis_index("orient") + offset, modulus)


def score_kernel(first, source, choices, *refs):
    images_refs, refs = refs[:choices], refs[choices:]
    offsets_ref, slices_ref, cos_ref, sin_ref = refs[:4]
    if first:
        terms_ref, based_ref, stats_ref, norm_ref, left_ref = refs[4:]
    else:
        norm_ref, _, _, stats_in_ref = refs[4:8]
        terms_ref, based_ref, stats_ref, left_ref = refs[8:]
    inv_noise = 100.0 / K
    rows = images_refs[0].shape[0]
    plane = source_plane(source)
    group = lax.axis_index("img") * lax.axis_size("brick") + lax.axis_index("brick")
    groups = lax.axis_size("img") * lax.axis_size("brick")
    count = offsets_ref.shape[1]
    row = lax.broadcasted_iota(jnp.int32, (rows, count), 0)
    col = lax.broadcasted_iota(jnp.int32, (rows, count), 1)
    mine = col == row + (plane * groups + group) * rows
    off = 2.0 * offsets_ref[...].astype(jnp.float32) - 1.0
    off_x, off_y = (
        jnp.sum(jnp.where(mine, off[i : i + 1, :], 0.0), axis=1, keepdims=True).astype(jnp.int32)
        for i in range(2)
    )
    if first:
        orient = slices_ref.shape[0]
        total = jnp.zeros((orient, LANES), jnp.float32)
        for k in range(2 * K // LANES):
            piece = slices_ref[:, k * LANES : (k + 1) * LANES].astype(jnp.float32)
            total = total + piece * piece
        norm_ref[...] = 0.5 * lax.dot_general(
            jnp.ones((8, LANES), jnp.float32),
            total,
            (((1,), (1,)), ((), ())),
            precision=lax.Precision.HIGHEST,
            preferred_element_type=jnp.float32,
        )
    lane = lax.broadcasted_iota(jnp.int32, (rows, LANES), 1)
    u = jnp.bitwise_and(lane, frame_side - 1) - frame_side // 2
    half = jnp.right_shift(lane, 6)
    c1, s1 = cos_sin(u * off_x + half * off_y)
    c2, s2 = cos_sin(2 * lane * off_y)
    at_end = (lax.axis_index("orient") == 0) | (
        lax.axis_index("orient") == lax.axis_size("orient") - 1
    )

    def pixels(at):
        if choices == 1:
            return images_refs[0][:, at].astype(jnp.float32)
        return jnp.where(at_end, images_refs[0][:, at], images_refs[1][:, at]).astype(jnp.float32)

    for k in range(K // LANES):
        re_at = slice(k * LANES, (k + 1) * LANES)
        im_at = slice(K + k * LANES, K + (k + 1) * LANES)
        x_re, x_im = pixels(re_at), pixels(im_at)
        ck, sk = c2[:, k : k + 1], s2[:, k : k + 1]
        cb = c1 * ck - s1 * sk
        sb = s1 * ck + c1 * sk
        y_re = x_re * cb + x_im * sb
        y_im = x_im * cb - x_re * sb
        where = pl.ds(pl.multiple_of(plane * rows, rows), rows)
        based_ref[where, re_at] = y_re.astype(jnp.bfloat16)
        based_ref[where, im_at] = y_im.astype(jnp.bfloat16)
        re_rows, im_rows = [], []
        for t in range(PAIRS):
            cos_t = cos_ref[t : t + 1, re_at]
            sin_t = sin_ref[t : t + 1, re_at]
            re_rows += [y_re * cos_t, y_im * sin_t]
            im_rows += [y_im * cos_t, -(y_re * sin_t)]
        left_ref[:, re_at] = jnp.concatenate(re_rows, axis=0).astype(jnp.bfloat16)
        left_ref[:, im_at] = jnp.concatenate(im_rows, axis=0).astype(jnp.bfloat16)
    both = lax.dot_general(
        left_ref[...],
        slices_ref[...],
        (((1,), (1,)), ((), ())),
        preferred_element_type=jnp.float32,
    )
    norm = norm_ref[0:1, :]
    scores = []
    for t in range(PAIRS):
        even = both[2 * t * rows : (2 * t + 1) * rows] - norm
        odd = both[(2 * t + 1) * rows : (2 * t + 2) * rows]
        scores += [inv_noise * (even + odd), inv_noise * (even - odd)]
    top = scores[0]
    for s in scores[1:]:
        top = jnp.maximum(top, s)
    top = jnp.max(top, axis=1, keepdims=True)
    mass = jnp.zeros_like(scores[0])
    for i, s in enumerate(scores):
        term = jnp.exp(s - top)
        mass = mass + term
        terms_ref[i, where, :] = term.astype(jnp.bfloat16)
    mass = jnp.sum(mass, axis=1, keepdims=True)
    count = stats_ref.shape[1]
    row = lax.broadcasted_iota(jnp.int32, (rows, count), 0)
    col = lax.broadcasted_iota(jnp.int32, (rows, count), 1)
    mine = col == row + plane * rows
    top_row = jnp.sum(jnp.where(mine, top, 0.0), axis=0, keepdims=True)
    mass_row = jnp.sum(jnp.where(mine, mass, 0.0), axis=0, keepdims=True)
    which = lax.broadcasted_iota(jnp.int32, (8, count), 0)
    part = jnp.where(which == 0, top_row, jnp.where(which == 1, mass_row, 0.0))
    stats_ref[...] = part if first else part + stats_in_ref[...]


def share_kernel(terms_ref, hit_ref, share_ref):
    for t in range(PAIRS):
        plus, minus = (
            lax.dot_general(
                hit_ref[...],
                terms_ref[2 * t + i],
                (((1,), (1,)), ((), ())),
                preferred_element_type=jnp.float32,
            )
            for i in range(2)
        )
        share_ref[2 * t] = plus + minus
        share_ref[2 * t + 1] = plus - minus


def brick_kernel(others, share_ref, based_ref, cos_ref, sin_ref, *rest):
    stats_refs, (out_ref, pairs_ref, sums_ref) = rest[:others], rest[others:]
    bricks = share_ref.shape[1] // NSEG
    count = based_ref.shape[0]
    own_top = stats_refs[0][0:1, :]
    top = own_top
    for ref in stats_refs[1:]:
        top = jnp.maximum(top, ref[0:1, :])
    mass = jnp.zeros_like(top)
    for ref in stats_refs:
        mass = mass + ref[1:2, :] * jnp.exp(ref[0:1, :] - top)
    factor = jnp.exp(own_top - top) / mass
    mass_sum = jnp.zeros((NSEG * bricks, count), jnp.float32)
    for t in range(PAIRS):
        even = share_ref[2 * t] * factor
        odd = share_ref[2 * t + 1] * factor
        mass_sum = mass_sum + even
        for j in range(NSEG):
            at = slice(j * bricks, (j + 1) * bricks)
            pairs_ref[j, t * bricks : (t + 1) * bricks, :] = even[at].astype(jnp.bfloat16)
            pairs_ref[j, (PAIRS + t) * bricks : (PAIRS + t + 1) * bricks, :] = odd[at].astype(
                jnp.bfloat16
            )
    mass_sum = jnp.sum(mass_sum, axis=1, keepdims=True)
    mass_high = mass_sum.astype(jnp.bfloat16).astype(jnp.float32)
    mass_low = mass_sum - mass_high
    lane = lax.broadcasted_iota(jnp.int32, (bricks, LANES), 1)
    high = low = jnp.zeros((bricks, LANES), jnp.float32)
    for j in range(NSEG):
        at = slice(j * bricks, (j + 1) * bricks)
        re_at = slice(j * SEG, (j + 1) * SEG)
        im_at = slice(K + j * SEG, K + (j + 1) * SEG)
        left = pairs_ref[j]
        with_re = jnp.dot(left, based_ref[:, re_at], preferred_element_type=jnp.float32)
        with_im = jnp.dot(left, based_ref[:, im_at], preferred_element_type=jnp.float32)
        sum_re = jnp.zeros((bricks, SEG), jnp.float32)
        sum_im = jnp.zeros((bricks, SEG), jnp.float32)
        for t in range(PAIRS):
            cos_t = cos_ref[t : t + 1, re_at]
            sin_t = sin_ref[t : t + 1, re_at]
            even = slice(t * bricks, (t + 1) * bricks)
            odd = slice((PAIRS + t) * bricks, (PAIRS + t + 1) * bricks)
            sum_re = sum_re + cos_t * with_re[even] + sin_t * with_im[odd]
            sum_im = sum_im + cos_t * with_im[even] - sin_t * with_re[odd]
        sums_ref[:, 0, re_at] = sum_re
        sums_ref[:, 1, re_at] = sum_im
        high = jnp.where(lane == j, mass_high[at], high)
        low = jnp.where(lane == j, mass_low[at], low)
    sums_ref[:, 0, K:] = high
    sums_ref[:, 1, K:] = low
    out_ref[...] = sums_ref[...].astype(jnp.bfloat16)


def final_kernel(arrived_ref, weight_ref, cover_ref, values_ref, mass_ref):
    vox = cover_ref.shape[1]
    total = jnp.sum(arrived_ref[...].astype(jnp.float32), axis=0)
    rest = total[:, :K]
    parts = []
    for _ in range(3):
        high = rest.astype(jnp.bfloat16).astype(jnp.float32)
        parts.append(high)
        rest = rest - high
    left = jnp.concatenate(parts + [jnp.zeros_like(rest)], axis=0).astype(jnp.bfloat16)
    product = jnp.dot(left, weight_ref[...], preferred_element_type=jnp.float32)
    product = product[0:2] + product[2:4] + product[4:6]
    values_ref[0] = (product[:, :vox] * float(1 << interp_bits) + product[:, vox:]) * interp_scale
    seg_mass = total[0:1, K:] + total[1:2, K:]
    weight = jnp.zeros((1, vox), jnp.float32)
    for j in range(NSEG):
        weight = weight + seg_mass[:, j : j + 1] * cover_ref[j : j + 1, :]
    mass_ref[0] = weight


def on_chip(*arrays):
    return [pltpu.with_memory_space_constraint(x, pltpu.VMEM) for x in arrays]


def call(kernel, name, out_shape, inputs, scratch=(), aliases=None, chip_out=True, hbm_in=False):
    spec = pl.BlockSpec(memory_space=pltpu.VMEM)
    in_spec = pl.BlockSpec(memory_space=pltpu.HBM) if hbm_in else spec
    single = not isinstance(out_shape, list)
    shapes = [out_shape] if single else out_shape
    if chip_out:
        shapes = [pltpu.VMEM(x.shape, x.dtype) for x in shapes]
    out = pl.pallas_call(
        kernel,
        in_specs=[in_spec] * len(inputs),
        out_specs=[spec] * len(shapes),
        out_shape=shapes,
        scratch_shapes=list(scratch),
        input_output_aliases=aliases or {},
        compiler_params=pltpu.CompilerParams(vmem_limit_bytes=VMEM_LIMIT),
        name=name,
    )(*inputs)
    return out[0] if single else out


VMEM_LIMIT = 24 * 2**20


def swap(array, amount):
    count = lax.axis_size("orient")
    return lax.ppermute(array, "orient", [(i, i ^ amount) for i in range(count)])


def shift(array, amount):
    count = lax.axis_size("orient")
    return lax.ppermute(array, "orient", [(i, (i + amount) % count) for i in range(count)])


def everyone(array):
    count = lax.axis_size("orient")
    if count != 4:
        return [array] + [shift(array, k) for k in range(1, count)]
    return [array] + [swap(array, k) for k in (1, 2, 3)]


def after(state, images):
    terms, based, stats = state
    stats, images = lax.optimization_barrier((stats, images))
    return [terms, based, stats], images


def per_device(images, offsets, slices, seg_map, interp):
    orient_count = lax.axis_size("orient")
    group_count = lax.axis_size("img") * lax.axis_size("brick")
    bricks = orient_count * group_count
    rows = images.shape[0]
    orient = slices.shape[0]
    count = rows * orient_count
    vox = interp.shape[3]
    f32, bf16 = jnp.float32, jnp.bfloat16
    relay = orient_count == 4
    if relay:
        first = lax.ppermute(images, "orient", [(0, 2), (3, 1), (2, 3), (1, 0)])
    else:
        waiting = [
            ((1, orient_count - k, orient_count), shift(images, k))
            for k in range(1, orient_count)
        ]

    weights, cover, hit, cos_table, sin_table, own, offsets_v = call(
        functools.partial(setup_kernel, bricks),
        "setup",
        [
            jax.ShapeDtypeStruct((K, 2 * vox), bf16),
            jax.ShapeDtypeStruct((NSEG, vox), f32),
            jax.ShapeDtypeStruct((NSEG * bricks, orient), bf16),
            jax.ShapeDtypeStruct((PAIRS, K), f32),
            jax.ShapeDtypeStruct((PAIRS, K), f32),
            jax.ShapeDtypeStruct(images.shape, bf16),
            jax.ShapeDtypeStruct(offsets.shape[::-1], jnp.int32),
        ],
        [
            pltpu.with_memory_space_constraint(x, pltpu.HBM)
            for x in (interp, seg_map.reshape(-1, LANES), images, offsets.T)
        ],
        scratch=[
            pltpu.VMEM(interp.shape[1:], jnp.int32),
            pltpu.VMEM((seg_map.shape[0] // LANES, LANES), jnp.int32),
            pltpu.SemaphoreType.DMA((NSEG + 3,)),
        ],
        hbm_in=True,
    )
    constant = on_chip(offsets_v, slices, cos_table, sin_table)
    state_shapes = [
        jax.ShapeDtypeStruct((SHIFTS, count, orient), bf16),
        jax.ShapeDtypeStruct((count, 2 * K), bf16),
        jax.ShapeDtypeStruct((8, count), f32),
    ]

    def scored(source, arrays, earlier):
        first = earlier is None
        inputs = on_chip(*arrays) + constant
        if not first:
            inputs += on_chip(*earlier)
        at = len(arrays) + 5
        return call(
            functools.partial(score_kernel, first, source, len(arrays)),
            "scores",
            state_shapes + ([jax.ShapeDtypeStruct((8, orient), f32)] if first else []),
            inputs,
            scratch=[pltpu.VMEM((SHIFTS * rows, 2 * K), bf16)],
            aliases={} if first else {at + i: i for i in range(3)},
        )

    *state, norm = scored((1, 0, orient_count), [own], None)
    if relay:
        state, again = after(state, images)
        second = lax.ppermute(again, "orient", [(0, 1), (3, 2), (1, 3), (2, 0)])
        first, again = lax.optimization_barrier((first, again))
        relayed = lax.ppermute(first, "orient", [(2, 3), (1, 0)])
        middle = lax.ppermute(again, "orient", [(1, 2), (2, 1)])
        state = scored((2, 1, 5), [first], [norm, *state])
        state = scored((3, 2, 5), [second], [norm, *state])
        state = scored((4, 3, 5), [relayed, middle], [norm, *state])
    else:
        for source, array in waiting:
            state = scored(source, [array], [norm, *state])
    terms, based, stats = state
    gathered = everyone(stats)
    shares = call(
        share_kernel,
        "shares",
        jax.ShapeDtypeStruct((SHIFTS, NSEG * bricks, count), f32),
        on_chip(terms, hit),
    )
    outgoing = call(
        functools.partial(brick_kernel, orient_count),
        "bricks",
        jax.ShapeDtypeStruct((bricks, 2, K + LANES), bf16),
        on_chip(shares, based, cos_table, sin_table, *gathered),
        scratch=[
            pltpu.VMEM((NSEG, SHIFTS * bricks, count), bf16),
            pltpu.VMEM((bricks, 2, K + LANES), f32),
        ],
    )
    received = lax.all_to_all(
        outgoing, ("orient", "img", "brick"), split_axis=0, concat_axis=0, tiled=True
    )
    return call(
        final_kernel,
        "insert",
        [
            jax.ShapeDtypeStruct((1, 2, vox), f32),
            jax.ShapeDtypeStruct((1, 1, vox), f32),
        ],
        on_chip(received, weights, cover),
        chip_out=False,
    )


def solution(mesh):
    placed = (
        P(("groups", "orient", "img", "brick"), None),
        P("groups", None),
        P(("groups", "orient"), None),
        P(),
        P(("orient", "img", "brick"), None, None, None),
    )

    def device(*args):
        values, weight = per_device(*args)
        return values, weight.reshape(1, -1)

    return jax.shard_map(
        device,
        mesh=mesh,
        in_specs=placed,
        out_specs=(
            P(("groups", "orient", "img", "brick"), None, None),
            P(("groups", "orient", "img", "brick"), None),
        ),
        check_vma=False,
    )
```

```python
import functools

import jax
import jax.numpy as jnp
import numpy as np
from jax import lax
from jax.experimental import pallas as pl
from jax.experimental.pallas import tpu as pltpu
from jax.sharding import PartitionSpec as P

SHIFTS = 16
SEG = 256
NSEG = 8
K = SEG * NSEG
LANES = 128

frame_side = 64
interp_bits = 4
interp_scale = 1.0 / 256.0
PAIRS = SHIFTS // 2


def cos_sin(steps):
    centred = jnp.bitwise_and(steps + frame_side, 2 * frame_side - 1) - frame_side
    x = centred.astype(jnp.float32) * (np.pi / frame_side)
    x2 = x * x
    c = jnp.full_like(x, (-1.0) ** 10 / float(np.prod(np.arange(1.0, 21.0))))
    s = jnp.full_like(x, (-1.0) ** 10 / float(np.prod(np.arange(1.0, 22.0))))
    for k in range(9, -1, -1):
        c = c * x2 + (-1.0) ** k / float(np.prod(np.arange(1.0, 2 * k + 1.0)))
        s = s * x2 + (-1.0) ** k / float(np.prod(np.arange(1.0, 2 * k + 2.0)))
    return c, s * x


def setup_kernel(
    bricks,
    interp_hbm,
    map_hbm,
    images_hbm,
    offsets_hbm,
    weight_ref,
    cover_ref,
    hit_ref,
    cos_ref,
    sin_ref,
    images_ref,
    offsets_ref,
    interp_ref,
    map_ref,
    sems,
):
    small = [
        pltpu.make_async_copy(source, target, sems.at[NSEG + i])
        for i, (source, target) in enumerate(
            [(images_hbm, images_ref), (offsets_hbm, offsets_ref), (map_hbm, map_ref)]
        )
    ]
    large = [
        pltpu.make_async_copy(interp_hbm.at[0, j], interp_ref.at[j], sems.at[j])
        for j in range(NSEG)
    ]
    for copy in small + large:
        copy.start()
    coef = lax.broadcasted_iota(jnp.int32, (PAIRS, K), 1)
    pair = lax.broadcasted_iota(jnp.int32, (PAIRS, K), 0)
    u = jnp.bitwise_and(coef, frame_side - 1) - frame_side // 2
    w = coef // frame_side
    dx = 2 * jnp.bitwise_and(pair, 3) - 3
    dy = 2 * (pair // 4) - 3
    cos_ref[...], sin_ref[...] = cos_sin(u * dx + w * dy)
    for copy in small:
        copy.wait()
    vox = interp_ref.shape[2]
    covers = []
    for j in range(NSEG):
        large[j].wait()
        raw = interp_ref[j]
        high = jnp.right_shift(raw, interp_bits).astype(jnp.float32)
        low = jnp.bitwise_and(raw, (1 << interp_bits) - 1).astype(jnp.float32)
        weight_ref[j * SEG : (j + 1) * SEG, :vox] = high.astype(jnp.bfloat16)
        weight_ref[j * SEG : (j + 1) * SEG, vox:] = low.astype(jnp.bfloat16)
        covers.append(jnp.sum(raw.astype(jnp.float32), axis=0, keepdims=True) * interp_scale)
    cover_ref[...] = jnp.concatenate(covers, axis=0)
    orient = hit_ref.shape[1]
    rows = orient * NSEG // LANES
    per_row = LANES // NSEG
    start = pl.multiple_of(lax.axis_index("orient") * rows, rows)
    entries = map_ref[pl.ds(start, rows), :].astype(jnp.float32)
    lane = lax.broadcasted_iota(jnp.int32, (rows, LANES), 1)
    masked = jnp.concatenate(
        [jnp.where(lane % NSEG == j, entries, 0.0) for j in range(NSEG)], axis=0
    )
    source = lax.broadcasted_iota(jnp.int32, (LANES, orient), 0) // NSEG
    target = lax.broadcasted_iota(jnp.int32, (LANES, orient), 1) % per_row
    spread = jnp.dot(
        masked,
        (source == target).astype(jnp.float32),
        precision=lax.Precision.HIGHEST,
        preferred_element_type=jnp.float32,
    )
    row = lax.broadcasted_iota(jnp.int32, (rows, orient), 0)
    own = lax.broadcasted_iota(jnp.int32, (rows, orient), 1) // per_row == row
    brick = lax.broadcasted_iota(jnp.int32, (bricks, orient), 0).astype(jnp.float32)
    hits = []
    for j in range(NSEG):
        named = jnp.where(own, spread[j * rows : (j + 1) * rows], 0.0)
        named = jnp.sum(named, axis=0, keepdims=True)
        hits.append((brick == named).astype(jnp.float32))
    hit_ref[...] = jnp.concatenate(hits, axis=0).astype(jnp.bfloat16)


def source_plane(source):
    factor, offset, modulus = source
    return lax.rem(factor * lax.axis_index("orient") + offset, modulus)


def score_kernel(first, source, choices, *refs):
    images_refs, refs = refs[:choices], refs[choices:]
    offsets_ref, slices_ref, cos_ref, sin_ref = refs[:4]
    if first:
        terms_ref, based_ref, stats_ref, norm_ref, left_ref = refs[4:]
    else:
        norm_ref, _, _, stats_in_ref = refs[4:8]
        terms_ref, based_ref, stats_ref, left_ref = refs[8:]
    inv_noise = 100.0 / K
    rows = images_refs[0].shape[0]
    plane = source_plane(source)
    group = lax.axis_index("img") * lax.axis_size("brick") + lax.axis_index("brick")
    groups = lax.axis_size("img") * lax.axis_size("brick")
    count = offsets_ref.shape[1]
    row = lax.broadcasted_iota(jnp.int32, (rows, count), 0)
    col = lax.broadcasted_iota(jnp.int32, (rows, count), 1)
    mine = col == row + (plane * groups + group) * rows
    off = 2.0 * offsets_ref[...].astype(jnp.float32) - 1.0
    off_x, off_y = (
        jnp.sum(jnp.where(mine, off[i : i + 1, :], 0.0), axis=1, keepdims=True).astype(jnp.int32)
        for i in range(2)
    )
    if first:
        orient = slices_ref.shape[0]
        total = jnp.zeros((orient, LANES), jnp.float32)
        for k in range(2 * K // LANES):
            piece = slices_ref[:, k * LANES : (k + 1) * LANES].astype(jnp.float32)
            total = total + piece * piece
        norm_ref[...] = 0.5 * lax.dot_general(
            jnp.ones((8, LANES), jnp.float32),
            total,
            (((1,), (1,)), ((), ())),
            precision=lax.Precision.HIGHEST,
            preferred_element_type=jnp.float32,
        )
    lane = lax.broadcasted_iota(jnp.int32, (rows, LANES), 1)
    u = jnp.bitwise_and(lane, frame_side - 1) - frame_side // 2
    half = jnp.right_shift(lane, 6)
    c1, s1 = cos_sin(u * off_x + half * off_y)
    c2, s2 = cos_sin(2 * lane * off_y)
    at_end = (lax.axis_index("orient") == 0) | (
        lax.axis_index("orient") == lax.axis_size("orient") - 1
    )

    def pixels(at):
        if choices == 1:
            return images_refs[0][:, at].astype(jnp.float32)
        return jnp.where(at_end, images_refs[0][:, at], images_refs[1][:, at]).astype(jnp.float32)

    for k in range(K // LANES):
        re_at = slice(k * LANES, (k + 1) * LANES)
        im_at = slice(K + k * LANES, K + (k + 1) * LANES)
        x_re, x_im = pixels(re_at), pixels(im_at)
        ck, sk = c2[:, k : k + 1], s2[:, k : k + 1]
        cb = c1 * ck - s1 * sk
        sb = s1 * ck + c1 * sk
        y_re = x_re * cb + x_im * sb
        y_im = x_im * cb - x_re * sb
        where = pl.ds(pl.multiple_of(plane * rows, rows), rows)
        based_ref[where, re_at] = y_re.astype(jnp.bfloat16)
        based_ref[where, im_at] = y_im.astype(jnp.bfloat16)
        re_rows, im_rows = [], []
        for t in range(PAIRS):
            cos_t = cos_ref[t : t + 1, re_at]
            sin_t = sin_ref[t : t + 1, re_at]
            re_rows += [y_re * cos_t, y_im * sin_t]
            im_rows += [y_im * cos_t, -(y_re * sin_t)]
        left_ref[:, re_at] = jnp.concatenate(re_rows, axis=0).astype(jnp.bfloat16)
        left_ref[:, im_at] = jnp.concatenate(im_rows, axis=0).astype(jnp.bfloat16)
    both = lax.dot_general(
        left_ref[...],
        slices_ref[...],
        (((1,), (1,)), ((), ())),
        preferred_element_type=jnp.float32,
    )
    norm = norm_ref[0:1, :]
    scores = []
    for t in range(PAIRS):
        even = both[2 * t * rows : (2 * t + 1) * rows] - norm
        odd = both[(2 * t + 1) * rows : (2 * t + 2) * rows]
        scores += [inv_noise * (even + odd), inv_noise * (even - odd)]
    top = scores[0]
    for s in scores[1:]:
        top = jnp.maximum(top, s)
    top = jnp.max(top, axis=1, keepdims=True)
    mass = jnp.zeros_like(scores[0])
    for i, s in enumerate(scores):
        term = jnp.exp(s - top)
        mass = mass + term
        terms_ref[i, where, :] = term.astype(jnp.bfloat16)
    mass = jnp.sum(mass, axis=1, keepdims=True)
    count = stats_ref.shape[1]
    row = lax.broadcasted_iota(jnp.int32, (rows, count), 0)
    col = lax.broadcasted_iota(jnp.int32, (rows, count), 1)
    mine = col == row + plane * rows
    top_row = jnp.sum(jnp.where(mine, top, 0.0), axis=0, keepdims=True)
    mass_row = jnp.sum(jnp.where(mine, mass, 0.0), axis=0, keepdims=True)
    which = lax.broadcasted_iota(jnp.int32, (8, count), 0)
    part = jnp.where(which == 0, top_row, jnp.where(which == 1, mass_row, 0.0))
    stats_ref[...] = part if first else part + stats_in_ref[...]


def share_kernel(terms_ref, hit_ref, share_ref):
    for t in range(PAIRS):
        plus, minus = (
            lax.dot_general(
                hit_ref[...],
                terms_ref[2 * t + i],
                (((1,), (1,)), ((), ())),
                preferred_element_type=jnp.float32,
            )
            for i in range(2)
        )
        share_ref[2 * t] = plus + minus
        share_ref[2 * t + 1] = plus - minus


def brick_kernel(others, share_ref, based_ref, cos_ref, sin_ref, *rest):
    stats_refs, (out_ref, pairs_ref, sums_ref) = rest[:others], rest[others:]
    bricks = share_ref.shape[1] // NSEG
    count = based_ref.shape[0]
    own_top = stats_refs[0][0:1, :]
    top = own_top
    for ref in stats_refs[1:]:
        top = jnp.maximum(top, ref[0:1, :])
    mass = jnp.zeros_like(top)
    for ref in stats_refs:
        mass = mass + ref[1:2, :] * jnp.exp(ref[0:1, :] - top)
    factor = jnp.exp(own_top - top) / mass
    mass_sum = jnp.zeros((NSEG * bricks, count), jnp.float32)
    for t in range(PAIRS):
        even = share_ref[2 * t] * factor
        odd = share_ref[2 * t + 1] * factor
        mass_sum = mass_sum + even
        for j in range(NSEG):
            at = slice(j * bricks, (j + 1) * bricks)
            pairs_ref[j, t * bricks : (t + 1) * bricks, :] = even[at].astype(jnp.bfloat16)
            pairs_ref[j, (PAIRS + t) * bricks : (PAIRS + t + 1) * bricks, :] = odd[at].astype(
                jnp.bfloat16
            )
    mass_sum = jnp.sum(mass_sum, axis=1, keepdims=True)
    mass_high = mass_sum.astype(jnp.bfloat16).astype(jnp.float32)
    mass_low = mass_sum - mass_high
    lane = lax.broadcasted_iota(jnp.int32, (bricks, LANES), 1)
    high = low = jnp.zeros((bricks, LANES), jnp.float32)
    for j in range(NSEG):
        at = slice(j * bricks, (j + 1) * bricks)
        re_at = slice(j * SEG, (j + 1) * SEG)
        im_at = slice(K + j * SEG, K + (j + 1) * SEG)
        left = pairs_ref[j]
        with_re = jnp.dot(left, based_ref[:, re_at], preferred_element_type=jnp.float32)
        with_im = jnp.dot(left, based_ref[:, im_at], preferred_element_type=jnp.float32)
        sum_re = jnp.zeros((bricks, SEG), jnp.float32)
        sum_im = jnp.zeros((bricks, SEG), jnp.float32)
        for t in range(PAIRS):
            cos_t = cos_ref[t : t + 1, re_at]
            sin_t = sin_ref[t : t + 1, re_at]
            even = slice(t * bricks, (t + 1) * bricks)
            odd = slice((PAIRS + t) * bricks, (PAIRS + t + 1) * bricks)
            sum_re = sum_re + cos_t * with_re[even] + sin_t * with_im[odd]
            sum_im = sum_im + cos_t * with_im[even] - sin_t * with_re[odd]
        sums_ref[:, 0, re_at] = sum_re
        sums_ref[:, 1, re_at] = sum_im
        high = jnp.where(lane == j, mass_high[at], high)
        low = jnp.where(lane == j, mass_low[at], low)
    sums_ref[:, 0, K:] = high
    sums_ref[:, 1, K:] = low
    out_ref[...] = sums_ref[...].astype(jnp.bfloat16)


def final_kernel(arrived_ref, weight_ref, cover_ref, values_ref, mass_ref):
    vox = cover_ref.shape[1]
    total = jnp.sum(arrived_ref[...].astype(jnp.float32), axis=0)
    rest = total[:, :K]
    parts = []
    for _ in range(3):
        high = rest.astype(jnp.bfloat16).astype(jnp.float32)
        parts.append(high)
        rest = rest - high
    left = jnp.concatenate(parts + [jnp.zeros_like(rest)], axis=0).astype(jnp.bfloat16)
    product = jnp.dot(left, weight_ref[...], preferred_element_type=jnp.float32)
    product = product[0:2] + product[2:4] + product[4:6]
    values_ref[0] = (product[:, :vox] * float(1 << interp_bits) + product[:, vox:]) * interp_scale
    seg_mass = total[0:1, K:] + total[1:2, K:]
    weight = jnp.zeros((1, vox), jnp.float32)
    for j in range(NSEG):
        weight = weight + seg_mass[:, j : j + 1] * cover_ref[j : j + 1, :]
    mass_ref[0] = weight


def on_chip(*arrays):
    return [pltpu.with_memory_space_constraint(x, pltpu.VMEM) for x in arrays]


def call(kernel, name, out_shape, inputs, scratch=(), aliases=None, chip_out=True, hbm_in=False):
    spec = pl.BlockSpec(memory_space=pltpu.VMEM)
    in_spec = pl.BlockSpec(memory_space=pltpu.HBM) if hbm_in else spec
    single = not isinstance(out_shape, list)
    shapes = [out_shape] if single else out_shape
    if chip_out:
        shapes = [pltpu.VMEM(x.shape, x.dtype) for x in shapes]
    out = pl.pallas_call(
        kernel,
        in_specs=[in_spec] * len(inputs),
        out_specs=[spec] * len(shapes),
        out_shape=shapes,
        scratch_shapes=list(scratch),
        input_output_aliases=aliases or {},
        compiler_params=pltpu.CompilerParams(vmem_limit_bytes=VMEM_LIMIT),
        name=name,
    )(*inputs)
    return out[0] if single else out


VMEM_LIMIT = 24 * 2**20


def swap(array, amount):
    count = lax.axis_size("orient")
    return lax.ppermute(array, "orient", [(i, i ^ amount) for i in range(count)])


def shift(array, amount):
    count = lax.axis_size("orient")
    return lax.ppermute(array, "orient", [(i, (i + amount) % count) for i in range(count)])


def everyone(array):
    count = lax.axis_size("orient")
    if count != 4:
        return [array] + [shift(array, k) for k in range(1, count)]
    return [array] + [swap(array, k) for k in (3, 2, 1)]


def after(state, images):
    terms, based, stats = state
    stats, images = lax.optimization_barrier((stats, images))
    return [terms, based, stats], images


def per_device(images, offsets, slices, seg_map, interp):
    orient_count = lax.axis_size("orient")
    group_count = lax.axis_size("img") * lax.axis_size("brick")
    bricks = orient_count * group_count
    rows = images.shape[0]
    orient = slices.shape[0]
    count = rows * orient_count
    vox = interp.shape[3]
    f32, bf16 = jnp.float32, jnp.bfloat16
    relay = orient_count == 4
    if relay:
        first = lax.ppermute(images, "orient", [(0, 2), (3, 1), (2, 3), (1, 0)])
    else:
        waiting = [
            ((1, orient_count - k, orient_count), shift(images, k))
            for k in range(1, orient_count)
        ]

    weights, cover, hit, cos_table, sin_table, own, offsets_v = call(
        functools.partial(setup_kernel, bricks),
        "setup",
        [
            jax.ShapeDtypeStruct((K, 2 * vox), bf16),
            jax.ShapeDtypeStruct((NSEG, vox), f32),
            jax.ShapeDtypeStruct((NSEG * bricks, orient), bf16),
            jax.ShapeDtypeStruct((PAIRS, K), f32),
            jax.ShapeDtypeStruct((PAIRS, K), f32),
            jax.ShapeDtypeStruct(images.shape, bf16),
            jax.ShapeDtypeStruct(offsets.shape[::-1], jnp.int32),
        ],
        [
            pltpu.with_memory_space_constraint(x, pltpu.HBM)
            for x in (interp, seg_map.reshape(-1, LANES), images, offsets.T)
        ],
        scratch=[
            pltpu.VMEM(interp.shape[1:], jnp.int32),
            pltpu.VMEM((seg_map.shape[0] // LANES, LANES), jnp.int32),
            pltpu.SemaphoreType.DMA((NSEG + 3,)),
        ],
        hbm_in=True,
    )
    constant = on_chip(offsets_v, slices, cos_table, sin_table)
    state_shapes = [
        jax.ShapeDtypeStruct((SHIFTS, count, orient), bf16),
        jax.ShapeDtypeStruct((count, 2 * K), bf16),
        jax.ShapeDtypeStruct((8, count), f32),
    ]

    def scored(source, arrays, earlier):
        first = earlier is None
        inputs = on_chip(*arrays) + constant
        if not first:
            inputs += on_chip(*earlier)
        at = len(arrays) + 5
        return call(
            functools.partial(score_kernel, first, source, len(arrays)),
            "scores",
            state_shapes + ([jax.ShapeDtypeStruct((8, orient), f32)] if first else []),
            inputs,
            scratch=[pltpu.VMEM((SHIFTS * rows, 2 * K), bf16)],
            aliases={} if first else {at + i: i for i in range(3)},
        )

    *state, norm = scored((1, 0, orient_count), [own], None)
    if relay:
        state, again = after(state, images)
        second = lax.ppermute(again, "orient", [(0, 1), (3, 2), (1, 3), (2, 0)])
        first, again = lax.optimization_barrier((first, again))
        relayed = lax.ppermute(first, "orient", [(2, 3), (1, 0)])
        middle = lax.ppermute(again, "orient", [(1, 2), (2, 1)])
        state = scored((2, 1, 5), [first], [norm, *state])
        state = scored((3, 2, 5), [second], [norm, *state])
        state = scored((4, 3, 5), [relayed, middle], [norm, *state])
    else:
        for source, array in waiting:
            state = scored(source, [array], [norm, *state])
    terms, based, stats = state
    gathered = everyone(stats)
    shares = call(
        share_kernel,
        "shares",
        jax.ShapeDtypeStruct((SHIFTS, NSEG * bricks, count), f32),
        on_chip(terms, hit),
    )
    outgoing = call(
        functools.partial(brick_kernel, orient_count),
        "bricks",
        jax.ShapeDtypeStruct((bricks, 2, K + LANES), bf16),
        on_chip(shares, based, cos_table, sin_table, *gathered),
        scratch=[
            pltpu.VMEM((NSEG, SHIFTS * bricks, count), bf16),
            pltpu.VMEM((bricks, 2, K + LANES), f32),
        ],
    )
    received = lax.all_to_all(
        outgoing, ("orient", "img", "brick"), split_axis=0, concat_axis=0, tiled=True
    )
    return call(
        final_kernel,
        "insert",
        [
            jax.ShapeDtypeStruct((1, 2, vox), f32),
            jax.ShapeDtypeStruct((1, 1, vox), f32),
        ],
        on_chip(received, weights, cover),
        chip_out=False,
    )


def solution(mesh):
    placed = (
        P(("groups", "orient", "img", "brick"), None),
        P("groups", None),
        P(("groups", "orient"), None),
        P(),
        P(("orient", "img", "brick"), None, None, None),
    )

    def device(*args):
        values, weight = per_device(*args)
        return values, weight.reshape(1, -1)

    return jax.shard_map(
        device,
        mesh=mesh,
        in_specs=placed,
        out_specs=(
            P(("groups", "orient", "img", "brick"), None, None),
            P(("groups", "orient", "img", "brick"), None),
        ),
        check_vma=False,
    )
```

```python
import functools

import jax
import jax.numpy as jnp
import numpy as np
from jax import lax
from jax.experimental import pallas as pl
from jax.experimental.pallas import tpu as pltpu
from jax.sharding import PartitionSpec as P


SHIFTS = 16
SEG = 256
NSEG = 8
K = SEG * NSEG
LANES = 128

frame_side = 64
interp_bits = 4
interp_scale = 1.0 / 256.0
PAIRS = SHIFTS // 2


def cos_sin(steps):
    centred = jnp.bitwise_and(steps + frame_side, 2 * frame_side - 1) - frame_side
    x = centred.astype(jnp.float32) * (np.pi / frame_side)
    x2 = x * x
    c = jnp.full_like(x, (-1.0) ** 10 / float(np.prod(np.arange(1.0, 21.0))))
    s = jnp.full_like(x, (-1.0) ** 10 / float(np.prod(np.arange(1.0, 22.0))))
    for k in range(9, -1, -1):
        c = c * x2 + (-1.0) ** k / float(np.prod(np.arange(1.0, 2 * k + 1.0)))
        s = s * x2 + (-1.0) ** k / float(np.prod(np.arange(1.0, 2 * k + 2.0)))
    return c, s * x


def phase_kernel(
    images_hbm,
    offsets_hbm,
    slices_hbm,
    cos_ref,
    sin_ref,
    images_ref,
    phase_cos_ref,
    phase_sin_ref,
    norm_ref,
    slices_ref,
    offsets_ref,
    sems,
):
    tiles, orient = slices_ref.shape[:2]
    copies = [
        pltpu.make_async_copy(offsets_hbm, offsets_ref, sems.at[tiles]),
        pltpu.make_async_copy(images_hbm, images_ref, sems.at[tiles + 1]),
    ]
    packed = [
        pltpu.make_async_copy(
            slices_hbm.at[:, k * LANES : (k + 1) * LANES], slices_ref.at[k], sems.at[k]
        )
        for k in range(tiles)
    ]
    for copy in copies + packed:
        copy.start()
    coef = lax.broadcasted_iota(jnp.int32, (PAIRS, K), 1)
    pair = lax.broadcasted_iota(jnp.int32, (PAIRS, K), 0)
    u = jnp.bitwise_and(coef, frame_side - 1) - frame_side // 2
    w = coef // frame_side
    dx = 2 * jnp.bitwise_and(pair, 3) - 3
    dy = 2 * (pair // 4) - 3
    cos_ref[...], sin_ref[...] = cos_sin(u * dx + w * dy)
    for copy in copies:
        copy.wait()
    base_phases(images_ref.shape[0], offsets_ref, phase_cos_ref, phase_sin_ref)
    total = jnp.zeros((orient, LANES), jnp.float32)
    for k in range(tiles):
        packed[k].wait()
        piece = slices_ref[k].astype(jnp.float32)
        total = total + piece * piece
    norm_ref[...] = 0.5 * lax.dot_general(
        jnp.ones((8, LANES), jnp.float32),
        total,
        (((1,), (1,)), ((), ())),
        precision=lax.Precision.HIGHEST,
        preferred_element_type=jnp.float32,
    )


def weight_kernel(
    bricks, interp_hbm, map_hbm, weight_ref, cover_ref, hit_ref, interp_ref, map_ref, sems
):
    small = pltpu.make_async_copy(map_hbm, map_ref, sems.at[NSEG])
    large = [
        pltpu.make_async_copy(interp_hbm.at[0, j], interp_ref.at[j], sems.at[j])
        for j in range(NSEG)
    ]
    for copy in [small] + large:
        copy.start()
    small.wait()
    vox = interp_ref.shape[2]
    covers = []
    for j in range(NSEG):
        large[j].wait()
        raw = interp_ref[j]
        high = jnp.right_shift(raw, interp_bits).astype(jnp.float32)
        low = jnp.bitwise_and(raw, (1 << interp_bits) - 1).astype(jnp.float32)
        weight_ref[j * SEG : (j + 1) * SEG, :vox] = high.astype(jnp.bfloat16)
        weight_ref[j * SEG : (j + 1) * SEG, vox:] = low.astype(jnp.bfloat16)
        covers.append(jnp.sum(raw.astype(jnp.float32), axis=0, keepdims=True) * interp_scale)
    cover_ref[...] = jnp.concatenate(covers, axis=0)
    orient = hit_ref.shape[1]
    rows = orient * NSEG // LANES
    per_row = LANES // NSEG
    start = pl.multiple_of(lax.axis_index("orient") * rows, rows)
    entries = map_ref[pl.ds(start, rows), :].astype(jnp.float32)
    lane = lax.broadcasted_iota(jnp.int32, (rows, LANES), 1)
    masked = jnp.concatenate(
        [jnp.where(lane % NSEG == j, entries, 0.0) for j in range(NSEG)], axis=0
    )
    source = lax.broadcasted_iota(jnp.int32, (LANES, orient), 0) // NSEG
    target = lax.broadcasted_iota(jnp.int32, (LANES, orient), 1) % per_row
    spread = jnp.dot(
        masked,
        (source == target).astype(jnp.float32),
        precision=lax.Precision.HIGHEST,
        preferred_element_type=jnp.float32,
    )
    row = lax.broadcasted_iota(jnp.int32, (rows, orient), 0)
    own = lax.broadcasted_iota(jnp.int32, (rows, orient), 1) // per_row == row
    brick = lax.broadcasted_iota(jnp.int32, (bricks, orient), 0).astype(jnp.float32)
    hits = []
    for j in range(NSEG):
        named = jnp.where(own, spread[j * rows : (j + 1) * rows], 0.0)
        named = jnp.sum(named, axis=0, keepdims=True)
        hits.append((brick == named).astype(jnp.float32))
    hit_ref[...] = jnp.concatenate(hits, axis=0).astype(jnp.bfloat16)


def base_phases(rows, offsets_ref, phase_cos_ref, phase_sin_ref):
    group = lax.axis_index("img") * lax.axis_size("brick") + lax.axis_index("brick")
    groups = lax.axis_size("img") * lax.axis_size("brick")
    images = offsets_ref.shape[1]
    off = 2.0 * offsets_ref[...].astype(jnp.float32) - 1.0
    step = max(rows, 8)
    for start in range(0, phase_cos_ref.shape[0], step):
        at = slice(start, start + step)
        row = start + lax.broadcasted_iota(jnp.int32, (step, images), 0)
        col = lax.broadcasted_iota(jnp.int32, (step, images), 1)
        mine = col == (row // rows * groups + group) * rows + row % rows
        off_x, off_y = (
            jnp.sum(jnp.where(mine, off[i : i + 1, :], 0.0), axis=1, keepdims=True).astype(
                jnp.int32
            )
            for i in range(2)
        )
        lane = lax.broadcasted_iota(jnp.int32, (step, LANES), 1)
        u = jnp.bitwise_and(lane, frame_side - 1) - frame_side // 2
        half = jnp.right_shift(lane, 6)
        c1, s1 = cos_sin(u * off_x + half * off_y)
        c2, s2 = cos_sin(2 * lane * off_y)
        for k in range(K // LANES):
            ck, sk = c2[:, k : k + 1], s2[:, k : k + 1]
            phase_cos_ref[at, k * LANES : (k + 1) * LANES] = c1 * ck - s1 * sk
            phase_sin_ref[at, k * LANES : (k + 1) * LANES] = s1 * ck + c1 * sk


def source_plane(source):
    factor, offset, modulus = source
    return lax.rem(factor * lax.axis_index("orient") + offset, modulus)


def score_kernel(first, source, choices, *refs):
    images_refs, refs = refs[:choices], refs[choices:]
    phase_cos_ref, phase_sin_ref, cos_ref, sin_ref = refs[:4]
    norm_ref, slices_ref = refs[4:6]
    stats_in_ref = None if first else refs[8]
    terms_ref, based_ref, stats_ref, left_ref = refs[6 if first else 9 :]
    inv_noise = 100.0 / K
    rows = images_refs[0].shape[0]
    plane = source_plane(source)
    tiles = 2 * K // LANES
    at_end = (lax.axis_index("orient") == 0) | (
        lax.axis_index("orient") == lax.axis_size("orient") - 1
    )

    def pixels(at):
        if choices == 1:
            return images_refs[0][:, at].astype(jnp.float32)
        return jnp.where(at_end, images_refs[0][:, at], images_refs[1][:, at]).astype(jnp.float32)

    where = pl.ds(pl.multiple_of(plane * rows, rows), rows)
    for k in range(tiles // 2):
        re_at = slice(k * LANES, (k + 1) * LANES)
        im_at = slice(K + k * LANES, K + (k + 1) * LANES)
        x_re, x_im = pixels(re_at), pixels(im_at)
        cb, sb = phase_cos_ref[where, re_at], phase_sin_ref[where, re_at]
        y_re = x_re * cb + x_im * sb
        y_im = x_im * cb - x_re * sb
        based_ref[where, re_at] = y_re.astype(jnp.bfloat16)
        based_ref[where, im_at] = y_im.astype(jnp.bfloat16)
        minus_re = -y_re
        re_rows, im_rows = [], []
        for t in range(PAIRS):
            cos_t = cos_ref[t : t + 1, re_at]
            sin_t = sin_ref[t : t + 1, re_at]
            re_rows += [y_re * cos_t, y_im * sin_t]
            im_rows += [y_im * cos_t, minus_re * sin_t]
        left_ref[k] = jnp.concatenate(re_rows, axis=0).astype(jnp.bfloat16)
        left_ref[tiles // 2 + k] = jnp.concatenate(im_rows, axis=0).astype(jnp.bfloat16)
    both = lax.dot_general(
        jnp.concatenate([left_ref[k] for k in range(tiles)], axis=1),
        jnp.concatenate([slices_ref[k] for k in range(tiles)], axis=1),
        (((1,), (1,)), ((), ())),
        preferred_element_type=jnp.float32,
    )
    norm = norm_ref[0:1, :]
    scores = []
    for t in range(PAIRS):
        even = both[2 * t * rows : (2 * t + 1) * rows] - norm
        odd = both[(2 * t + 1) * rows : (2 * t + 2) * rows]
        scores += [inv_noise * (even + odd), inv_noise * (even - odd)]
    top = scores[0]
    for s in scores[1:]:
        top = jnp.maximum(top, s)
    top = jnp.max(top, axis=1, keepdims=True)
    mass = jnp.zeros_like(scores[0])
    for i, s in enumerate(scores):
        term = jnp.exp(s - top)
        mass = mass + term
        terms_ref[i, where, :] = term.astype(jnp.bfloat16)
    mass = jnp.sum(mass, axis=1, keepdims=True)
    count = stats_ref.shape[1]
    row = lax.broadcasted_iota(jnp.int32, (rows, count), 0)
    col = lax.broadcasted_iota(jnp.int32, (rows, count), 1)
    mine = col == row + plane * rows
    top_row = jnp.sum(jnp.where(mine, top, 0.0), axis=0, keepdims=True)
    mass_row = jnp.sum(jnp.where(mine, mass, 0.0), axis=0, keepdims=True)
    which = lax.broadcasted_iota(jnp.int32, (8, count), 0)
    part = jnp.where(which == 0, top_row, jnp.where(which == 1, mass_row, 0.0))
    stats_ref[...] = part if first else part + stats_in_ref[...]


def share_kernel(terms_ref, hit_ref, share_ref):
    for t in range(PAIRS):
        plus, minus = (
            lax.dot_general(
                hit_ref[...],
                terms_ref[2 * t + i],
                (((1,), (1,)), ((), ())),
                preferred_element_type=jnp.float32,
            )
            for i in range(2)
        )
        share_ref[2 * t] = plus + minus
        share_ref[2 * t + 1] = plus - minus


def brick_kernel(others, share_ref, based_ref, cos_ref, sin_ref, *rest):
    stats_refs, (out_ref, pairs_ref, sums_ref) = rest[:others], rest[others:]
    bricks = share_ref.shape[1] // NSEG
    count = based_ref.shape[0]
    own_top = stats_refs[0][0:1, :]
    top = own_top
    for ref in stats_refs[1:]:
        top = jnp.maximum(top, ref[0:1, :])
    mass = jnp.zeros_like(top)
    for ref in stats_refs:
        mass = mass + ref[1:2, :] * jnp.exp(ref[0:1, :] - top)
    factor = jnp.exp(own_top - top) / mass
    mass_sum = jnp.zeros((NSEG * bricks, count), jnp.float32)
    for t in range(PAIRS):
        even = share_ref[2 * t] * factor
        odd = share_ref[2 * t + 1] * factor
        mass_sum = mass_sum + even
        for j in range(NSEG):
            at = slice(j * bricks, (j + 1) * bricks)
            pairs_ref[j, t * bricks : (t + 1) * bricks, :] = even[at].astype(jnp.bfloat16)
            pairs_ref[j, (PAIRS + t) * bricks : (PAIRS + t + 1) * bricks, :] = odd[at].astype(
                jnp.bfloat16
            )
    mass_sum = jnp.sum(mass_sum, axis=1, keepdims=True)
    mass_high = mass_sum.astype(jnp.bfloat16).astype(jnp.float32)
    mass_low = mass_sum - mass_high
    lane = lax.broadcasted_iota(jnp.int32, (bricks, LANES), 1)
    high = low = jnp.zeros((bricks, LANES), jnp.float32)
    for j in range(NSEG):
        at = slice(j * bricks, (j + 1) * bricks)
        re_at = slice(j * SEG, (j + 1) * SEG)
        im_at = slice(K + j * SEG, K + (j + 1) * SEG)
        left = pairs_ref[j]
        with_re = jnp.dot(left, based_ref[:, re_at], preferred_element_type=jnp.float32)
        with_im = jnp.dot(left, based_ref[:, im_at], preferred_element_type=jnp.float32)
        sum_re = jnp.zeros((bricks, SEG), jnp.float32)
        sum_im = jnp.zeros((bricks, SEG), jnp.float32)
        for t in range(PAIRS):
            cos_t = cos_ref[t : t + 1, re_at]
            sin_t = sin_ref[t : t + 1, re_at]
            even = slice(t * bricks, (t + 1) * bricks)
            odd = slice((PAIRS + t) * bricks, (PAIRS + t + 1) * bricks)
            sum_re = sum_re + cos_t * with_re[even] + sin_t * with_im[odd]
            sum_im = sum_im + cos_t * with_im[even] - sin_t * with_re[odd]
        sums_ref[:, 0, re_at] = sum_re
        sums_ref[:, 1, re_at] = sum_im
        high = jnp.where(lane == j, mass_high[at], high)
        low = jnp.where(lane == j, mass_low[at], low)
    sums_ref[:, 0, K:] = high
    sums_ref[:, 1, K:] = low
    out_ref[...] = sums_ref[...].astype(jnp.bfloat16)


def final_kernel(arrived_ref, weight_ref, cover_ref, values_ref, mass_ref):
    vox = cover_ref.shape[1]
    total = jnp.sum(arrived_ref[...].astype(jnp.float32), axis=0)
    rest = total[:, :K]
    parts = []
    for _ in range(3):
        high = rest.astype(jnp.bfloat16).astype(jnp.float32)
        parts.append(high)
        rest = rest - high
    left = jnp.concatenate(parts + [jnp.zeros_like(rest)], axis=0).astype(jnp.bfloat16)
    product = jnp.dot(left, weight_ref[...], preferred_element_type=jnp.float32)
    product = product[0:2] + product[2:4] + product[4:6]
    values_ref[0] = (product[:, :vox] * float(1 << interp_bits) + product[:, vox:]) * interp_scale
    seg_mass = total[0:1, K:] + total[1:2, K:]
    weight = jnp.zeros((1, vox), jnp.float32)
    for j in range(NSEG):
        weight = weight + seg_mass[:, j : j + 1] * cover_ref[j : j + 1, :]
    mass_ref[0] = weight


def on_chip(*arrays):
    return [pltpu.with_memory_space_constraint(x, pltpu.VMEM) for x in arrays]


def off_chip(*arrays):
    return [pltpu.with_memory_space_constraint(x, pltpu.HBM) for x in arrays]


def call(kernel, out_shape, inputs, scratch=(), aliases=None, chip_out=True, hbm_in=False):
    spec = pl.BlockSpec(memory_space=pltpu.VMEM)
    in_spec = pl.BlockSpec(memory_space=pltpu.HBM) if hbm_in else spec
    single = not isinstance(out_shape, list)
    shapes = [out_shape] if single else out_shape
    if chip_out:
        shapes = [pltpu.VMEM(x.shape, x.dtype) for x in shapes]
    out = pl.pallas_call(
        kernel,
        in_specs=[in_spec] * len(inputs),
        out_specs=[spec] * len(shapes),
        out_shape=shapes,
        scratch_shapes=list(scratch),
        input_output_aliases=aliases or {},
        compiler_params=pltpu.CompilerParams(vmem_limit_bytes=VMEM_LIMIT),
    )(*inputs)
    return out[0] if single else out


VMEM_LIMIT = 24 * 2**20


def swap(array, amount):
    count = lax.axis_size("orient")
    return lax.ppermute(array, "orient", [(i, i ^ amount) for i in range(count)])


def shift(array, amount):
    count = lax.axis_size("orient")
    return lax.ppermute(array, "orient", [(i, (i + amount) % count) for i in range(count)])


def everyone(array):
    count = lax.axis_size("orient")
    if count != 4:
        return [array] + [shift(array, k) for k in range(1, count)]
    moved = [array]
    for k in (3, 2, 1):
        moved.append(swap(array, k))
    return moved


def after(state, images):
    terms, based, stats = state
    stats, images = lax.optimization_barrier((stats, images))
    return [terms, based, stats], images


def per_device(images, offsets, slices, seg_map, interp):
    orient_count = lax.axis_size("orient")
    group_count = lax.axis_size("img") * lax.axis_size("brick")
    bricks = orient_count * group_count
    rows = images.shape[0]
    orient = slices.shape[0]
    count = rows * orient_count
    vox = interp.shape[3]
    f32, bf16 = jnp.float32, jnp.bfloat16
    tiles = 2 * K // LANES
    relay = orient_count == 4
    if relay:
        first = lax.ppermute(images, "orient", [(0, 2), (3, 1), (2, 3), (1, 0)])
    else:
        waiting = [
            ((1, orient_count - k, orient_count), shift(images, k))
            for k in range(1, orient_count)
        ]

    cos_table, sin_table, own, phase_cos, phase_sin, norm, packed = call(
        phase_kernel,
        [
            jax.ShapeDtypeStruct((PAIRS, K), f32),
            jax.ShapeDtypeStruct((PAIRS, K), f32),
            jax.ShapeDtypeStruct(images.shape, bf16),
            jax.ShapeDtypeStruct((count, K), f32),
            jax.ShapeDtypeStruct((count, K), f32),
            jax.ShapeDtypeStruct((8, orient), f32),
            jax.ShapeDtypeStruct((tiles, orient, LANES), bf16),
        ],
        off_chip(images, offsets.T, slices),
        scratch=[
            pltpu.VMEM(offsets.shape[::-1], jnp.int32),
            pltpu.SemaphoreType.DMA((tiles + 2,)),
        ],
        hbm_in=True,
    )
    constant = on_chip(phase_cos, phase_sin, cos_table, sin_table, norm, packed)
    state_shapes = [
        jax.ShapeDtypeStruct((SHIFTS, count, orient), bf16),
        jax.ShapeDtypeStruct((count, 2 * K), bf16),
        jax.ShapeDtypeStruct((8, count), f32),
    ]

    def scored(source, arrays, earlier):
        first = earlier is None
        inputs = on_chip(*arrays) + constant
        if not first:
            inputs += on_chip(*earlier)
        at = len(arrays) + 6
        return call(
            functools.partial(score_kernel, first, source, len(arrays)),
            state_shapes,
            inputs,
            scratch=[pltpu.VMEM((tiles, SHIFTS * rows, LANES), bf16)],
            aliases={} if first else {at + i: i for i in range(3)},
        )

    if relay:
        own, again = lax.optimization_barrier((own, images))
        second = lax.ppermute(again, "orient", [(0, 1), (3, 2), (1, 3), (2, 0)])
    state = scored((1, 0, orient_count), [own], None)
    state, raw = after(state, interp)
    weights, cover, hit = call(
        functools.partial(weight_kernel, bricks),
        [
            jax.ShapeDtypeStruct((K, 2 * vox), bf16),
            jax.ShapeDtypeStruct((NSEG, vox), f32),
            jax.ShapeDtypeStruct((NSEG * bricks, orient), bf16),
        ],
        off_chip(raw, seg_map.reshape(-1, LANES)),
        scratch=[
            pltpu.VMEM(interp.shape[1:], jnp.int32),
            pltpu.VMEM((seg_map.shape[0] // LANES, LANES), jnp.int32),
            pltpu.SemaphoreType.DMA((NSEG + 1,)),
        ],
        hbm_in=True,
    )
    if relay:
        state, first = after(state, first)
        first, again = lax.optimization_barrier((first, images))
        relayed = lax.ppermute(first, "orient", [(2, 3), (1, 0)])
        middle = lax.ppermute(again, "orient", [(1, 2), (2, 1), (0, 0), (3, 3)])
        first, cover = lax.optimization_barrier((first, cover))
        state = scored((2, 1, 5), [first], state)
        state = scored((3, 2, 5), [second], state)
        state = scored((4, 3, 5), [relayed, middle], state)
    else:
        for source, array in waiting:
            state = scored(source, [array], state)
    terms, based, stats = state
    gathered = everyone(stats)
    shares = call(
        share_kernel,
        jax.ShapeDtypeStruct((SHIFTS, NSEG * bricks, count), f32),
        on_chip(terms, hit),
    )
    outgoing = call(
        functools.partial(brick_kernel, orient_count),
        jax.ShapeDtypeStruct((bricks, 2, K + LANES), bf16),
        on_chip(shares, based, cos_table, sin_table, *gathered),
        scratch=[
            pltpu.VMEM((NSEG, SHIFTS * bricks, count), bf16),
            pltpu.VMEM((bricks, 2, K + LANES), f32),
        ],
    )
    received = lax.all_to_all(
        outgoing, ("orient", "img", "brick"), split_axis=0, concat_axis=0, tiled=True
    )
    return call(
        final_kernel,
        [
            jax.ShapeDtypeStruct((1, 2, vox), f32),
            jax.ShapeDtypeStruct((1, 1, vox), f32),
        ],
        on_chip(received, weights, cover),
        chip_out=False,
    )


def solution(mesh):
    placed = (
        P(("groups", "orient", "img", "brick"), None),
        P("groups", None),
        P(("groups", "orient"), None),
        P(),
        P(("orient", "img", "brick"), None, None, None),
    )

    def device(*args):
        values, weight = per_device(*args)
        return values, weight.reshape(1, -1)

    return jax.shard_map(
        device,
        mesh=mesh,
        in_specs=placed,
        out_specs=(
            P(("groups", "orient", "img", "brick"), None, None),
            P(("groups", "orient", "img", "brick"), None),
        ),
        check_vma=False,
    )
```

```python
import functools

import jax
import jax.numpy as jnp
import numpy as np
from jax import lax
from jax.experimental import pallas as pl
from jax.experimental.pallas import tpu as pltpu
from jax.sharding import PartitionSpec as P


SHIFTS = 16
SEG = 256
NSEG = 8
K = SEG * NSEG
LANES = 128

frame_side = 64
interp_bits = 4
interp_scale = 1.0 / 256.0
PAIRS = SHIFTS // 2


def cos_sin(steps):
    centred = jnp.bitwise_and(steps + frame_side, 2 * frame_side - 1) - frame_side
    x = centred.astype(jnp.float32) * (np.pi / frame_side)
    x2 = x * x
    c = jnp.full_like(x, (-1.0) ** 10 / float(np.prod(np.arange(1.0, 21.0))))
    s = jnp.full_like(x, (-1.0) ** 10 / float(np.prod(np.arange(1.0, 22.0))))
    for k in range(9, -1, -1):
        c = c * x2 + (-1.0) ** k / float(np.prod(np.arange(1.0, 2 * k + 1.0)))
        s = s * x2 + (-1.0) ** k / float(np.prod(np.arange(1.0, 2 * k + 2.0)))
    return c, s * x


def phase_kernel(
    images_hbm,
    offsets_hbm,
    slices_hbm,
    cos_ref,
    sin_ref,
    images_ref,
    phase_cos_ref,
    phase_sin_ref,
    norm_ref,
    slices_ref,
    offsets_ref,
    sems,
):
    tiles, orient = slices_ref.shape[:2]
    copies = [
        pltpu.make_async_copy(offsets_hbm, offsets_ref, sems.at[tiles]),
        pltpu.make_async_copy(images_hbm, images_ref, sems.at[tiles + 1]),
    ]
    packed = [
        pltpu.make_async_copy(
            slices_hbm.at[:, k * LANES : (k + 1) * LANES], slices_ref.at[k], sems.at[k]
        )
        for k in range(tiles)
    ]
    for copy in copies + packed:
        copy.start()
    coef = lax.broadcasted_iota(jnp.int32, (PAIRS, K), 1)
    pair = lax.broadcasted_iota(jnp.int32, (PAIRS, K), 0)
    u = jnp.bitwise_and(coef, frame_side - 1) - frame_side // 2
    w = coef // frame_side
    dx = 2 * jnp.bitwise_and(pair, 3) - 3
    dy = 2 * (pair // 4) - 3
    cos_ref[...], sin_ref[...] = cos_sin(u * dx + w * dy)
    for copy in copies:
        copy.wait()
    base_phases(images_ref.shape[0], offsets_ref, phase_cos_ref, phase_sin_ref)
    total = jnp.zeros((orient, LANES), jnp.float32)
    for k in range(tiles):
        packed[k].wait()
        piece = slices_ref[k].astype(jnp.float32)
        total = total + piece * piece
    norm_ref[...] = 0.5 * lax.dot_general(
        jnp.ones((8, LANES), jnp.float32),
        total,
        (((1,), (1,)), ((), ())),
        precision=lax.Precision.HIGHEST,
        preferred_element_type=jnp.float32,
    )


def weight_kernel(
    bricks, interp_hbm, map_hbm, weight_ref, cover_ref, hit_ref, interp_ref, map_ref, sems
):
    small = pltpu.make_async_copy(map_hbm, map_ref, sems.at[NSEG])
    large = [
        pltpu.make_async_copy(interp_hbm.at[0, j], interp_ref.at[j], sems.at[j])
        for j in range(NSEG)
    ]
    for copy in [small] + large:
        copy.start()
    small.wait()
    vox = interp_ref.shape[2]
    covers = []
    for j in range(NSEG):
        large[j].wait()
        raw = interp_ref[j]
        high = jnp.right_shift(raw, interp_bits).astype(jnp.float32)
        low = jnp.bitwise_and(raw, (1 << interp_bits) - 1).astype(jnp.float32)
        weight_ref[j * SEG : (j + 1) * SEG, :vox] = high.astype(jnp.bfloat16)
        weight_ref[j * SEG : (j + 1) * SEG, vox:] = low.astype(jnp.bfloat16)
        covers.append(jnp.sum(raw.astype(jnp.float32), axis=0, keepdims=True) * interp_scale)
    cover_ref[...] = jnp.concatenate(covers, axis=0)
    orient = hit_ref.shape[1]
    rows = orient * NSEG // LANES
    per_row = LANES // NSEG
    start = pl.multiple_of(lax.axis_index("orient") * rows, rows)
    entries = map_ref[pl.ds(start, rows), :].astype(jnp.float32)
    lane = lax.broadcasted_iota(jnp.int32, (rows, LANES), 1)
    masked = jnp.concatenate(
        [jnp.where(lane % NSEG == j, entries, 0.0) for j in range(NSEG)], axis=0
    )
    source = lax.broadcasted_iota(jnp.int32, (LANES, orient), 0) // NSEG
    target = lax.broadcasted_iota(jnp.int32, (LANES, orient), 1) % per_row
    spread = jnp.dot(
        masked,
        (source == target).astype(jnp.float32),
        precision=lax.Precision.HIGHEST,
        preferred_element_type=jnp.float32,
    )
    row = lax.broadcasted_iota(jnp.int32, (rows, orient), 0)
    own = lax.broadcasted_iota(jnp.int32, (rows, orient), 1) // per_row == row
    brick = lax.broadcasted_iota(jnp.int32, (bricks, orient), 0).astype(jnp.float32)
    hits = []
    for j in range(NSEG):
        named = jnp.where(own, spread[j * rows : (j + 1) * rows], 0.0)
        named = jnp.sum(named, axis=0, keepdims=True)
        hits.append((brick == named).astype(jnp.float32))
    hit_ref[...] = jnp.concatenate(hits, axis=0).astype(jnp.bfloat16)


def base_phases(rows, offsets_ref, phase_cos_ref, phase_sin_ref):
    group = lax.axis_index("img") * lax.axis_size("brick") + lax.axis_index("brick")
    groups = lax.axis_size("img") * lax.axis_size("brick")
    images = offsets_ref.shape[1]
    off = 2.0 * offsets_ref[...].astype(jnp.float32) - 1.0
    step = max(rows, 8)
    for start in range(0, phase_cos_ref.shape[0], step):
        at = slice(start, start + step)
        row = start + lax.broadcasted_iota(jnp.int32, (step, images), 0)
        col = lax.broadcasted_iota(jnp.int32, (step, images), 1)
        mine = col == (row // rows * groups + group) * rows + row % rows
        off_x, off_y = (
            jnp.sum(jnp.where(mine, off[i : i + 1, :], 0.0), axis=1, keepdims=True).astype(
                jnp.int32
            )
            for i in range(2)
        )
        lane = lax.broadcasted_iota(jnp.int32, (step, LANES), 1)
        u = jnp.bitwise_and(lane, frame_side - 1) - frame_side // 2
        half = jnp.right_shift(lane, 6)
        c1, s1 = cos_sin(u * off_x + half * off_y)
        c2, s2 = cos_sin(2 * lane * off_y)
        for k in range(K // LANES):
            ck, sk = c2[:, k : k + 1], s2[:, k : k + 1]
            phase_cos_ref[at, k * LANES : (k + 1) * LANES] = c1 * ck - s1 * sk
            phase_sin_ref[at, k * LANES : (k + 1) * LANES] = s1 * ck + c1 * sk


def source_plane(source):
    factor, offset, modulus = source
    return lax.rem(factor * lax.axis_index("orient") + offset, modulus)


def score_kernel(first, source, choices, *refs):
    images_refs, refs = refs[:choices], refs[choices:]
    phase_cos_ref, phase_sin_ref, cos_ref, sin_ref = refs[:4]
    norm_ref, slices_ref = refs[4:6]
    stats_in_ref = None if first else refs[8]
    terms_ref, based_ref, stats_ref, left_ref = refs[6 if first else 9 :]
    inv_noise = 100.0 / K
    rows = images_refs[0].shape[0]
    plane = source_plane(source)
    tiles = 2 * K // LANES
    at_end = (lax.axis_index("orient") == 0) | (
        lax.axis_index("orient") == lax.axis_size("orient") - 1
    )

    def pixels(at):
        if choices == 1:
            return images_refs[0][:, at].astype(jnp.float32)
        return jnp.where(at_end, images_refs[0][:, at], images_refs[1][:, at]).astype(jnp.float32)

    where = pl.ds(pl.multiple_of(plane * rows, rows), rows)
    for k in range(tiles // 2):
        re_at = slice(k * LANES, (k + 1) * LANES)
        im_at = slice(K + k * LANES, K + (k + 1) * LANES)
        x_re, x_im = pixels(re_at), pixels(im_at)
        cb, sb = phase_cos_ref[where, re_at], phase_sin_ref[where, re_at]
        y_re = x_re * cb + x_im * sb
        y_im = x_im * cb - x_re * sb
        based_ref[where, re_at] = y_re.astype(jnp.bfloat16)
        based_ref[where, im_at] = y_im.astype(jnp.bfloat16)
        minus_re = -y_re
        re_rows, im_rows = [], []
        for t in range(PAIRS):
            cos_t = cos_ref[t : t + 1, re_at]
            sin_t = sin_ref[t : t + 1, re_at]
            re_rows += [y_re * cos_t, y_im * sin_t]
            im_rows += [y_im * cos_t, minus_re * sin_t]
        left_ref[k] = jnp.concatenate(re_rows, axis=0).astype(jnp.bfloat16)
        left_ref[tiles // 2 + k] = jnp.concatenate(im_rows, axis=0).astype(jnp.bfloat16)
    both = lax.dot_general(
        jnp.concatenate([left_ref[k] for k in range(tiles)], axis=1),
        jnp.concatenate([slices_ref[k] for k in range(tiles)], axis=1),
        (((1,), (1,)), ((), ())),
        preferred_element_type=jnp.float32,
    )
    norm = norm_ref[0:1, :]
    scores = []
    for t in range(PAIRS):
        even = both[2 * t * rows : (2 * t + 1) * rows] - norm
        odd = both[(2 * t + 1) * rows : (2 * t + 2) * rows]
        scores += [inv_noise * (even + odd), inv_noise * (even - odd)]
    top = scores[0]
    for s in scores[1:]:
        top = jnp.maximum(top, s)
    top = jnp.max(top, axis=1, keepdims=True)
    mass = jnp.zeros_like(scores[0])
    for i, s in enumerate(scores):
        term = jnp.exp(s - top)
        mass = mass + term
        terms_ref[i, where, :] = term.astype(jnp.bfloat16)
    mass = jnp.sum(mass, axis=1, keepdims=True)
    count = stats_ref.shape[1]
    row = lax.broadcasted_iota(jnp.int32, (rows, count), 0)
    col = lax.broadcasted_iota(jnp.int32, (rows, count), 1)
    mine = col == row + plane * rows
    top_row = jnp.sum(jnp.where(mine, top, 0.0), axis=0, keepdims=True)
    mass_row = jnp.sum(jnp.where(mine, mass, 0.0), axis=0, keepdims=True)
    which = lax.broadcasted_iota(jnp.int32, (8, count), 0)
    part = jnp.where(which == 0, top_row, jnp.where(which == 1, mass_row, 0.0))
    stats_ref[...] = part if first else part + stats_in_ref[...]


def share_kernel(terms_ref, hit_ref, share_ref):
    for t in range(PAIRS):
        plus, minus = (
            lax.dot_general(
                hit_ref[...],
                terms_ref[2 * t + i],
                (((1,), (1,)), ((), ())),
                preferred_element_type=jnp.float32,
            )
            for i in range(2)
        )
        share_ref[2 * t] = plus + minus
        share_ref[2 * t + 1] = plus - minus


def brick_kernel(others, share_ref, based_ref, cos_ref, sin_ref, *rest):
    stats_refs, out_refs, (pairs_ref, sums_ref) = rest[:others], rest[others:-2], rest[-2:]
    bricks = share_ref.shape[1] // NSEG
    count = based_ref.shape[0]
    own_top = stats_refs[0][0:1, :]
    top = own_top
    for ref in stats_refs[1:]:
        top = jnp.maximum(top, ref[0:1, :])
    mass = jnp.zeros_like(top)
    for ref in stats_refs:
        mass = mass + ref[1:2, :] * jnp.exp(ref[0:1, :] - top)
    factor = jnp.exp(own_top - top) / mass
    mass_sum = jnp.zeros((NSEG * bricks, count), jnp.float32)
    for t in range(PAIRS):
        even = share_ref[2 * t] * factor
        odd = share_ref[2 * t + 1] * factor
        mass_sum = mass_sum + even
        for j in range(NSEG):
            at = slice(j * bricks, (j + 1) * bricks)
            pairs_ref[j, t * bricks : (t + 1) * bricks, :] = even[at].astype(jnp.bfloat16)
            pairs_ref[j, (PAIRS + t) * bricks : (PAIRS + t + 1) * bricks, :] = odd[at].astype(
                jnp.bfloat16
            )
    mass_sum = jnp.sum(mass_sum, axis=1, keepdims=True)
    mass_high = mass_sum.astype(jnp.bfloat16).astype(jnp.float32)
    mass_low = mass_sum - mass_high
    lane = lax.broadcasted_iota(jnp.int32, (bricks, LANES), 1)
    high = low = jnp.zeros((bricks, LANES), jnp.float32)
    for j in range(NSEG):
        at = slice(j * bricks, (j + 1) * bricks)
        re_at = slice(j * SEG, (j + 1) * SEG)
        im_at = slice(K + j * SEG, K + (j + 1) * SEG)
        left = pairs_ref[j]
        with_re = jnp.dot(left, based_ref[:, re_at], preferred_element_type=jnp.float32)
        with_im = jnp.dot(left, based_ref[:, im_at], preferred_element_type=jnp.float32)
        sum_re = jnp.zeros((bricks, SEG), jnp.float32)
        sum_im = jnp.zeros((bricks, SEG), jnp.float32)
        for t in range(PAIRS):
            cos_t = cos_ref[t : t + 1, re_at]
            sin_t = sin_ref[t : t + 1, re_at]
            even = slice(t * bricks, (t + 1) * bricks)
            odd = slice((PAIRS + t) * bricks, (PAIRS + t + 1) * bricks)
            sum_re = sum_re + cos_t * with_re[even] + sin_t * with_im[odd]
            sum_im = sum_im + cos_t * with_im[even] - sin_t * with_re[odd]
        sums_ref[:, 0, re_at] = sum_re
        sums_ref[:, 1, re_at] = sum_im
        high = jnp.where(lane == j, mass_high[at], high)
        low = jnp.where(lane == j, mass_low[at], low)
    sums_ref[:, 0, K:] = high
    sums_ref[:, 1, K:] = low
    if len(out_refs) == 1:
        out_refs[0][...] = sums_ref[...].astype(jnp.bfloat16)
        return
    near = 2 * lax.axis_index("img") + lax.axis_index("brick")
    for m, ref in enumerate(out_refs):
        for z in range(ref.shape[0]):
            ref[z] = sums_ref[z * len(out_refs) + jnp.bitwise_xor(near, m)].astype(jnp.bfloat16)


def plane_kernel(*refs):
    in_refs, out_refs = refs[: len(refs) // 2], refs[len(refs) // 2 :]
    plane = lax.axis_index("orient")
    for m, ref in enumerate(out_refs):
        target = jnp.bitwise_xor(plane, m)
        total = in_refs[0][target].astype(jnp.float32)
        for other in in_refs[1:]:
            total = total + other[target].astype(jnp.float32)
        ref[...] = total.astype(jnp.bfloat16)


def final_kernel(*refs):
    weight_ref, cover_ref, values_ref, mass_ref = refs[-4:]
    vox = cover_ref.shape[1]
    if len(refs) == 5:
        total = jnp.sum(refs[0][...].astype(jnp.float32), axis=0)
    else:
        total = refs[0][...].astype(jnp.float32)
        for ref in refs[1:-4]:
            total = total + ref[...].astype(jnp.float32)
    rest = total[:, :K]
    parts = []
    for _ in range(3):
        high = rest.astype(jnp.bfloat16).astype(jnp.float32)
        parts.append(high)
        rest = rest - high
    left = jnp.concatenate(parts + [jnp.zeros_like(rest)], axis=0).astype(jnp.bfloat16)
    product = jnp.dot(left, weight_ref[...], preferred_element_type=jnp.float32)
    product = product[0:2] + product[2:4] + product[4:6]
    values_ref[0] = (product[:, :vox] * float(1 << interp_bits) + product[:, vox:]) * interp_scale
    seg_mass = total[0:1, K:] + total[1:2, K:]
    weight = jnp.zeros((1, vox), jnp.float32)
    for j in range(NSEG):
        weight = weight + seg_mass[:, j : j + 1] * cover_ref[j : j + 1, :]
    mass_ref[0] = weight


def on_chip(*arrays):
    return [pltpu.with_memory_space_constraint(x, pltpu.VMEM) for x in arrays]


def off_chip(*arrays):
    return [pltpu.with_memory_space_constraint(x, pltpu.HBM) for x in arrays]


def call(kernel, out_shape, inputs, scratch=(), aliases=None, chip_out=True, hbm_in=False):
    spec = pl.BlockSpec(memory_space=pltpu.VMEM)
    in_spec = pl.BlockSpec(memory_space=pltpu.HBM) if hbm_in else spec
    single = not isinstance(out_shape, list)
    shapes = [out_shape] if single else out_shape
    if chip_out:
        shapes = [pltpu.VMEM(x.shape, x.dtype) for x in shapes]
    out = pl.pallas_call(
        kernel,
        in_specs=[in_spec] * len(inputs),
        out_specs=[spec] * len(shapes),
        out_shape=shapes,
        scratch_shapes=list(scratch),
        input_output_aliases=aliases or {},
        compiler_params=pltpu.CompilerParams(vmem_limit_bytes=VMEM_LIMIT),
    )(*inputs)
    return out[0] if single else out


VMEM_LIMIT = 24 * 2**20


def swap(array, amount):
    count = lax.axis_size("orient")
    return lax.ppermute(array, "orient", [(i, i ^ amount) for i in range(count)])


def shift(array, amount):
    count = lax.axis_size("orient")
    return lax.ppermute(array, "orient", [(i, (i + amount) % count) for i in range(count)])


def everyone(array):
    count = lax.axis_size("orient")
    if count != 4:
        return [array] + [shift(array, k) for k in range(1, count)]
    moved = [array]
    for k in (3, 2, 1):
        moved.append(swap(array, k))
    return moved


def after(state, images):
    terms, based, stats = state
    stats, images = lax.optimization_barrier((stats, images))
    return [terms, based, stats], images


def per_device(images, offsets, slices, seg_map, interp):
    orient_count = lax.axis_size("orient")
    group_count = lax.axis_size("img") * lax.axis_size("brick")
    bricks = orient_count * group_count
    rows = images.shape[0]
    orient = slices.shape[0]
    count = rows * orient_count
    vox = interp.shape[3]
    f32, bf16 = jnp.float32, jnp.bfloat16
    tiles = 2 * K // LANES
    relay = orient_count == 4
    staged = relay and group_count == 4
    if relay:
        first = lax.ppermute(images, "orient", [(0, 2), (3, 1), (2, 3), (1, 0)])
    else:
        waiting = [
            ((1, orient_count - k, orient_count), shift(images, k))
            for k in range(1, orient_count)
        ]

    cos_table, sin_table, own, phase_cos, phase_sin, norm, packed = call(
        phase_kernel,
        [
            jax.ShapeDtypeStruct((PAIRS, K), f32),
            jax.ShapeDtypeStruct((PAIRS, K), f32),
            jax.ShapeDtypeStruct(images.shape, bf16),
            jax.ShapeDtypeStruct((count, K), f32),
            jax.ShapeDtypeStruct((count, K), f32),
            jax.ShapeDtypeStruct((8, orient), f32),
            jax.ShapeDtypeStruct((tiles, orient, LANES), bf16),
        ],
        off_chip(images, offsets.T, slices),
        scratch=[
            pltpu.VMEM(offsets.shape[::-1], jnp.int32),
            pltpu.SemaphoreType.DMA((tiles + 2,)),
        ],
        hbm_in=True,
    )
    constant = on_chip(phase_cos, phase_sin, cos_table, sin_table, norm, packed)
    state_shapes = [
        jax.ShapeDtypeStruct((SHIFTS, count, orient), bf16),
        jax.ShapeDtypeStruct((count, 2 * K), bf16),
        jax.ShapeDtypeStruct((8, count), f32),
    ]

    def scored(source, arrays, earlier):
        first = earlier is None
        inputs = on_chip(*arrays) + constant
        if not first:
            inputs += on_chip(*earlier)
        at = len(arrays) + 6
        return call(
            functools.partial(score_kernel, first, source, len(arrays)),
            state_shapes,
            inputs,
            scratch=[pltpu.VMEM((tiles, SHIFTS * rows, LANES), bf16)],
            aliases={} if first else {at + i: i for i in range(3)},
        )

    if relay:
        own, again = lax.optimization_barrier((own, images))
        second = lax.ppermute(again, "orient", [(0, 1), (3, 2), (1, 3), (2, 0)])
    state = scored((1, 0, orient_count), [own], None)
    state, raw = after(state, interp)
    weights, cover, hit = call(
        functools.partial(weight_kernel, bricks),
        [
            jax.ShapeDtypeStruct((K, 2 * vox), bf16),
            jax.ShapeDtypeStruct((NSEG, vox), f32),
            jax.ShapeDtypeStruct((NSEG * bricks, orient), bf16),
        ],
        off_chip(raw, seg_map.reshape(-1, LANES)),
        scratch=[
            pltpu.VMEM(interp.shape[1:], jnp.int32),
            pltpu.VMEM((seg_map.shape[0] // LANES, LANES), jnp.int32),
            pltpu.SemaphoreType.DMA((NSEG + 1,)),
        ],
        hbm_in=True,
    )
    if relay:
        state, first = after(state, first)
        first, again = lax.optimization_barrier((first, images))
        relayed = lax.ppermute(first, "orient", [(2, 3), (1, 0)])
        middle = lax.ppermute(again, "orient", [(1, 2), (2, 1), (0, 0), (3, 3)])
        first, cover = lax.optimization_barrier((first, cover))
        state = scored((2, 1, 5), [first], state)
        state = scored((3, 2, 5), [second], state)
        state = scored((4, 3, 5), [relayed, middle], state)
    else:
        for source, array in waiting:
            state = scored(source, [array], state)
    terms, based, stats = state
    gathered = everyone(stats)
    shares = call(
        share_kernel, jax.ShapeDtypeStruct((SHIFTS, NSEG * bricks, count), f32), on_chip(terms, hit)
    )
    outgoing = call(
        functools.partial(brick_kernel, orient_count),
        [jax.ShapeDtypeStruct((bricks // 4, 2, K + LANES), bf16)] * 4
        if staged
        else jax.ShapeDtypeStruct((bricks, 2, K + LANES), bf16),
        on_chip(shares, based, cos_table, sin_table, *gathered),
        scratch=[
            pltpu.VMEM((NSEG, SHIFTS * bricks, count), bf16),
            pltpu.VMEM((bricks, 2, K + LANES), f32),
        ],
    )
    if staged:
        parts = [outgoing[0]] + [
            lax.ppermute(outgoing[m], ("img", "brick"), [(i, i ^ m) for i in range(4)])
            for m in (1, 2, 3)
        ]
        sums = call(plane_kernel, [jax.ShapeDtypeStruct((2, K + LANES), bf16)] * 4, on_chip(*parts))
        received = [sums[0]] + [swap(sums[m], m) for m in (3, 2, 1)]
    else:
        received = [
            lax.all_to_all(
                outgoing, ("orient", "img", "brick"), split_axis=0, concat_axis=0, tiled=True
            )
        ]
    return call(
        final_kernel,
        [
            jax.ShapeDtypeStruct((1, 2, vox), f32),
            jax.ShapeDtypeStruct((1, 1, vox), f32),
        ],
        on_chip(*received, weights, cover),
        chip_out=False,
    )


def solution(mesh):
    placed = (
        P(("groups", "orient", "img", "brick"), None),
        P("groups", None),
        P(("groups", "orient"), None),
        P(),
        P(("orient", "img", "brick"), None, None, None),
    )

    def device(*args):
        values, weight = per_device(*args)
        return values, weight.reshape(1, -1)

    return jax.shard_map(
        device,
        mesh=mesh,
        in_specs=placed,
        out_specs=(
            P(("groups", "orient", "img", "brick"), None, None),
            P(("groups", "orient", "img", "brick"), None),
        ),
        check_vma=False,
    )
```

```python
import functools

import jax
import jax.numpy as jnp
import numpy as np
from jax import lax
from jax.experimental import pallas as pl
from jax.experimental.pallas import tpu as pltpu
from jax.sharding import PartitionSpec as P


SHIFTS = 16
SEG = 256
NSEG = 8
K = SEG * NSEG
LANES = 128

frame_side = 64
interp_bits = 4
interp_scale = 1.0 / 256.0
PAIRS = SHIFTS // 2


def cos_sin(steps):
    centred = jnp.bitwise_and(steps + frame_side, 2 * frame_side - 1) - frame_side
    x = centred.astype(jnp.float32) * (np.pi / frame_side)
    x2 = x * x
    c = jnp.full_like(x, (-1.0) ** 10 / float(np.prod(np.arange(1.0, 21.0))))
    s = jnp.full_like(x, (-1.0) ** 10 / float(np.prod(np.arange(1.0, 22.0))))
    for k in range(9, -1, -1):
        c = c * x2 + (-1.0) ** k / float(np.prod(np.arange(1.0, 2 * k + 1.0)))
        s = s * x2 + (-1.0) ** k / float(np.prod(np.arange(1.0, 2 * k + 2.0)))
    return c, s * x


def phase_kernel(
    images_hbm,
    offsets_hbm,
    slices_hbm,
    cos_ref,
    sin_ref,
    images_ref,
    phase_cos_ref,
    phase_sin_ref,
    norm_ref,
    slices_ref,
    offsets_ref,
    sems,
):
    tiles, orient = slices_ref.shape[:2]
    copies = [
        pltpu.make_async_copy(offsets_hbm, offsets_ref, sems.at[tiles]),
        pltpu.make_async_copy(images_hbm, images_ref, sems.at[tiles + 1]),
    ]
    packed = [
        pltpu.make_async_copy(
            slices_hbm.at[:, k * LANES : (k + 1) * LANES], slices_ref.at[k], sems.at[k]
        )
        for k in range(tiles)
    ]
    for copy in copies + packed:
        copy.start()
    coef = lax.broadcasted_iota(jnp.int32, (PAIRS, K), 1)
    pair = lax.broadcasted_iota(jnp.int32, (PAIRS, K), 0)
    u = jnp.bitwise_and(coef, frame_side - 1) - frame_side // 2
    w = coef // frame_side
    dx = 2 * jnp.bitwise_and(pair, 3) - 3
    dy = 2 * (pair // 4) - 3
    cos_ref[...], sin_ref[...] = cos_sin(u * dx + w * dy)
    for copy in copies:
        copy.wait()
    base_phases(images_ref.shape[0], offsets_ref, phase_cos_ref, phase_sin_ref)
    total = jnp.zeros((orient, LANES), jnp.float32)
    for k in range(tiles):
        packed[k].wait()
        piece = slices_ref[k].astype(jnp.float32)
        total = total + piece * piece
    norm_ref[...] = 0.5 * lax.dot_general(
        jnp.ones((8, LANES), jnp.float32),
        total,
        (((1,), (1,)), ((), ())),
        precision=lax.Precision.HIGHEST,
        preferred_element_type=jnp.float32,
    )


def weight_kernel(
    bricks, interp_hbm, map_hbm, weight_ref, cover_ref, hit_ref, interp_ref, map_ref, sems
):
    small = pltpu.make_async_copy(map_hbm, map_ref, sems.at[NSEG])
    large = [
        pltpu.make_async_copy(interp_hbm.at[0, j], interp_ref.at[j], sems.at[j])
        for j in range(NSEG)
    ]
    for copy in [small] + large:
        copy.start()
    small.wait()
    vox = interp_ref.shape[2]
    covers = []
    for j in range(NSEG):
        large[j].wait()
        raw = interp_ref[j]
        high = jnp.right_shift(raw, interp_bits).astype(jnp.float32)
        low = jnp.bitwise_and(raw, (1 << interp_bits) - 1).astype(jnp.float32)
        weight_ref[j * SEG : (j + 1) * SEG, :vox] = high.astype(jnp.bfloat16)
        weight_ref[j * SEG : (j + 1) * SEG, vox:] = low.astype(jnp.bfloat16)
        covers.append(jnp.sum(raw.astype(jnp.float32), axis=0, keepdims=True) * interp_scale)
    cover_ref[...] = jnp.concatenate(covers, axis=0)
    orient = hit_ref.shape[1]
    rows = orient * NSEG // LANES
    per_row = LANES // NSEG
    start = pl.multiple_of(lax.axis_index("orient") * rows, rows)
    entries = map_ref[pl.ds(start, rows), :].astype(jnp.float32)
    lane = lax.broadcasted_iota(jnp.int32, (rows, LANES), 1)
    masked = jnp.concatenate(
        [jnp.where(lane % NSEG == j, entries, 0.0) for j in range(NSEG)], axis=0
    )
    source = lax.broadcasted_iota(jnp.int32, (LANES, orient), 0) // NSEG
    target = lax.broadcasted_iota(jnp.int32, (LANES, orient), 1) % per_row
    spread = jnp.dot(
        masked,
        (source == target).astype(jnp.float32),
        precision=lax.Precision.HIGHEST,
        preferred_element_type=jnp.float32,
    )
    row = lax.broadcasted_iota(jnp.int32, (rows, orient), 0)
    own = lax.broadcasted_iota(jnp.int32, (rows, orient), 1) // per_row == row
    brick = lax.broadcasted_iota(jnp.int32, (bricks, orient), 0).astype(jnp.float32)
    hits = []
    for j in range(NSEG):
        named = jnp.where(own, spread[j * rows : (j + 1) * rows], 0.0)
        named = jnp.sum(named, axis=0, keepdims=True)
        hits.append((brick == named).astype(jnp.float32))
    hit_ref[...] = jnp.concatenate(hits, axis=0).astype(jnp.bfloat16)


def base_phases(rows, offsets_ref, phase_cos_ref, phase_sin_ref):
    group = lax.axis_index("img") * lax.axis_size("brick") + lax.axis_index("brick")
    groups = lax.axis_size("img") * lax.axis_size("brick")
    images = offsets_ref.shape[1]
    off = 2.0 * offsets_ref[...].astype(jnp.float32) - 1.0
    step = max(rows, 8)
    for start in range(0, phase_cos_ref.shape[0], step):
        at = slice(start, start + step)
        row = start + lax.broadcasted_iota(jnp.int32, (step, images), 0)
        col = lax.broadcasted_iota(jnp.int32, (step, images), 1)
        mine = col == (row // rows * groups + group) * rows + row % rows
        off_x, off_y = (
            jnp.sum(jnp.where(mine, off[i : i + 1, :], 0.0), axis=1, keepdims=True).astype(
                jnp.int32
            )
            for i in range(2)
        )
        lane = lax.broadcasted_iota(jnp.int32, (step, LANES), 1)
        u = jnp.bitwise_and(lane, frame_side - 1) - frame_side // 2
        half = jnp.right_shift(lane, 6)
        c1, s1 = cos_sin(u * off_x + half * off_y)
        c2, s2 = cos_sin(2 * lane * off_y)
        for k in range(K // LANES):
            ck, sk = c2[:, k : k + 1], s2[:, k : k + 1]
            phase_cos_ref[at, k * LANES : (k + 1) * LANES] = c1 * ck - s1 * sk
            phase_sin_ref[at, k * LANES : (k + 1) * LANES] = s1 * ck + c1 * sk


def source_plane(source):
    factor, offset, modulus = source
    return lax.rem(factor * lax.axis_index("orient") + offset, modulus)


def score_kernel(first, source, choices, *refs):
    images_refs, refs = refs[:choices], refs[choices:]
    phase_cos_ref, phase_sin_ref, cos_ref, sin_ref = refs[:4]
    norm_ref, slices_ref = refs[4:6]
    stats_in_ref = None if first else refs[8]
    terms_ref, based_ref, stats_ref, left_ref = refs[6 if first else 9 :]
    inv_noise = 100.0 / K
    rows = images_refs[0].shape[0]
    plane = source_plane(source)
    tiles = 2 * K // LANES
    at_end = (lax.axis_index("orient") == 0) | (
        lax.axis_index("orient") == lax.axis_size("orient") - 1
    )

    def pixels(at):
        if choices == 1:
            return images_refs[0][:, at].astype(jnp.float32)
        return jnp.where(at_end, images_refs[0][:, at], images_refs[1][:, at]).astype(jnp.float32)

    where = pl.ds(pl.multiple_of(plane * rows, rows), rows)
    for k in range(tiles // 2):
        re_at = slice(k * LANES, (k + 1) * LANES)
        im_at = slice(K + k * LANES, K + (k + 1) * LANES)
        x_re, x_im = pixels(re_at), pixels(im_at)
        cb, sb = phase_cos_ref[where, re_at], phase_sin_ref[where, re_at]
        y_re = x_re * cb + x_im * sb
        y_im = x_im * cb - x_re * sb
        based_ref[where, re_at] = y_re.astype(jnp.bfloat16)
        based_ref[where, im_at] = y_im.astype(jnp.bfloat16)
        minus_re = -y_re
        re_rows, im_rows = [], []
        for t in range(PAIRS):
            cos_t = cos_ref[t : t + 1, re_at]
            sin_t = sin_ref[t : t + 1, re_at]
            re_rows += [y_re * cos_t, y_im * sin_t]
            im_rows += [y_im * cos_t, minus_re * sin_t]
        left_ref[k] = jnp.concatenate(re_rows, axis=0).astype(jnp.bfloat16)
        left_ref[tiles // 2 + k] = jnp.concatenate(im_rows, axis=0).astype(jnp.bfloat16)
    both = lax.dot_general(
        jnp.concatenate([left_ref[k] for k in range(tiles)], axis=1),
        jnp.concatenate([slices_ref[k] for k in range(tiles)], axis=1),
        (((1,), (1,)), ((), ())),
        preferred_element_type=jnp.float32,
    )
    norm = norm_ref[0:1, :]
    scores = []
    for t in range(PAIRS):
        even = both[2 * t * rows : (2 * t + 1) * rows] - norm
        odd = both[(2 * t + 1) * rows : (2 * t + 2) * rows]
        scores += [inv_noise * (even + odd), inv_noise * (even - odd)]
    top = scores[0]
    for s in scores[1:]:
        top = jnp.maximum(top, s)
    top = jnp.max(top, axis=1, keepdims=True)
    mass = jnp.zeros_like(scores[0])
    for i, s in enumerate(scores):
        term = jnp.exp(s - top)
        mass = mass + term
        terms_ref[i, where, :] = term.astype(jnp.bfloat16)
    mass = jnp.sum(mass, axis=1, keepdims=True)
    count = stats_ref.shape[1]
    row = lax.broadcasted_iota(jnp.int32, (rows, count), 0)
    col = lax.broadcasted_iota(jnp.int32, (rows, count), 1)
    mine = col == row + plane * rows
    top_row = jnp.sum(jnp.where(mine, top, 0.0), axis=0, keepdims=True)
    mass_row = jnp.sum(jnp.where(mine, mass, 0.0), axis=0, keepdims=True)
    which = lax.broadcasted_iota(jnp.int32, (8, count), 0)
    part = jnp.where(which == 0, top_row, jnp.where(which == 1, mass_row, 0.0))
    stats_ref[...] = part if first else part + stats_in_ref[...]


def share_kernel(terms_ref, hit_ref, share_ref):
    for t in range(PAIRS):
        plus, minus = (
            lax.dot_general(
                hit_ref[...],
                terms_ref[2 * t + i],
                (((1,), (1,)), ((), ())),
                preferred_element_type=jnp.float32,
            )
            for i in range(2)
        )
        share_ref[2 * t] = plus + minus
        share_ref[2 * t + 1] = plus - minus


def brick_kernel(others, share_ref, based_ref, cos_ref, sin_ref, *rest):
    stats_refs, out_refs, (pairs_ref, sums_ref) = rest[:others], rest[others:-2], rest[-2:]
    bricks = share_ref.shape[1] // NSEG
    count = based_ref.shape[0]
    own_top = stats_refs[0][0:1, :]
    top = own_top
    for ref in stats_refs[1:]:
        top = jnp.maximum(top, ref[0:1, :])
    mass = jnp.zeros_like(top)
    for ref in stats_refs:
        mass = mass + ref[1:2, :] * jnp.exp(ref[0:1, :] - top)
    factor = jnp.exp(own_top - top) / mass
    mass_sum = jnp.zeros((NSEG * bricks, count), jnp.float32)
    for t in range(PAIRS):
        even = share_ref[2 * t] * factor
        odd = share_ref[2 * t + 1] * factor
        mass_sum = mass_sum + even
        for j in range(NSEG):
            at = slice(j * bricks, (j + 1) * bricks)
            pairs_ref[j, t * bricks : (t + 1) * bricks, :] = even[at].astype(jnp.bfloat16)
            pairs_ref[j, (PAIRS + t) * bricks : (PAIRS + t + 1) * bricks, :] = odd[at].astype(
                jnp.bfloat16
            )
    mass_sum = jnp.sum(mass_sum, axis=1, keepdims=True)
    mass_high = mass_sum.astype(jnp.bfloat16).astype(jnp.float32)
    mass_low = mass_sum - mass_high
    lane = lax.broadcasted_iota(jnp.int32, (bricks, LANES), 1)
    high = low = jnp.zeros((bricks, LANES), jnp.float32)
    for j in range(NSEG):
        at = slice(j * bricks, (j + 1) * bricks)
        re_at = slice(j * SEG, (j + 1) * SEG)
        im_at = slice(K + j * SEG, K + (j + 1) * SEG)
        left = pairs_ref[j]
        with_re = jnp.dot(left, based_ref[:, re_at], preferred_element_type=jnp.float32)
        with_im = jnp.dot(left, based_ref[:, im_at], preferred_element_type=jnp.float32)
        sum_re = jnp.zeros((bricks, SEG), jnp.float32)
        sum_im = jnp.zeros((bricks, SEG), jnp.float32)
        for t in range(PAIRS):
            cos_t = cos_ref[t : t + 1, re_at]
            sin_t = sin_ref[t : t + 1, re_at]
            even = slice(t * bricks, (t + 1) * bricks)
            odd = slice((PAIRS + t) * bricks, (PAIRS + t + 1) * bricks)
            sum_re = sum_re + cos_t * with_re[even] + sin_t * with_im[odd]
            sum_im = sum_im + cos_t * with_im[even] - sin_t * with_re[odd]
        sums_ref[:, 0, re_at] = sum_re
        sums_ref[:, 1, re_at] = sum_im
        high = jnp.where(lane == j, mass_high[at], high)
        low = jnp.where(lane == j, mass_low[at], low)
    sums_ref[:, 0, K:] = high
    sums_ref[:, 1, K:] = low
    if len(out_refs) == 1:
        out_refs[0][...] = sums_ref[...].astype(jnp.bfloat16)
        return
    core = lax.axis_index("brick")
    for m, ref in enumerate(out_refs):
        for z in range(ref.shape[0]):
            ref[z] = sums_ref[2 * z + jnp.bitwise_xor(core, m)].astype(jnp.bfloat16)


def core_kernel(own_ref, other_ref, *out_refs):
    side = lax.axis_index("img")
    for m, ref in enumerate(out_refs):
        for z in range(ref.shape[0]):
            at = 2 * z + jnp.bitwise_xor(side, m)
            total = own_ref[at].astype(jnp.float32) + other_ref[at].astype(jnp.float32)
            ref[z] = total.astype(jnp.bfloat16)


def plane_kernel(*refs):
    in_refs, out_refs = refs[:2], refs[2:]
    plane = lax.axis_index("orient")
    for m, ref in enumerate(out_refs):
        target = jnp.bitwise_xor(plane, m)
        total = in_refs[0][target].astype(jnp.float32)
        for other in in_refs[1:]:
            total = total + other[target].astype(jnp.float32)
        ref[...] = total.astype(jnp.bfloat16)


def final_kernel(*refs):
    weight_ref, cover_ref, values_ref, mass_ref = refs[-4:]
    vox = cover_ref.shape[1]
    if len(refs) == 5:
        total = jnp.sum(refs[0][...].astype(jnp.float32), axis=0)
    else:
        total = refs[0][...].astype(jnp.float32)
        for ref in refs[1:-4]:
            total = total + ref[...].astype(jnp.float32)
    rest = total[:, :K]
    parts = []
    for _ in range(3):
        high = rest.astype(jnp.bfloat16).astype(jnp.float32)
        parts.append(high)
        rest = rest - high
    left = jnp.concatenate(parts + [jnp.zeros_like(rest)], axis=0).astype(jnp.bfloat16)
    product = jnp.dot(left, weight_ref[...], preferred_element_type=jnp.float32)
    product = product[0:2] + product[2:4] + product[4:6]
    values_ref[0] = (product[:, :vox] * float(1 << interp_bits) + product[:, vox:]) * interp_scale
    seg_mass = total[0:1, K:] + total[1:2, K:]
    weight = jnp.zeros((1, vox), jnp.float32)
    for j in range(NSEG):
        weight = weight + seg_mass[:, j : j + 1] * cover_ref[j : j + 1, :]
    mass_ref[0] = weight


def on_chip(*arrays):
    return [pltpu.with_memory_space_constraint(x, pltpu.VMEM) for x in arrays]


def off_chip(*arrays):
    return [pltpu.with_memory_space_constraint(x, pltpu.HBM) for x in arrays]


def call(kernel, out_shape, inputs, scratch=(), aliases=None, chip_out=True, hbm_in=False):
    spec = pl.BlockSpec(memory_space=pltpu.VMEM)
    in_spec = pl.BlockSpec(memory_space=pltpu.HBM) if hbm_in else spec
    single = not isinstance(out_shape, list)
    shapes = [out_shape] if single else out_shape
    if chip_out:
        shapes = [pltpu.VMEM(x.shape, x.dtype) for x in shapes]
    out = pl.pallas_call(
        kernel,
        in_specs=[in_spec] * len(inputs),
        out_specs=[spec] * len(shapes),
        out_shape=shapes,
        scratch_shapes=list(scratch),
        input_output_aliases=aliases or {},
        compiler_params=pltpu.CompilerParams(vmem_limit_bytes=VMEM_LIMIT),
    )(*inputs)
    return out[0] if single else out


VMEM_LIMIT = 24 * 2**20


def swap(array, amount):
    count = lax.axis_size("orient")
    return lax.ppermute(array, "orient", [(i, i ^ amount) for i in range(count)])


def shift(array, amount):
    count = lax.axis_size("orient")
    return lax.ppermute(array, "orient", [(i, (i + amount) % count) for i in range(count)])


def everyone(array):
    count = lax.axis_size("orient")
    if count != 4:
        return [array] + [shift(array, k) for k in range(1, count)]
    moved = [array]
    for k in (3, 2, 1):
        moved.append(swap(array, k))
    return moved


def after(state, images):
    terms, based, stats = state
    stats, images = lax.optimization_barrier((stats, images))
    return [terms, based, stats], images


def per_device(images, offsets, slices, seg_map, interp):
    orient_count = lax.axis_size("orient")
    group_count = lax.axis_size("img") * lax.axis_size("brick")
    bricks = orient_count * group_count
    rows = images.shape[0]
    orient = slices.shape[0]
    count = rows * orient_count
    vox = interp.shape[3]
    f32, bf16 = jnp.float32, jnp.bfloat16
    tiles = 2 * K // LANES
    relay = orient_count == 4
    staged = relay and lax.axis_size("img") == lax.axis_size("brick") == 2
    if relay:
        first = lax.ppermute(images, "orient", [(0, 2), (3, 1), (2, 3), (1, 0)])
    else:
        waiting = [
            ((1, orient_count - k, orient_count), shift(images, k))
            for k in range(1, orient_count)
        ]

    cos_table, sin_table, own, phase_cos, phase_sin, norm, packed = call(
        phase_kernel,
        [
            jax.ShapeDtypeStruct((PAIRS, K), f32),
            jax.ShapeDtypeStruct((PAIRS, K), f32),
            jax.ShapeDtypeStruct(images.shape, bf16),
            jax.ShapeDtypeStruct((count, K), f32),
            jax.ShapeDtypeStruct((count, K), f32),
            jax.ShapeDtypeStruct((8, orient), f32),
            jax.ShapeDtypeStruct((tiles, orient, LANES), bf16),
        ],
        off_chip(images, offsets.T, slices),
        scratch=[
            pltpu.VMEM(offsets.shape[::-1], jnp.int32),
            pltpu.SemaphoreType.DMA((tiles + 2,)),
        ],
        hbm_in=True,
    )
    constant = on_chip(phase_cos, phase_sin, cos_table, sin_table, norm, packed)
    state_shapes = [
        jax.ShapeDtypeStruct((SHIFTS, count, orient), bf16),
        jax.ShapeDtypeStruct((count, 2 * K), bf16),
        jax.ShapeDtypeStruct((8, count), f32),
    ]

    def scored(source, arrays, earlier):
        first = earlier is None
        inputs = on_chip(*arrays) + constant
        if not first:
            inputs += on_chip(*earlier)
        at = len(arrays) + 6
        return call(
            functools.partial(score_kernel, first, source, len(arrays)),
            state_shapes,
            inputs,
            scratch=[pltpu.VMEM((tiles, SHIFTS * rows, LANES), bf16)],
            aliases={} if first else {at + i: i for i in range(3)},
        )

    if relay:
        own, again = lax.optimization_barrier((own, images))
        second = lax.ppermute(again, "orient", [(0, 1), (3, 2), (1, 3), (2, 0)])
    state = scored((1, 0, orient_count), [own], None)
    state, raw = after(state, interp)
    weights, cover, hit = call(
        functools.partial(weight_kernel, bricks),
        [
            jax.ShapeDtypeStruct((K, 2 * vox), bf16),
            jax.ShapeDtypeStruct((NSEG, vox), f32),
            jax.ShapeDtypeStruct((NSEG * bricks, orient), bf16),
        ],
        off_chip(raw, seg_map.reshape(-1, LANES)),
        scratch=[
            pltpu.VMEM(interp.shape[1:], jnp.int32),
            pltpu.VMEM((seg_map.shape[0] // LANES, LANES), jnp.int32),
            pltpu.SemaphoreType.DMA((NSEG + 1,)),
        ],
        hbm_in=True,
    )
    if relay:
        state, first = after(state, first)
        first, again = lax.optimization_barrier((first, images))
        relayed = lax.ppermute(first, "orient", [(2, 3), (1, 0)])
        middle = lax.ppermute(again, "orient", [(1, 2), (2, 1), (0, 0), (3, 3)])
        first, cover = lax.optimization_barrier((first, cover))
        state = scored((2, 1, 5), [first], state)
        state = scored((3, 2, 5), [second], state)
        state = scored((4, 3, 5), [relayed, middle], state)
    else:
        for source, array in waiting:
            state = scored(source, [array], state)
    terms, based, stats = state
    gathered = everyone(stats)
    shares = call(
        share_kernel,
        jax.ShapeDtypeStruct((SHIFTS, NSEG * bricks, count), f32),
        on_chip(terms, hit),
    )
    outgoing = call(
        functools.partial(brick_kernel, orient_count),
        [jax.ShapeDtypeStruct((bricks // 2, 2, K + LANES), bf16)] * 2
        if staged
        else jax.ShapeDtypeStruct((bricks, 2, K + LANES), bf16),
        on_chip(shares, based, cos_table, sin_table, *gathered),
        scratch=[
            pltpu.VMEM((NSEG, SHIFTS * bricks, count), bf16),
            pltpu.VMEM((bricks, 2, K + LANES), f32),
        ],
    )
    if staged:
        halves = call(
            core_kernel,
            [jax.ShapeDtypeStruct((bricks // 4, 2, K + LANES), bf16)] * 2,
            on_chip(outgoing[0], lax.ppermute(outgoing[1], "brick", [(0, 1), (1, 0)])),
        )
        parts = [halves[0], lax.ppermute(halves[1], "img", [(0, 1), (1, 0)])]
        sums = call(
            plane_kernel,
            [jax.ShapeDtypeStruct((2, K + LANES), bf16)] * 4,
            on_chip(*parts),
        )
        received = [sums[0]] + [swap(sums[m], m) for m in (3, 2, 1)]
    else:
        received = [
            lax.all_to_all(
                outgoing, ("orient", "img", "brick"), split_axis=0, concat_axis=0, tiled=True
            )
        ]
    return call(
        final_kernel,
        [
            jax.ShapeDtypeStruct((1, 2, vox), f32),
            jax.ShapeDtypeStruct((1, 1, vox), f32),
        ],
        on_chip(*received, weights, cover),
        chip_out=False,
    )


def solution(mesh):
    placed = (
        P(("groups", "orient", "img", "brick"), None),
        P("groups", None),
        P(("groups", "orient"), None),
        P(),
        P(("orient", "img", "brick"), None, None, None),
    )

    def device(*args):
        values, weight = per_device(*args)
        return values, weight.reshape(1, -1)

    return jax.shard_map(
        device,
        mesh=mesh,
        in_specs=placed,
        out_specs=(
            P(("groups", "orient", "img", "brick"), None, None),
            P(("groups", "orient", "img", "brick"), None),
        ),
        check_vma=False,
    )
```
